32 devices in a mesh: region: 4 (over z), tile: 8 (over y, x, core).
Axes of the slice: x: 2, y: 2, z: 4, core: 2. Of those that a mesh axis runs over, the one named last changes fastest.
Arguments:
- water_depth: float32 [1536, 2048], P('region', 'tile'), may hold values from 0.12 to 3
- momentum: float32 [2, 1536, 2048], P(None, 'region', 'tile'), may hold values from -3 to 3
- wet_mask: int32 [96, 8], P('region', 'tile'), may hold values from 0 to 1, as said below
- helper_plan: int32 [96, 8], P('region', 'tile'), may hold values from -1 to 7, as said below
- breach_cells: int32 [4, 8, 64], P('region', 'tile'), may hold values from 0 to 98303
- breach_rate: float32 [4, 8, 64], P('region', 'tile'), may hold values from 1 to 4
Outputs:
- new_depth: float32 [1536, 2048], P('region', 'tile')
- new_momentum: float32 [2, 1536, 2048], P(None, 'region', 'tile')
- helper_speed: float32 [4, 8], P('region', 'tile')
The draws below stay inside these ranges and needn't reach their ends.
Inputs may be any that keep to these rules, and one draw needn't show every extreme that they name: `wet_mask`: along the tile axis the wet block counts of a region's devices run cyclically through 24, 12, 8, 6, 4, 4, 4, 2, at a starting point drawn for each region. `helper_plan`: -1 exactly on dry blocks. The k-th wet block of device t (k from 0), in an order drawn from the seed, goes to helper (t + k - 1) mod 8 of the same region; so one device hands one helper at most 3 blocks, a helper receives at most 10 blocks in all, and some helper of every region receives exactly 10.
All inputs are finite; a program needn't handle non-finite values.
Results may differ from the reference program's by a relative error of at most 0.0003.
Values sent between devices are 32-bit elements; how exact they have to be, the bound alone decides.
No kernel may reach another device: no remote copies, remote signals or barrier semaphores. Data moves between devices by JAX's collectives and lax.ppermute only.
A program may use at most 128 MiB of HBM per device.

```python
import math
import jax
import jax.numpy as jnp
from jax import lax

NBLK = 24
BR = 16
CC = 256
STEPS = 4
NBREACH = 64
NR = 1536
NC = 2048
N_REGION = 4
N_TILE = 8


def wet_layout(key):
    rotation = jax.random.randint(jax.random.fold_in(key, 101), (N_REGION,), 0, 8)
    pattern = jnp.array([24, 12, 8, 6, 4, 4, 4, 2], jnp.int32)
    position = (jnp.arange(N_TILE, dtype=jnp.int32)[None, :] + rotation[:, None]) % 8
    counts = pattern[position]
    scores = jax.random.randint(jax.random.fold_in(key, 102), (N_REGION, N_TILE, NBLK), 0, 1 << 20)
    keyed_scores = scores * NBLK + jnp.arange(NBLK, dtype=jnp.int32)
    wet_order = jnp.argsort(jnp.argsort(keyed_scores, axis=-1), axis=-1).astype(jnp.int32)
    wet_cells = wet_order < counts[:, :, None]
    helper = (jnp.arange(N_TILE, dtype=jnp.int32)[None, :, None] + wet_order - 1 + N_TILE) % N_TILE
    plan_grid = jnp.where(wet_cells, helper, -1)
    wet_out = jnp.transpose(wet_cells.astype(jnp.int32), (0, 2, 1)).reshape(N_REGION * NBLK, N_TILE)
    plan_out = jnp.transpose(plan_grid, (0, 2, 1)).reshape(N_REGION * NBLK, N_TILE)
    return (wet_out, plan_out)


def depth_field(key):
    wet_out, plan_out = wet_layout(key)
    cells = jnp.repeat(jnp.repeat(wet_out, BR, axis=0), CC, axis=1).astype(jnp.float32)
    center = jax.random.uniform(jax.random.fold_in(key, 202), (2,), jnp.float32, 0.0, 1.0)
    row_pos = (jnp.arange(NR, dtype=jnp.float32) + 0.5) / NR
    col_pos = (jnp.arange(NC, dtype=jnp.float32) + 0.5) / NC
    row_gap = (row_pos - center[0]) * 4.0
    col_gap = (col_pos - center[1]) * 8.0
    bump_rows = jnp.exp(-row_gap * row_gap)
    bump_cols = jnp.exp(-col_gap * col_gap)
    base = 0.5 + 1.5 * bump_rows[:, None] * bump_cols[None, :]
    rough = jax.random.uniform(jax.random.fold_in(key, 201), (NR, NC), jnp.float32, 0.6, 1.4)
    return base * rough * (0.5 + 0.5 * cells)


def draw_wet_mask(key, part):
    return wet_layout(key)[0]


def draw_helper_plan(key, part):
    return wet_layout(key)[1]


def draw_water_depth(key, part):
    return depth_field(key)


def draw_momentum(key, part):
    depth_now = depth_field(key)
    velocity = jax.random.uniform(jax.random.fold_in(key, 301), (2, NR, NC), jnp.float32, -0.8, 0.8)
    return depth_now[None] * velocity


def place_ends(values, stream_key, low, high):
    extent = values.shape
    spot = [jax.random.randint(jax.random.fold_in(stream_key, axis), (), 0, extent[axis]) for axis in range(len(extent))]
    values = values.at[tuple(spot)].set(low)
    longest = extent.index(max(extent))
    spot[longest] = (spot[longest] + 1) % extent[longest]
    return values.at[tuple(spot)].set(high)


def steps_of(key, extent, pieces, least, high):
    loudness, own = 1.0, jax.random.fold_in(key, 6)
    for dim, shards_of in pieces:
        draws = jnp.exp(jax.random.uniform(jax.random.fold_in(own, dim), (shards_of,), jnp.float32, least / len(pieces), high / len(pieces)))
        loudness = loudness * jnp.repeat(draws, extent[dim] // shards_of).reshape([-1 if axis == dim else 1 for axis in range(len(extent))])
    return loudness


def setup_inputs(seed: int = 0) -> dict:
    seeds = jax.random.split(jax.random.key(seed), 7)
    water_depth = draw_water_depth(jax.random.fold_in(seeds[6], 71), 0)
    momentum = draw_momentum(jax.random.fold_in(seeds[6], 71), 0)
    wet_mask = draw_wet_mask(jax.random.fold_in(seeds[6], 71), 0)
    helper_plan = draw_helper_plan(jax.random.fold_in(seeds[6], 71), 0)
    breach_cells = place_ends(jax.random.randint(seeds[4], (N_REGION, N_TILE, NBREACH), 0, NBLK * BR * CC), jax.random.fold_in(seeds[4], 1), 0, (NBLK * BR * CC) - 1).astype(jnp.int32)
    breach_rate = jnp.clip(jnp.exp(math.log(4.0) - 1.3862944 * jax.random.uniform(seeds[5], (N_REGION, N_TILE, NBREACH), jnp.float32) ** steps_of(seeds[5], (N_REGION, N_TILE, NBREACH), ((0, 4), (1, 8)), -0.2, 0.2)), 1.0, 4.0)
    return {"water_depth": water_depth, "momentum": momentum, "wet_mask": wet_mask, "helper_plan": helper_plan, "breach_cells": breach_cells, "breach_rate": breach_rate}


GRAVITY = 9.81
COURANT = 0.45
SPACING = 1.0

def wave_speed(depth_now, along_now, across_now):
    return jnp.maximum(jnp.abs(along_now / depth_now), jnp.abs(across_now / depth_now)) + jnp.sqrt(GRAVITY * depth_now)

def roe_flux(depth_left, normal_left, tangent_left, depth_right, normal_right, tangent_right):
    speed_left = normal_left / depth_left
    speed_right = normal_right / depth_right
    drift_left = tangent_left / depth_left
    drift_right = tangent_right / depth_right
    root_left = jnp.sqrt(depth_left)
    root_right = jnp.sqrt(depth_right)
    root_sum = root_left + root_right
    mean_speed = (root_left * speed_left + root_right * speed_right) / root_sum
    mean_drift = (root_left * drift_left + root_right * drift_right) / root_sum
    celerity = jnp.sqrt(GRAVITY * 0.5 * (depth_left + depth_right))
    jump_depth = depth_right - depth_left
    jump_normal = normal_right - normal_left
    jump_tangent = tangent_right - tangent_left
    strength_one = ((mean_speed + celerity) * jump_depth - jump_normal) / (2.0 * celerity)
    strength_three = (jump_normal - (mean_speed - celerity) * jump_depth) / (2.0 * celerity)
    strength_two = jump_tangent - mean_drift * jump_depth
    wave_one = jnp.abs(mean_speed - celerity) * strength_one
    wave_two = jnp.abs(mean_speed) * strength_two
    wave_three = jnp.abs(mean_speed + celerity) * strength_three
    flux_depth = 0.5 * (normal_left + normal_right) - 0.5 * (wave_one + wave_three)
    flux_normal = 0.5 * (normal_left * speed_left + normal_right * speed_right + 0.5 * GRAVITY * (depth_left * depth_left + depth_right * depth_right)) - 0.5 * (wave_one * (mean_speed - celerity) + wave_three * (mean_speed + celerity))
    flux_tangent = 0.5 * (normal_left * drift_left + normal_right * drift_right) - 0.5 * ((wave_one + wave_three) * mean_drift + wave_two)
    return (flux_depth, flux_normal, flux_tangent)

def advance(depth_pad, along_pad, across_pad, active, source, step_size):
    step_ratio = step_size / SPACING
    row_depth, row_along, row_across = roe_flux(depth_pad[..., :-1, 1:-1], along_pad[..., :-1, 1:-1], across_pad[..., :-1, 1:-1], depth_pad[..., 1:, 1:-1], along_pad[..., 1:, 1:-1], across_pad[..., 1:, 1:-1])
    col_depth, col_across, col_along = roe_flux(depth_pad[..., 1:-1, :-1], across_pad[..., 1:-1, :-1], along_pad[..., 1:-1, :-1], depth_pad[..., 1:-1, 1:], across_pad[..., 1:-1, 1:], along_pad[..., 1:-1, 1:])
    depth_now = depth_pad[..., 1:-1, 1:-1]
    along_now = along_pad[..., 1:-1, 1:-1]
    across_now = across_pad[..., 1:-1, 1:-1]
    new_depth = depth_now - step_ratio * (row_depth[..., 1:, :] - row_depth[..., :-1, :] + col_depth[..., 1:] - col_depth[..., :-1]) + step_size * source
    new_along = along_now - step_ratio * (row_along[..., 1:, :] - row_along[..., :-1, :] + col_along[..., 1:] - col_along[..., :-1])
    new_across = across_now - step_ratio * (row_across[..., 1:, :] - row_across[..., :-1, :] + col_across[..., 1:] - col_across[..., :-1])
    keep_cell = active > 0.5
    return (jnp.where(keep_cell, new_depth, depth_now), jnp.where(keep_cell, new_along, along_now), jnp.where(keep_cell, new_across, across_now))

def reflect_pad(values, flip_rows, flip_cols):
    padded = jnp.pad(values, 1, mode='symmetric')
    if flip_rows:
        padded = padded.at[0].multiply(-1.0).at[-1].multiply(-1.0)
    if flip_cols:
        padded = padded.at[:, 0].multiply(-1.0).at[:, -1].multiply(-1.0)
    return padded

def reference(water_depth, momentum, wet_mask, helper_plan, breach_cells, breach_rate):
    active = jnp.repeat(jnp.repeat(wet_mask, BR, axis=0), CC, axis=1).astype(jnp.float32)
    block_rows = NBLK * BR
    row_index = breach_cells // CC + (jnp.arange(N_REGION, dtype=jnp.int32) * block_rows)[:, None, None]
    col_index = breach_cells % CC + (jnp.arange(N_TILE, dtype=jnp.int32) * CC)[None, :, None]
    source = jnp.zeros((NR, NC), jnp.float32).at[row_index.reshape(-1), col_index.reshape(-1)].add(breach_rate.reshape(-1))
    depth_now = water_depth
    along_now = momentum[0]
    across_now = momentum[1]
    for step_index in range(STEPS):
        speed_peak = jnp.max(jnp.where(active > 0.5, wave_speed(depth_now, along_now, across_now), jnp.float32(0.0)))
        step_size = COURANT * SPACING / speed_peak
        depth_now, along_now, across_now = advance(reflect_pad(depth_now, False, False), reflect_pad(along_now, True, False), reflect_pad(across_now, False, True), active, source, step_size)
    final_speed = jnp.where(active > 0.5, wave_speed(depth_now, along_now, across_now), jnp.float32(0.0))
    block_peak = lax.optimization_barrier(jnp.max(final_speed.reshape(N_REGION * NBLK, BR, N_TILE, CC), axis=(1, 3))).reshape(N_REGION, NBLK, N_TILE)
    plan_grid = helper_plan.reshape(N_REGION, NBLK, N_TILE)
    hit_table = plan_grid[..., None] == jnp.arange(N_TILE, dtype=jnp.int32)
    helper_speed = lax.optimization_barrier(jnp.max(jnp.where(hit_table, block_peak[..., None], jnp.float32(0.0)), axis=(1, 2)))
    return (depth_now, jnp.stack([along_now, across_now]), helper_speed)
```

```python
import jax
import jax.numpy as jnp
from jax import lax
from jax.experimental import pallas as pl
from jax.experimental.pallas import tpu as pltpu
from jax.sharding import PartitionSpec as P

STEPS = 4
HALO = 4
LANES = 128
TOP = 8

GRAVITY = 9.81
COURANT = 0.45
SPACING = 1.0

VMEM_LIMIT = 20 << 20


def vmem_spec():
    return pl.BlockSpec(memory_space=pltpu.VMEM)


def smem_spec():
    return pl.BlockSpec(memory_space=pltpu.SMEM)


def vmem_out(*shape):
    return pltpu.VMEM(shape, jnp.float32)


def params():
    return pltpu.CompilerParams(vmem_limit_bytes=VMEM_LIMIT)


def cost(flops, nbytes):
    return pl.CostEstimate(flops=flops, bytes_accessed=nbytes, transcendentals=0)


def lane_ids(rows):
    return lax.broadcasted_iota(jnp.int32, (rows, LANES), 1)


def speed_of(depth, along, across):
    root = lax.rsqrt(depth)
    inverse = root * root
    return jnp.maximum(jnp.abs(along), jnp.abs(across)) * inverse + jnp.sqrt(
        jnp.float32(GRAVITY)
    ) * (depth * root)


def spread_peak(acc, out_ref):
    top = jnp.max(jnp.max(acc, axis=0, keepdims=True), axis=1, keepdims=True)
    out_ref[...] = jnp.broadcast_to(top[None], out_ref.shape)


def start_kernel(
    wet_ref, cell_ref, rate_ref, depth_ref, mom_ref, peak_ref, src_ref, up_ref, down_ref
):
    rows, cols = depth_ref.shape
    blocks = wet_ref.shape[0]
    block_rows = rows // blocks
    src_ref[...] = jnp.zeros_like(src_ref)
    lane = lax.broadcasted_iota(jnp.int32, (1, cols), 1)

    def add_cell(i, carry):
        cell = cell_ref[i]
        row = cell // cols
        col = cell - row * cols
        old = src_ref[pl.ds(row, 1), :]
        src_ref[pl.ds(row, 1), :] = old + jnp.where(lane == col, rate_ref[i], 0.0)
        return carry

    lax.fori_loop(0, cell_ref.shape[0], add_cell, 0)

    def one_block(b, acc):
        at = pl.multiple_of(b * block_rows, 8)
        wet = wet_ref[b, 0] > 0
        rows_at = pl.ds(at, block_rows)
        speed = speed_of(depth_ref[rows_at, :], mom_ref[0, rows_at, :], mom_ref[1, rows_at, :])
        speed = jnp.where(wet, speed, 0.0)
        for r in range(0, block_rows, 8):
            for c in range(0, cols, LANES):
                acc = jnp.maximum(acc, speed[r : r + 8, c : c + LANES])
        return acc

    acc = lax.fori_loop(0, blocks, one_block, jnp.zeros((8, LANES), jnp.float32))
    spread_peak(acc, peak_ref)
    for ref, lo, block in ((up_ref, 0, 0), (down_ref, rows - HALO, blocks - 1)):
        at = slice(lo, lo + HALO)
        ref[0] = depth_ref[at, :]
        ref[1] = mom_ref[0, at, :]
        ref[2] = mom_ref[1, at, :]
        ref[3] = jnp.full((HALO, cols), wet_ref[block, 0].astype(jnp.float32))
        ref[4] = src_ref[at, :]


def rows_kernel(
    edge_ref,
    wet_ref,
    depth_ref,
    mom_ref,
    src_ref,
    above_ref,
    below_ref,
    state_ref,
    fixed_ref,
    left_ref,
    right_ref,
    pack,
):
    rows, cols = depth_ref.shape
    blocks = wet_ref.shape[0]
    block_rows = rows // blocks
    tiles = cols // LANES
    padded = state_ref.shape[2]
    bottom = TOP + rows
    is_top = edge_ref[0] > 0
    is_bottom = edge_ref[1] > 0
    fields = [(state_ref, 0), (state_ref, 1), (state_ref, 2), (fixed_ref, 0), (fixed_ref, 1)]
    own = [depth_ref, mom_ref.at[0], mom_ref.at[1], None, src_ref]

    for b in range(blocks):
        wet = wet_ref[b, 0].astype(jnp.float32)
        for c in range(tiles):
            fixed_ref[0, c, TOP + b * block_rows : TOP + (b + 1) * block_rows, :] = jnp.full(
                (block_rows, LANES), wet
            )
    for f, (ref, k) in enumerate(fields):
        fill = 1.0 if f == 0 else 0.0
        flip = -1.0 if f == 1 else 1.0
        for c in range(tiles):
            at = slice(c * LANES, (c + 1) * LANES)
            if own[f] is not None:
                ref[k, c, TOP:bottom, :] = own[f][:, at]
            ref[k, c, 0:TOP, :] = jnp.full((TOP, LANES), fill, jnp.float32)
            ref[k, c, bottom:padded, :] = jnp.full((padded - bottom, LANES), fill, jnp.float32)
            for j in range(HALO):
                inside = ref[k, c, TOP + j : TOP + j + 1, :] * flip
                other = above_ref[f, HALO - 1 - j : HALO - j, at]
                ref[k, c, TOP - 1 - j : TOP - j, :] = jnp.where(is_top, inside, other)
                inside = ref[k, c, bottom - 1 - j : bottom - j, :] * flip
                other = below_ref[f, j : j + 1, at]
                ref[k, c, bottom + j : bottom + j + 1, :] = jnp.where(is_bottom, inside, other)

    lane = lane_ids(8)
    pack[padded:, :] = jnp.zeros((pack.shape[0] - padded, LANES), jnp.float32)

    def pack_rows(r, carry):
        at = pl.ds(pl.multiple_of(r * 8, 8), 8)
        out = jnp.zeros((8, LANES), jnp.float32)
        for f, (ref, k) in enumerate(fields):
            head = ref[k, 0, at, :]
            tail = ref[k, tiles - 1, at, :]
            first, second = HALO * f, 64 + HALO * f
            if first:
                head = pltpu.roll(head, first, 1)
            tail = pltpu.roll(tail, (second - (LANES - HALO)) % LANES, 1)
            out = jnp.where((lane >= first) & (lane < first + HALO), head, out)
            out = jnp.where((lane >= second) & (lane < second + HALO), tail, out)
        pack[at, :] = out
        return carry

    lax.fori_loop(0, padded // 8, pack_rows, 0)
    for q in range(pack.shape[0] // LANES):
        turned = pack[q * LANES : (q + 1) * LANES, :].T
        left_ref[:, q * LANES : (q + 1) * LANES] = turned[0 : left_ref.shape[0], :]
        right_ref[:, q * LANES : (q + 1) * LANES] = turned[64 : 64 + right_ref.shape[0], :]


def columns_kernel(
    edge_ref,
    state_in,
    fixed_in,
    own_left,
    own_right,
    from_left,
    from_right,
    state_ref,
    fixed_ref,
    both,
    turned,
):
    padded = state_ref.shape[2]
    last = state_ref.shape[1] - 1
    high = own_left.shape[0]
    is_left = edge_ref[2] > 0
    is_right = edge_ref[3] > 0
    both[...] = jnp.zeros_like(both)
    for f in range(5):
        flip = -1.0 if f == 2 else 1.0
        for j in range(HALO):
            row = HALO * f + j
            back = HALO * f + HALO - 1 - j
            both[row : row + 1, :] = jnp.where(
                is_left, own_left[back : back + 1, :] * flip, from_left[row : row + 1, :]
            )
            both[high + row : high + row + 1, :] = jnp.where(
                is_right, own_right[back : back + 1, :] * flip, from_right[row : row + 1, :]
            )
    for q in range(turned.shape[0] // LANES):
        turned[q * LANES : (q + 1) * LANES, :] = both[:, q * LANES : (q + 1) * LANES].T
    lane = lane_ids(8)
    fields = [(state_ref, 0), (state_ref, 1), (state_ref, 2), (fixed_ref, 0), (fixed_ref, 1)]

    def place(r, carry):
        at = pl.ds(pl.multiple_of(r * 8, 8), 8)
        strip = turned[at, :]
        for f, (ref, k) in enumerate(fields):
            out = jnp.full((8, LANES), 1.0 if f == 0 else 0.0, jnp.float32)
            left = pltpu.roll(strip, (LANES - HALO - HALO * f) % LANES, 1)
            right = pltpu.roll(strip, (-(high + HALO * f)) % LANES, 1)
            out = jnp.where(lane >= LANES - HALO, left, out)
            out = jnp.where(lane < HALO, right, out)
            ref[k, last, at, :] = out
        return carry

    lax.fori_loop(0, padded // 8, place, 0)


def roe(left, right):
    depth_l, normal_l, tangent_l, root_l, sn_l, st_l, press_l, shear_l = left
    depth_r, normal_r, tangent_r, root_r, sn_r, st_r, press_r, shear_r = right
    weight = pl.reciprocal(root_l + root_r, approx=False)
    speed = (sn_l + sn_r) * weight
    drift = (st_l + st_r) * weight
    half = (0.5 * GRAVITY) * (depth_l + depth_r)
    inverse = lax.rsqrt(half)
    celerity = half * inverse
    jump = depth_r - depth_l
    excess = (normal_r - normal_l) - speed * jump
    bend = excess * (0.5 * inverse)
    half_jump = 0.5 * jump
    slow = speed - celerity
    fast = speed + celerity
    wave_one = jnp.abs(slow) * (half_jump - bend)
    wave_three = jnp.abs(fast) * (half_jump + bend)
    wave_two = jnp.abs(speed) * ((tangent_r - tangent_l) - drift * jump)
    both = wave_one + wave_three
    flux_depth = (normal_l + normal_r) - both
    flux_normal = (press_l + press_r) - speed * both - celerity * (wave_three - wave_one)
    flux_tangent = (shear_l + shear_r) - drift * both - wave_two
    return flux_depth, flux_normal, flux_tangent


def side(depth, normal, tangent, root, sn, st):
    press = sn * sn + (0.5 * GRAVITY) * (depth * depth)
    return (depth, normal, tangent, root, sn, st, press, sn * st)


def flux_kernel(state_ref, fixed_ref, diff_ref, derived, faces):
    lane_tiles = state_ref.shape[1]
    padded = state_ref.shape[2]
    row_tiles = padded // 8

    def derive(r, carry):
        at = pl.ds(pl.multiple_of(r * 24, 8), 24)
        for c in range(lane_tiles):
            depth = state_ref[0, c, at, :]
            inverse = lax.rsqrt(depth)
            derived[0, c, at, :] = depth * inverse
            derived[1, c, at, :] = state_ref[1, c, at, :] * inverse
            derived[2, c, at, :] = state_ref[2, c, at, :] * inverse
        return carry

    lax.fori_loop(0, padded // 24, derive, 0)
    lane = lane_ids(8)
    for f in range(3):
        for c in range(lane_tiles):
            faces[f, c, 0:8, :] = jnp.zeros((8, LANES), jnp.float32)
            diff_ref[f, c, padded - 8 : padded, :] = jnp.zeros((8, LANES), jnp.float32)

    def load(c, at):
        return [state_ref[k, c, at, :] for k in range(3)] + [derived[k, c, at, :] for k in range(3)]

    def flip(v):
        return (v[0], v[2], v[1], v[3], v[5], v[4])

    def row_faces(r, carry):
        at = pl.multiple_of(r * 8, 8)
        here, below = pl.ds(at, 8), pl.ds(at + 1, 8)
        now = [load(c, here) for c in range(lane_tiles)]
        across = []
        for c in range(lane_tiles):
            nxt = now[(c + 1) % lane_tiles]
            right = [
                pltpu.roll(jnp.where(lane == 0, b, a), LANES - 1, 1)
                for a, b in zip(now[c], nxt)
            ]
            f_depth, f_across, f_along = roe(side(*flip(now[c])), side(*flip(right)))
            across.append((f_depth, f_along, f_across))
            flux = roe(side(*now[c]), side(*load(c, below)))
            for f in range(3):
                faces[f, c, pl.ds(at + 8, 8), :] = flux[f]
        for c in range(lane_tiles):
            prev = across[(c - 1) % lane_tiles]
            active = fixed_ref[0, c, here, :] > 0.5
            for f in range(3):
                left = pltpu.roll(jnp.where(lane == LANES - 1, prev[f], across[c][f]), 1, 1)
                out = (across[c][f] - left) + (
                    faces[f, c, pl.ds(at + 8, 8), :] - faces[f, c, pl.ds(at + 7, 8), :]
                )
                if f == 0:
                    out = out - 2.0 * fixed_ref[1, c, here, :]
                diff_ref[f, c, here, :] = jnp.where(active, out, 0.0)
        return carry

    lax.fori_loop(0, row_tiles - 1, row_faces, 0)


def step_ratio(peak_ref):
    peak = jnp.max(jnp.max(peak_ref[...], axis=0), axis=0, keepdims=True)
    step = (COURANT * SPACING) / peak
    return jnp.broadcast_to((0.5 / SPACING) * step, (8, LANES))


def update_kernel(wet_ref, peak_ref, state_in, diff_ref, state_ref, next_ref):
    lane_tiles = state_in.shape[1]
    padded = state_in.shape[2]
    blocks = wet_ref.shape[0]
    own_tiles = lane_tiles - 1
    block_rows = (padded - 3 * 8) // blocks
    ratio = step_ratio(peak_ref)

    def move(c, at):
        new = [state_in[f, c, at, :] - ratio * diff_ref[f, c, at, :] for f in range(3)]
        for f in range(3):
            state_ref[f, c, at, :] = new[f]
        return new

    def one_block(b, acc):
        wet = wet_ref[b, 0] > 0
        for r in range(0, block_rows, 8):
            at = pl.ds(pl.multiple_of(b * block_rows + TOP + r, 8), 8)
            for c in range(lane_tiles):
                new = move(c, at)
                if c < own_tiles:
                    acc = jnp.maximum(acc, jnp.where(wet, speed_of(*new), 0.0))
        return acc

    acc = lax.fori_loop(0, blocks, one_block, jnp.zeros((8, LANES), jnp.float32))
    for at in (pl.ds(0, 8), pl.ds(padded - 16, 8), pl.ds(padded - 8, 8)):
        for c in range(lane_tiles):
            move(c, at)
    spread_peak(acc, next_ref)


def last_kernel(
    wet_ref, plan_ref, peak_ref, state_in, diff_ref, depth_ref, mom_ref, next_ref, best
):
    blocks = wet_ref.shape[0]
    rows, cols = depth_ref.shape
    block_rows = rows // blocks
    ratio = step_ratio(peak_ref)
    best[...] = jnp.zeros_like(best)

    def one_block(b, carry):
        wet = wet_ref[b, 0] > 0
        acc = jnp.zeros((8, LANES), jnp.float32)
        for r in range(0, block_rows, 8):
            out = pl.multiple_of(b * block_rows + r, 8)
            at = pl.ds(pl.multiple_of(out + TOP, 8), 8)
            out = pl.ds(out, 8)
            for c in range(cols // LANES):
                new = [state_in[f, c, at, :] - ratio * diff_ref[f, c, at, :] for f in range(3)]
                acc = jnp.maximum(acc, jnp.where(wet, speed_of(*new), 0.0))
                lanes = slice(c * LANES, (c + 1) * LANES)
                depth_ref[out, lanes] = new[0]
                mom_ref[0, out, lanes] = new[1]
                mom_ref[1, out, lanes] = new[2]
        helper = jnp.maximum(plan_ref[b, 0], 0)
        best[helper] = jnp.maximum(best[helper], acc)
        return carry

    lax.fori_loop(0, blocks, one_block, 0)
    for t in range(best.shape[0]):
        top = jnp.max(best[t], axis=0, keepdims=True)
        next_ref[t] = jnp.broadcast_to(jnp.max(top, axis=1, keepdims=True), (1, LANES))


def exchange(x, axes):
    return lax.all_to_all(x, axes, 0, 0)


def send(x, axis, forward):
    count = lax.axis_size(axis)
    pairs = [(i, i + 1) if forward else (i + 1, i) for i in range(count - 1)]
    return lax.ppermute(x, axis, pairs)


def on_device(water_depth, momentum, wet_mask, helper_plan, breach_cells, breach_rate):
    rows, cols = water_depth.shape
    tile_count = lax.axis_size("tile")
    region_count = lax.axis_size("region")
    everyone = tile_count * region_count
    region_at = lax.axis_index("region")
    tile_at = lax.axis_index("tile")
    lane_tiles = cols // LANES + 1
    padded = rows + 3 * 8
    lanes_up = -(-padded // LANES) * LANES
    strip = (5 * HALO + 7) // 8 * 8
    f32 = jnp.float32
    edges = jnp.stack(
        [region_at == 0, region_at == region_count - 1, tile_at == 0, tile_at == tile_count - 1]
    ).astype(jnp.int32)
    cells = breach_cells.reshape(-1)
    rates = breach_rate.reshape(-1)
    nbytes = 4 * 3 * rows * cols

    peak, source, up, down = pl.pallas_call(
        start_kernel,
        out_shape=(
            vmem_out(everyone, 1, LANES),
            vmem_out(rows, cols),
            vmem_out(5, HALO, cols),
            vmem_out(5, HALO, cols),
        ),
        in_specs=[smem_spec()] * 3 + [vmem_spec()] * 2,
        out_specs=(vmem_spec(),) * 4,
        compiler_params=params(),
        cost_estimate=cost(20 * rows * cols, nbytes),
        name="start",
    )(wet_mask, cells, rates, water_depth, momentum)

    peaks = exchange(peak, ("region", "tile"))
    above = send(down, "region", True)
    below = send(up, "region", False)

    state, fixed, left, right = pl.pallas_call(
        rows_kernel,
        out_shape=(
            vmem_out(3, lane_tiles, padded, LANES),
            vmem_out(2, lane_tiles, padded, LANES),
            vmem_out(strip, lanes_up),
            vmem_out(strip, lanes_up),
        ),
        in_specs=[smem_spec()] * 2 + [vmem_spec()] * 5,
        out_specs=(vmem_spec(),) * 4,
        scratch_shapes=[pltpu.VMEM((lanes_up, LANES), f32)],
        compiler_params=params(),
        cost_estimate=cost(20 * rows * cols, nbytes),
        name="rows",
    )(edges, wet_mask, water_depth, momentum, source, above, below)

    from_left = send(right, "tile", True)
    from_right = send(left, "tile", False)

    state, fixed = pl.pallas_call(
        columns_kernel,
        out_shape=(
            vmem_out(3, lane_tiles, padded, LANES),
            vmem_out(2, lane_tiles, padded, LANES),
        ),
        in_specs=[smem_spec()] + [vmem_spec()] * 6,
        out_specs=(vmem_spec(),) * 2,
        scratch_shapes=[pltpu.VMEM((LANES, lanes_up), f32), pltpu.VMEM((lanes_up, LANES), f32)],
        input_output_aliases={1: 0, 2: 1},
        compiler_params=params(),
        cost_estimate=cost(10 * rows * cols, nbytes),
        name="columns",
    )(edges, state, fixed, left, right, from_left, from_right)

    for step in range(STEPS):
        diff = pl.pallas_call(
            flux_kernel,
            out_shape=vmem_out(3, lane_tiles, padded, LANES),
            in_specs=[vmem_spec()] * 2,
            out_specs=vmem_spec(),
            scratch_shapes=[
                pltpu.VMEM((3, lane_tiles, padded, LANES), f32),
                pltpu.VMEM((3, lane_tiles, padded + 8, LANES), f32),
            ],
            compiler_params=params(),
            cost_estimate=cost(150 * rows * cols, 4 * nbytes),
            name="flux",
        )(state, fixed)
        if step < STEPS - 1:
            state, peak = pl.pallas_call(
                update_kernel,
                out_shape=(
                    vmem_out(3, lane_tiles, padded, LANES),
                    vmem_out(everyone, 1, LANES),
                ),
                in_specs=[smem_spec()] + [vmem_spec()] * 3,
                out_specs=(vmem_spec(),) * 2,
                input_output_aliases={2: 0},
                compiler_params=params(),
                cost_estimate=cost(20 * rows * cols, nbytes),
                name="update",
            )(wet_mask, peaks, state, diff)
            peaks = exchange(peak, ("region", "tile"))

    new_depth, new_momentum, best = pl.pallas_call(
        last_kernel,
        out_shape=(
            jax.ShapeDtypeStruct((rows, cols), f32),
            jax.ShapeDtypeStruct((2, rows, cols), f32),
            vmem_out(tile_count, 1, LANES),
        ),
        in_specs=[smem_spec()] * 2 + [vmem_spec()] * 3,
        out_specs=(vmem_spec(),) * 3,
        scratch_shapes=[pltpu.VMEM((tile_count, 8, LANES), f32)],
        compiler_params=params(),
        cost_estimate=cost(20 * rows * cols, 2 * nbytes),
        name="last",
    )(wet_mask, helper_plan, peaks, state, diff)
    helper = jnp.max(exchange(best, "tile")[:, :, :1], axis=0)
    return new_depth, new_momentum, helper


def solution(mesh):
    return jax.shard_map(
        on_device,
        mesh=mesh,
        in_specs=(
            P("region", "tile"),
            P(None, "region", "tile"),
            P("region", "tile"),
            P("region", "tile"),
            P("region", "tile", None),
            P("region", "tile", None),
        ),
        out_specs=(P("region", "tile"), P(None, "region", "tile"), P("region", "tile")),
        check_vma=False,
    )
```

```python
import jax
import jax.numpy as jnp
from jax import lax
from jax.experimental import pallas as pl
from jax.experimental.pallas import tpu as pltpu
from jax.sharding import PartitionSpec as P

STEPS = 4
HALO = 4
LANES = 128
TOP = 8

GRAVITY = 9.81
COURANT = 0.45
SPACING = 1.0

VMEM_LIMIT = 20 << 20


WORK = 8
SEND = 5
ACTIVE, SOURCE, DIFF = 3, 4, 5


def vmem_spec():
    return pl.BlockSpec(memory_space=pltpu.VMEM)


def hbm_spec():
    return pl.BlockSpec(memory_space=pltpu.HBM)


def vmem_out(*shape):
    return pltpu.VMEM(shape, jnp.float32)


def params():
    return pltpu.CompilerParams(vmem_limit_bytes=VMEM_LIMIT)


def cost(flops, nbytes):
    return pl.CostEstimate(flops=flops, bytes_accessed=nbytes, transcendentals=0)


def lane_ids(rows):
    return lax.broadcasted_iota(jnp.int32, (rows, LANES), 1)


def aligned(start, size):
    return pl.ds(pl.multiple_of(start, 8), size)


def speed_of(depth, along, across):
    root = lax.rsqrt(depth)
    inverse = root * root
    return jnp.maximum(jnp.abs(along), jnp.abs(across)) * inverse + jnp.sqrt(
        jnp.float32(GRAVITY)
    ) * (depth * root)


def spread_peak(acc, out_ref):
    top = jnp.max(jnp.max(acc, axis=0, keepdims=True), axis=1, keepdims=True)
    out_ref[...] = jnp.broadcast_to(top[None], out_ref.shape)


def start_kernel(
    wet_hbm,
    plan_hbm,
    cell_hbm,
    rate_hbm,
    depth_hbm,
    mom_hbm,
    work,
    plan_ref,
    up_ref,
    down_ref,
    wet_ref,
    plan_smem,
    cell_ref,
    rate_ref,
    small_sem,
    big_sem,
):
    rows, cols = depth_hbm.shape
    tiles = cols // LANES
    padded = work.shape[2]
    blocks = wet_hbm.shape[0]
    block_rows = rows // blocks
    bottom = TOP + rows
    small = [
        pltpu.make_async_copy(src, dst, small_sem.at[i])
        for i, (src, dst) in enumerate(
            [
                (cell_hbm, cell_ref),
                (rate_hbm, rate_ref),
                (wet_hbm, wet_ref),
                (plan_hbm, plan_smem),
            ]
        )
    ]
    big = []
    for k, src in enumerate([depth_hbm, mom_hbm.at[0], mom_hbm.at[1]]):
        for c in range(tiles):
            big.append(
                pltpu.make_async_copy(
                    src.at[:, pl.ds(c * LANES, LANES)],
                    work.at[k, c, pl.ds(TOP, rows), :],
                    big_sem.at[k, c],
                )
            )
    for copy in small + big:
        copy.start()
    for k in range(SEND):
        fill = 1.0 if k == 0 else 0.0
        for c in range(tiles):
            work[k, c, 0:TOP, :] = jnp.full((TOP, LANES), fill, jnp.float32)
            work[k, c, bottom:padded, :] = jnp.full((padded - bottom, LANES), fill, jnp.float32)
        work[k, tiles] = jnp.full((padded, LANES), fill, jnp.float32)
    for c in range(tiles):
        work[SOURCE, c, TOP:bottom, :] = jnp.zeros((rows, LANES), jnp.float32)
    for copy in small:
        copy.wait()
    lane = lane_ids(1)

    def add_cell(i, carry):
        cell = cell_ref[i]
        row = lax.div(cell, cols)
        col = cell - row * cols
        c = lax.div(col, LANES)
        at = pl.ds(row + TOP, 1)
        work[SOURCE, c, at, :] += jnp.where(lane == col - c * LANES, rate_ref[i], 0.0)
        return carry

    lax.fori_loop(0, cell_ref.shape[0], add_cell, 0)
    for b in range(blocks):
        wet = wet_ref[b].astype(jnp.float32)
        at = slice(TOP + b * block_rows, TOP + (b + 1) * block_rows)
        for c in range(tiles):
            work[ACTIVE, c, at, :] = jnp.full((block_rows, LANES), wet)
        plan_ref[b] = jnp.full((8, LANES), plan_smem[b])
    for copy in big:
        copy.wait()
    for k in range(SEND):
        for c in range(tiles):
            up_ref[k * tiles + c] = work[k, c, TOP : TOP + HALO, :]
            down_ref[k * tiles + c] = work[k, c, bottom - HALO : bottom, :]


def packed(work, at, size, lane):
    tiles = work.shape[1] - 1
    out = None
    for k in range(SEND):
        ends = jnp.where(lane < HALO, work[k, 0, at, :], work[k, tiles - 1, at, :])
        ends = pltpu.roll(ends, 2 * HALO * k + HALO, 1)
        out = ends if out is None else jnp.where(lane >= 2 * HALO * k, ends, out)
    return out


def split_packed(turned, left_ref, right_ref, at):
    for k in range(SEND):
        lo = 2 * HALO * k
        right_ref[k, :, at] = turned[lo : lo + HALO, :]
        left_ref[k, :, at] = turned[lo + HALO : lo + 2 * HALO, :]


def pack_kernel(work, peak_ref, left_ref, right_ref, pack):
    tiles = work.shape[1] - 1
    rows = pack.shape[0]
    lane = lane_ids(8)

    def one(r, acc):
        at = aligned(r * 8 + TOP, 8)
        pack[aligned(r * 8, 8), :] = packed(work, at, 8, lane)
        active = work[ACTIVE, 0, at, :] > 0.5
        for c in range(tiles):
            speed = speed_of(work[0, c, at, :], work[1, c, at, :], work[2, c, at, :])
            acc = jnp.maximum(acc, jnp.where(active, speed, 0.0))
        return acc

    acc = lax.fori_loop(0, rows // 8, one, jnp.zeros((8, LANES), jnp.float32), unroll=8)
    spread_peak(acc, peak_ref)
    for q in range(rows // LANES):
        at = slice(q * LANES, (q + 1) * LANES)
        split_packed(pack[at, :].T, left_ref, right_ref, at)


def rows_kernel(
    work_in, left_in, right_in, above_ref, below_ref, work, left_ref, right_ref, pack
):
    tiles = work.shape[1] - 1
    padded = work.shape[2]
    bottom = padded - 2 * 8
    own = left_ref.shape[2] - LANES
    is_top = lax.axis_index("region") == 0
    is_bottom = lax.axis_index("region") == lax.axis_size("region") - 1

    def mirrored(first, step, to):
        for k in range(SEND):
            flip = -1.0 if k == 1 else 1.0
            for c in range(tiles):
                for j in range(HALO):
                    work[k, c, to - step * (1 + j), :] = work[k, c, first + step * j, :] * flip

    def received(ref, lo):
        for k in range(SEND):
            for c in range(tiles):
                work[k, c, lo : lo + HALO, :] = ref[k * tiles + c]

    pl.when(is_top)(lambda: mirrored(TOP, 1, TOP))
    pl.when(jnp.logical_not(is_top))(lambda: received(above_ref, TOP - HALO))
    pl.when(is_bottom)(lambda: mirrored(bottom - 1, -1, bottom - 1))
    pl.when(jnp.logical_not(is_bottom))(lambda: received(below_ref, bottom))
    pack[...] = jnp.zeros_like(pack)
    lane = lane_ids(8)
    pack[0:8, :] = packed(work, slice(0, 8), 8, lane)
    pack[8:16, :] = packed(work, slice(bottom, bottom + 8), 8, lane)
    split_packed(pack[...].T, left_ref, right_ref, slice(own, own + LANES))


def columns_kernel(
    work_in, own_left, own_right, from_left, from_right, work, both, turned
):
    last = work.shape[1] - 1
    own = own_left.shape[2] - LANES
    bottom = TOP + own
    is_left = lax.axis_index("tile") == 0
    is_right = lax.axis_index("tile") == lax.axis_size("tile") - 1

    def mirrored(ref, to):
        for k in range(SEND):
            flip = -1.0 if k == 2 else 1.0
            for j in range(HALO):
                both[2 * HALO * k + to + HALO - 1 - j, :] = ref[k, j, :] * flip

    def received(ref, to):
        for k in range(SEND):
            at = 2 * HALO * k + to
            both[at : at + HALO, :] = ref[k]

    both[2 * HALO * SEND :, :] = jnp.zeros((LANES - 2 * HALO * SEND, own + LANES), jnp.float32)
    pl.when(is_left)(lambda: mirrored(own_left, 0))
    pl.when(jnp.logical_not(is_left))(lambda: received(from_left, 0))
    pl.when(is_right)(lambda: mirrored(own_right, HALO))
    pl.when(jnp.logical_not(is_right))(lambda: received(from_right, HALO))
    for q in range(turned.shape[0] // LANES):
        at = slice(q * LANES, (q + 1) * LANES)
        turned[at, :] = both[:, at].T
    lane = lane_ids(8)
    inside = (lane < HALO) | (lane >= LANES - HALO)

    def place(strip, at):
        for k in range(SEND):
            moved = pltpu.roll(strip, LANES - HALO - 2 * HALO * k, 1)
            work[k, last, at, :] = jnp.where(inside, moved, 1.0 if k == 0 else 0.0)

    def one(r, carry):
        place(turned[aligned(r * 8, 8), :], aligned(r * 8 + TOP, 8))
        return carry

    lax.fori_loop(0, own // 8, one, 0, unroll=8)
    place(turned[own : own + 8, :], slice(0, 8))
    place(turned[own + 8 : own + 16, :], slice(bottom, bottom + 8))


def roe(left, right):
    depth_l, normal_l, tangent_l, root_l, sn_l, st_l, press_l, shear_l = left
    depth_r, normal_r, tangent_r, root_r, sn_r, st_r, press_r, shear_r = right
    weight = pl.reciprocal(root_l + root_r, approx=False)
    speed = (sn_l + sn_r) * weight
    drift = (st_l + st_r) * weight
    half = (0.5 * GRAVITY) * (depth_l + depth_r)
    inverse = lax.rsqrt(half)
    celerity = half * inverse
    jump = depth_r - depth_l
    excess = (normal_r - normal_l) - speed * jump
    bend = excess * (0.5 * inverse)
    half_jump = 0.5 * jump
    slow = speed - celerity
    fast = speed + celerity
    wave_one = jnp.abs(slow) * (half_jump - bend)
    wave_three = jnp.abs(fast) * (half_jump + bend)
    wave_two = jnp.abs(speed) * ((tangent_r - tangent_l) - drift * jump)
    both = wave_one + wave_three
    flux_depth = (normal_l + normal_r) - both
    flux_normal = (press_l + press_r) - speed * both - celerity * (wave_three - wave_one)
    flux_tangent = (shear_l + shear_r) - drift * both - wave_two
    return flux_depth, flux_normal, flux_tangent


def side(depth, normal, tangent, root, sn, st):
    press = sn * sn + (0.5 * GRAVITY) * (depth * depth)
    return (depth, normal, tangent, root, sn, st, press, sn * st)


def flux_kernel(work_in, work, derived, faces):
    lane_tiles = work.shape[1]
    padded = work.shape[2]
    row_tiles = padded // 8

    def derive(r, carry):
        at = aligned(r * 24, 24)
        for c in range(lane_tiles):
            depth = work[0, c, at, :]
            inverse = lax.rsqrt(depth)
            derived[0, c, at, :] = depth * inverse
            derived[1, c, at, :] = work[1, c, at, :] * inverse
            derived[2, c, at, :] = work[2, c, at, :] * inverse
        return carry

    lax.fori_loop(0, padded // 24, derive, 0)
    lane = lane_ids(8)
    for f in range(3):
        for c in range(lane_tiles):
            faces[f, c, 0:8, :] = jnp.zeros((8, LANES), jnp.float32)

    def load(c, at):
        return [work[k, c, at, :] for k in range(3)] + [derived[k, c, at, :] for k in range(3)]

    def flip(v):
        return (v[0], v[2], v[1], v[3], v[5], v[4])

    def row_faces(r, carry):
        at = pl.multiple_of(r * 8, 8)
        here, below = pl.ds(at, 8), pl.ds(at + 1, 8)
        now = [load(c, here) for c in range(lane_tiles)]
        across = []
        for c in range(lane_tiles):
            nxt = now[(c + 1) % lane_tiles]
            right = [
                pltpu.roll(jnp.where(lane == 0, b, a), LANES - 1, 1)
                for a, b in zip(now[c], nxt)
            ]
            f_depth, f_across, f_along = roe(side(*flip(now[c])), side(*flip(right)))
            across.append((f_depth, f_along, f_across))
            flux = roe(side(*now[c]), side(*load(c, below)))
            for f in range(3):
                faces[f, c, pl.ds(at + 8, 8), :] = flux[f]
        for c in range(lane_tiles):
            prev = across[(c - 1) % lane_tiles]
            active = work[ACTIVE, c, here, :] > 0.5
            for f in range(3):
                left = pltpu.roll(jnp.where(lane == LANES - 1, prev[f], across[c][f]), 1, 1)
                out = (across[c][f] - left) + (
                    faces[f, c, pl.ds(at + 8, 8), :] - faces[f, c, pl.ds(at + 7, 8), :]
                )
                if f == 0:
                    out = out - 2.0 * work[SOURCE, c, here, :]
                work[DIFF + f, c, here, :] = jnp.where(active, out, 0.0)
        return carry

    lax.fori_loop(0, row_tiles - 1, row_faces, 0, unroll=5)


def step_ratio(peak_ref):
    peak = jnp.max(jnp.max(peak_ref[...], axis=0), axis=0, keepdims=True)
    step = (COURANT * SPACING) / peak
    return jnp.broadcast_to((0.5 / SPACING) * step, (8, LANES))


def moved(work, c, at, ratio):
    new = [work[f, c, at, :] - ratio * work[DIFF + f, c, at, :] for f in range(3)]
    for f in range(3):
        work[f, c, at, :] = new[f]
    return new


def update_kernel(peak_ref, work_in, work, next_ref):
    lane_tiles = work.shape[1]
    padded = work.shape[2]
    ratio = step_ratio(peak_ref)

    def one(r, acc):
        at = aligned(r * 8 + TOP, 8)
        active = work[ACTIVE, 0, at, :] > 0.5
        for c in range(lane_tiles):
            new = moved(work, c, at, ratio)
            if c < lane_tiles - 1:
                acc = jnp.maximum(acc, jnp.where(active, speed_of(*new), 0.0))
        return acc

    own_tiles = padded // 8 - 3
    acc = lax.fori_loop(0, own_tiles, one, jnp.zeros((8, LANES), jnp.float32), unroll=8)
    for at in (slice(0, 8), slice(padded - 16, padded - 8)):
        for c in range(lane_tiles):
            moved(work, c, at, ratio)
    spread_peak(acc, next_ref)


def last_kernel(peak_ref, plan_ref, work_in, work, next_ref, best):
    tiles = work.shape[1] - 1
    blocks = plan_ref.shape[0]
    block_rows = (work.shape[2] - 3 * 8) // blocks
    ratio = step_ratio(peak_ref)

    def one_block(b, carry):
        acc = jnp.zeros((8, LANES), jnp.float32)
        for r in range(0, block_rows, 8):
            at = aligned(b * block_rows + TOP + r, 8)
            for c in range(tiles):
                acc = jnp.maximum(acc, speed_of(*moved(work, c, at, ratio)))
        best[b] = acc
        return carry

    lax.fori_loop(0, blocks, one_block, 0, unroll=4)
    for t in range(next_ref.shape[0]):
        acc = jnp.zeros((8, LANES), jnp.float32)
        for b in range(blocks):
            acc = jnp.maximum(acc, jnp.where(plan_ref[b] == t, best[b], 0.0))
        top = jnp.max(acc, axis=0, keepdims=True)
        next_ref[t] = jnp.broadcast_to(jnp.max(top, axis=1, keepdims=True), (1, LANES))


def store_kernel(work, depth_hbm, mom_hbm, sem):
    rows, cols = depth_hbm.shape
    copies = []
    for k, dst in enumerate([depth_hbm, mom_hbm.at[0], mom_hbm.at[1]]):
        for c in range(cols // LANES):
            copies.append(
                pltpu.make_async_copy(
                    work.at[k, c, pl.ds(TOP, rows), :],
                    dst.at[:, pl.ds(c * LANES, LANES)],
                    sem.at[k, c],
                )
            )
    for copy in copies:
        copy.start()
    for copy in copies:
        copy.wait()


def exchange(x, axes):
    return lax.all_to_all(x, axes, 0, 0)


def send(x, axis, forward):
    count = lax.axis_size(axis)
    pairs = [(i, i + 1) if forward else (i + 1, i) for i in range(count - 1)]
    return lax.ppermute(x, axis, pairs)


def on_device(water_depth, momentum, wet_mask, helper_plan, breach_cells, breach_rate):
    rows, cols = water_depth.shape
    tile_count = lax.axis_size("tile")
    everyone = tile_count * lax.axis_size("region")
    blocks = wet_mask.shape[0]
    tiles = cols // LANES
    padded = rows + 3 * 8
    f32 = jnp.float32
    cells = breach_cells.reshape(-1)
    rates = breach_rate.reshape(-1)
    nbytes = 4 * 3 * rows * cols
    work_out = vmem_out(WORK, tiles + 1, padded, LANES)
    strip_out = vmem_out(SEND, HALO, rows + LANES)
    edge_out = vmem_out(SEND * tiles, HALO, LANES)
    peak_out = vmem_out(everyone, 1, LANES)

    work, plan, up, down = pl.pallas_call(
        start_kernel,
        out_shape=(work_out, pltpu.VMEM((blocks, 8, LANES), jnp.int32), edge_out, edge_out),
        in_specs=[hbm_spec()] * 6,
        out_specs=(vmem_spec(),) * 4,
        scratch_shapes=[
            pltpu.SMEM((blocks,), jnp.int32),
            pltpu.SMEM((blocks,), jnp.int32),
            pltpu.SMEM(cells.shape, jnp.int32),
            pltpu.SMEM(cells.shape, f32),
            pltpu.SemaphoreType.DMA((4,)),
            pltpu.SemaphoreType.DMA((3, tiles)),
        ],
        compiler_params=params(),
        cost_estimate=cost(2 * rows * cols, nbytes),
        name="start",
    )(wet_mask.reshape(-1), helper_plan.reshape(-1), cells, rates, water_depth, momentum)

    above = send(down, "region", True)
    below = send(up, "region", False)

    peak, left, right = pl.pallas_call(
        pack_kernel,
        out_shape=(peak_out, strip_out, strip_out),
        in_specs=[vmem_spec()],
        out_specs=(vmem_spec(),) * 3,
        scratch_shapes=[pltpu.VMEM((rows, LANES), f32)],
        compiler_params=params(),
        cost_estimate=cost(20 * rows * cols, nbytes),
        name="pack",
    )(work)

    work, left, right = pl.pallas_call(
        rows_kernel,
        out_shape=(work_out, strip_out, strip_out),
        in_specs=[vmem_spec()] * 5,
        out_specs=(vmem_spec(),) * 3,
        scratch_shapes=[pltpu.VMEM((LANES, LANES), f32)],
        input_output_aliases={0: 0, 1: 1, 2: 2},
        compiler_params=params(),
        cost_estimate=cost(rows * cols, nbytes // 8),
        name="rows",
    )(work, left, right, above, below)

    from_left = send(right, "tile", True)
    from_right = send(left, "tile", False)
    peaks = exchange(peak, ("region", "tile"))

    work = pl.pallas_call(
        columns_kernel,
        out_shape=work_out,
        in_specs=[vmem_spec()] * 5,
        out_specs=vmem_spec(),
        scratch_shapes=[
            pltpu.VMEM((LANES, rows + LANES), f32),
            pltpu.VMEM((rows + LANES, LANES), f32),
        ],
        input_output_aliases={0: 0},
        compiler_params=params(),
        cost_estimate=cost(10 * rows * cols, nbytes),
        name="columns",
    )(work, left, right, from_left, from_right)

    for step in range(STEPS):
        work = pl.pallas_call(
            flux_kernel,
            out_shape=work_out,
            in_specs=[vmem_spec()],
            out_specs=vmem_spec(),
            scratch_shapes=[
                pltpu.VMEM((3, tiles + 1, padded, LANES), f32),
                pltpu.VMEM((3, tiles + 1, padded + 8, LANES), f32),
            ],
            input_output_aliases={0: 0},
            compiler_params=params(),
            cost_estimate=cost(150 * rows * cols, 4 * nbytes),
            name="flux",
        )(work)
        if step < STEPS - 1:
            work, peak = pl.pallas_call(
                update_kernel,
                out_shape=(work_out, peak_out),
                in_specs=[vmem_spec()] * 2,
                out_specs=(vmem_spec(),) * 2,
                input_output_aliases={1: 0},
                compiler_params=params(),
                cost_estimate=cost(20 * rows * cols, nbytes),
                name="update",
            )(peaks, work)
            peaks = exchange(peak, ("region", "tile"))

    work, best = pl.pallas_call(
        last_kernel,
        out_shape=(work_out, vmem_out(tile_count, 1, LANES)),
        in_specs=[vmem_spec()] * 3,
        out_specs=(vmem_spec(),) * 2,
        scratch_shapes=[pltpu.VMEM((blocks, 8, LANES), f32)],
        input_output_aliases={2: 0},
        compiler_params=params(),
        cost_estimate=cost(20 * rows * cols, 2 * nbytes),
        name="last",
    )(peaks, plan, work)
    helpers = exchange(best, "tile")
    new_depth, new_momentum = pl.pallas_call(
        store_kernel,
        out_shape=(
            jax.ShapeDtypeStruct((rows, cols), f32),
            jax.ShapeDtypeStruct((2, rows, cols), f32),
        ),
        in_specs=[vmem_spec()],
        out_specs=(hbm_spec(),) * 2,
        scratch_shapes=[pltpu.SemaphoreType.DMA((3, tiles))],
        compiler_params=params(),
        cost_estimate=cost(10 * rows * cols, 2 * nbytes),
        name="store",
    )(work)
    return new_depth, new_momentum, jnp.max(helpers[:, :, :1], axis=0)


def solution(mesh):
    return jax.shard_map(
        on_device,
        mesh=mesh,
        in_specs=(
            P("region", "tile"),
            P(None, "region", "tile"),
            P("region", "tile"),
            P("region", "tile"),
            P("region", "tile", None),
            P("region", "tile", None),
        ),
        out_specs=(P("region", "tile"), P(None, "region", "tile"), P("region", "tile")),
        check_vma=False,
    )
```

```python
import jax
import jax.numpy as jnp
from jax import lax
from jax.experimental import pallas as pl
from jax.experimental.pallas import tpu as pltpu
from jax.sharding import PartitionSpec as P

STEPS = 4
HALO = 4
LANES = 128
TOP = 8

GRAVITY = 9.81
COURANT = 0.45
SPACING = 1.0

VMEM_LIMIT = 20 << 20
FLUX_UNROLL = 7


SOURCE, DIFF, FIELDS = 3, 4, 7
SEND = 5
STRIP_DIFF = 2 * HALO * SEND
STRIP_END = STRIP_DIFF + 2 * HALO * 3


def tiles_of(work):
    return (work.shape[0] - 2) // FIELDS


def active_at(work):
    return work.shape[0] - 2


def strip_at(work):
    return work.shape[0] - 1


def sent_plane(work, k, c):
    tiles = tiles_of(work)
    return (k * tiles + c, active_at(work), SOURCE * tiles + c)[max(k - 2, 0)]


def vmem_spec():
    return pl.BlockSpec(memory_space=pltpu.VMEM)


def hbm_spec():
    return pl.BlockSpec(memory_space=pltpu.HBM)


def vmem_out(*shape):
    return pltpu.VMEM(shape, jnp.float32)


def params():
    return pltpu.CompilerParams(vmem_limit_bytes=VMEM_LIMIT)


def cost(flops, nbytes):
    return pl.CostEstimate(flops=flops, bytes_accessed=nbytes, transcendentals=0)


def lane_ids(rows):
    return lax.broadcasted_iota(jnp.int32, (rows, LANES), 1)


def aligned(start, size):
    return pl.ds(pl.multiple_of(start, 8), size)


def speed_of(depth, along, across):
    root = lax.rsqrt(depth)
    inverse = root * root
    return jnp.maximum(jnp.abs(along), jnp.abs(across)) * inverse + jnp.sqrt(
        jnp.float32(GRAVITY)
    ) * (depth * root)


def spread_peak(acc, out_ref):
    top = jnp.max(jnp.max(acc, axis=0, keepdims=True), axis=1, keepdims=True)
    out_ref[...] = jnp.broadcast_to(top[None], out_ref.shape)


def start_kernel(
    wet_hbm,
    plan_hbm,
    cell_hbm,
    rate_hbm,
    depth_hbm,
    mom_hbm,
    work,
    plan_ref,
    up_ref,
    down_ref,
    wet_ref,
    plan_smem,
    cell_ref,
    rate_ref,
    small_sem,
    big_sem,
):
    rows, cols = depth_hbm.shape
    tiles = cols // LANES
    padded = work.shape[1]
    blocks = wet_hbm.shape[0]
    block_rows = rows // blocks
    bottom = TOP + rows
    small = [
        pltpu.make_async_copy(src, dst, small_sem.at[i])
        for i, (src, dst) in enumerate(
            [
                (cell_hbm, cell_ref),
                (rate_hbm, rate_ref),
                (wet_hbm, wet_ref),
                (plan_hbm, plan_smem),
            ]
        )
    ]
    big = []
    for k, src in enumerate([depth_hbm, mom_hbm.at[0], mom_hbm.at[1]]):
        for c in range(tiles):
            big.append(
                pltpu.make_async_copy(
                    src.at[:, pl.ds(c * LANES, LANES)],
                    work.at[k * tiles + c, pl.ds(TOP, rows), :],
                    big_sem.at[k, c],
                )
            )
    for copy in small + big:
        copy.start()
    for k in range(SEND):
        for c in range(tiles):
            plane = sent_plane(work, k, c)
            fill = 1.0 if k == 0 else 0.0
            work[plane, 0:TOP, :] = jnp.full((TOP, LANES), fill, jnp.float32)
            work[plane, bottom:padded, :] = jnp.full((padded - bottom, LANES), fill, jnp.float32)
    for c in range(tiles):
        work[SOURCE * tiles + c, TOP:bottom, :] = jnp.zeros((rows, LANES), jnp.float32)
    for copy in small:
        copy.wait()
    lane = lane_ids(1)

    def add_cell(i, carry):
        cell = cell_ref[i]
        row = lax.div(cell, cols)
        col = cell - row * cols
        c = lax.div(col, LANES)
        at = pl.ds(row + TOP, 1)
        work[SOURCE * tiles + c, at, :] += jnp.where(lane == col - c * LANES, rate_ref[i], 0.0)
        return carry

    lax.fori_loop(0, cell_ref.shape[0], add_cell, 0)
    for b in range(blocks):
        wet = wet_ref[b].astype(jnp.float32)
        at = slice(TOP + b * block_rows, TOP + (b + 1) * block_rows)
        work[active_at(work), at, :] = jnp.full((block_rows, LANES), wet)
        plan_ref[b] = jnp.full((1, LANES), plan_smem[b])
    for copy in big:
        copy.wait()
    for k in range(SEND):
        for c in range(tiles):
            plane = sent_plane(work, k, c)
            up_ref[k * tiles + c] = work[plane, TOP : TOP + HALO, :]
            down_ref[k * tiles + c] = work[plane, bottom - HALO : bottom, :]


def packed(work, at, lane):
    tiles = tiles_of(work)
    out = None
    for k in range(SEND):
        first, last = sent_plane(work, k, 0), sent_plane(work, k, tiles - 1)
        ends = jnp.where(lane < HALO, work[first, at, :], work[last, at, :])
        ends = pltpu.roll(ends, 2 * HALO * k + HALO, 1)
        out = ends if out is None else jnp.where(lane >= 2 * HALO * k, ends, out)
    return out


def split_packed(turned, left_ref, right_ref, at):
    for k in range(SEND):
        lo = 2 * HALO * k
        right_ref[k, :, at] = turned[lo : lo + HALO, :]
        left_ref[k, :, at] = turned[lo + HALO : lo + 2 * HALO, :]


def pack_kernel(work, peak_ref, left_ref, right_ref, pack):
    tiles = tiles_of(work)
    rows = pack.shape[0]
    lane = lane_ids(8)

    def one(r, acc):
        at = aligned(r * 8 + TOP, 8)
        pack[aligned(r * 8, 8), :] = packed(work, at, lane)
        active = work[active_at(work), at, :] > 0.5
        for c in range(tiles):
            speed = speed_of(*[work[k * tiles + c, at, :] for k in range(3)])
            acc = jnp.maximum(acc, jnp.where(active, speed, 0.0))
        return acc

    acc = lax.fori_loop(0, rows // 8, one, jnp.zeros((8, LANES), jnp.float32), unroll=8)
    spread_peak(acc, peak_ref)
    for q in range(rows // LANES):
        at = slice(q * LANES, (q + 1) * LANES)
        split_packed(pack[at, :].T, left_ref, right_ref, at)


def rows_kernel(
    work_in, left_in, right_in, above_ref, below_ref, work, left_ref, right_ref, pack
):
    tiles = tiles_of(work)
    own = left_ref.shape[2] - LANES
    bottom = TOP + own
    is_top = lax.axis_index("region") == 0
    is_bottom = lax.axis_index("region") == lax.axis_size("region") - 1

    def mirrored(first, step, to):
        for k in range(SEND):
            flip = -1.0 if k == 1 else 1.0
            for c in range(tiles):
                plane = sent_plane(work, k, c)
                for j in range(HALO):
                    work[plane, to - step * (1 + j), :] = work[plane, first + step * j, :] * flip

    def received(ref, lo):
        for k in range(SEND):
            for c in range(tiles):
                work[sent_plane(work, k, c), lo : lo + HALO, :] = ref[k * tiles + c]

    pl.when(is_top)(lambda: mirrored(TOP, 1, TOP))
    pl.when(jnp.logical_not(is_top))(lambda: received(above_ref, TOP - HALO))
    pl.when(is_bottom)(lambda: mirrored(bottom - 1, -1, bottom - 1))
    pl.when(jnp.logical_not(is_bottom))(lambda: received(below_ref, bottom))
    pack[...] = jnp.zeros_like(pack)
    lane = lane_ids(8)
    pack[0:8, :] = packed(work, slice(0, 8), lane)
    pack[8:16, :] = packed(work, slice(bottom, bottom + 8), lane)
    split_packed(pack[...].T, left_ref, right_ref, slice(own, own + LANES))


def columns_kernel(work_in, own_left, own_right, from_left, from_right, work, both):
    own = own_left.shape[2] - LANES
    bottom = TOP + own
    is_left = lax.axis_index("tile") == 0
    is_right = lax.axis_index("tile") == lax.axis_size("tile") - 1

    def mirrored(ref, to):
        for k in range(SEND):
            flip = -1.0 if k == 2 else 1.0
            for j in range(HALO):
                both[2 * HALO * k + to + HALO - 1 - j, :] = ref[k, j, :] * flip

    def received(ref, to):
        for k in range(SEND):
            at = 2 * HALO * k + to
            both[at : at + HALO, :] = ref[k]

    both[STRIP_DIFF:, :] = jnp.zeros((LANES - STRIP_DIFF, own + LANES), jnp.float32)
    pl.when(is_left)(lambda: mirrored(own_left, 0))
    pl.when(jnp.logical_not(is_left))(lambda: received(from_left, 0))
    pl.when(is_right)(lambda: mirrored(own_right, HALO))
    pl.when(jnp.logical_not(is_right))(lambda: received(from_right, HALO))
    strip = strip_at(work)
    for q in range(own // LANES):
        at = slice(q * LANES, (q + 1) * LANES)
        work[strip, TOP + q * LANES : TOP + (q + 1) * LANES, :] = both[:, at].T
    ends = both[:, own : own + LANES].T
    work[strip, 0:8, :] = ends[0:8, :]
    work[strip, bottom : bottom + 8, :] = ends[8:16, :]


def roe(left, right):
    depth_l, normal_l, tangent_l, root_l, sn_l, st_l, press_l, shear_l = left
    depth_r, normal_r, tangent_r, root_r, sn_r, st_r, press_r, shear_r = right
    weight = pl.reciprocal(root_l + root_r, approx=False)
    speed = (sn_l + sn_r) * weight
    drift = (st_l + st_r) * weight
    half = (0.5 * GRAVITY) * (depth_l + depth_r)
    inverse = lax.rsqrt(half)
    celerity = half * inverse
    jump = depth_r - depth_l
    excess = (normal_r - normal_l) - speed * jump
    bend = excess * (0.5 * inverse)
    half_jump = 0.5 * jump
    slow = speed - celerity
    fast = speed + celerity
    wave_one = jnp.abs(slow) * (half_jump - bend)
    wave_three = jnp.abs(fast) * (half_jump + bend)
    wave_two = jnp.abs(speed) * ((tangent_r - tangent_l) - drift * jump)
    both = wave_one + wave_three
    flux_depth = (normal_l + normal_r) - both
    flux_normal = (press_l + press_r) - speed * both - celerity * (wave_three - wave_one)
    flux_tangent = (shear_l + shear_r) - drift * both - wave_two
    return flux_depth, flux_normal, flux_tangent


def side(depth, normal, tangent, root, sn, st):
    press = sn * sn + (0.5 * GRAVITY) * (depth * depth)
    return (depth, normal, tangent, root, sn, st, press, sn * st)


def flux_kernel(work_in, work, beside, derived, faces):
    tiles = tiles_of(work)
    padded = work.shape[1]
    row_tiles = padded // 8
    strip, active_rows = strip_at(work), active_at(work)
    lane = lane_ids(8)
    inside = (lane < HALO) | (lane >= LANES - HALO)

    def derive(r, carry):
        for i in range(5):
            at = aligned(r * 40 + i * 8, 8)
            packed_columns = work[strip, at, :]
            for k in range(SEND):
                out = pltpu.roll(packed_columns, LANES - HALO - 2 * HALO * k, 1)
                beside[k, at, :] = jnp.where(inside, out, 1.0) if k == 0 else out
            for c in range(tiles + 1):
                state = own_state(c, at)
                inverse = lax.rsqrt(state[0])
                derived[c, at, :] = state[0] * inverse
                derived[tiles + 1 + c, at, :] = state[1] * inverse
                derived[2 * (tiles + 1) + c, at, :] = state[2] * inverse
        return carry

    def own_state(c, at):
        if c == tiles:
            return [beside[k, at, :] for k in range(3)]
        return [work[k * tiles + c, at, :] for k in range(3)]

    lax.fori_loop(0, row_tiles // 5, derive, 0)
    for f in range(3):
        for c in range(tiles + 1):
            faces[f * (tiles + 1) + c, 0:8, :] = jnp.zeros((8, LANES), jnp.float32)

    def load(c, at):
        return own_state(c, at) + [derived[k * (tiles + 1) + c, at, :] for k in range(3)]

    def flip(v):
        return (v[0], v[2], v[1], v[3], v[5], v[4])

    def row_faces(at, wrap):
        here, below = pl.ds(at, 8), pl.ds(at + 1, 8)
        now = [load(c, here) for c in range(tiles + 1)]
        across = []
        for c in range(tiles + 1):
            nxt = now[(c + 1) % (tiles + 1)]
            right = [
                pltpu.roll(jnp.where(lane == 0, b, a), LANES - 1, 1)
                for a, b in zip(now[c], nxt)
            ]
            f_depth, f_across, f_along = roe(side(*flip(now[c])), side(*flip(right)))
            across.append((f_depth, f_along, f_across))
            under = [pltpu.roll(v, 7, 0) for v in now[c]] if wrap else load(c, below)
            flux = roe(side(*now[c]), side(*under))
            for f in range(3):
                faces[f * (tiles + 1) + c, pl.ds(at + 8, 8), :] = flux[f]
        strip_out = work[strip, here, :]
        for c in range(tiles + 1):
            prev = across[(c - 1) % (tiles + 1)]
            own = c < tiles
            active = (work[active_rows, here, :] if own else beside[3, here, :]) > 0.5
            for f in range(3):
                left = pltpu.roll(jnp.where(lane == LANES - 1, prev[f], across[c][f]), 1, 1)
                plane = f * (tiles + 1) + c
                out = (across[c][f] - left) + (
                    faces[plane, pl.ds(at + 8, 8), :] - faces[plane, pl.ds(at + 7, 8), :]
                )
                if f == 0:
                    source = work[SOURCE * tiles + c, here, :] if own else beside[4, here, :]
                    out = out - 2.0 * source
                out = jnp.where(active, out, 0.0)
                if own:
                    work[(DIFF + f) * tiles + c, here, :] = out
                else:
                    lo = STRIP_DIFF + 2 * HALO * f
                    strip_out = jnp.where(lane >= lo, pltpu.roll(out, lo + HALO, 1), strip_out)
        work[strip, here, :] = strip_out

    def one(r, carry):
        row_faces(pl.multiple_of(r * 8, 8), False)
        return carry

    lax.fori_loop(0, row_tiles - 1, one, 0, unroll=FLUX_UNROLL)
    row_faces(padded - 8, True)


def step_ratio(peak_ref):
    peak = jnp.max(jnp.max(peak_ref[...], axis=0), axis=0, keepdims=True)
    step = (COURANT * SPACING) / peak
    return jnp.broadcast_to((0.5 / SPACING) * step, (8, LANES))


def moved(work, c, at, ratio):
    tiles = tiles_of(work)
    new = [
        work[f * tiles + c, at, :] - ratio * work[(DIFF + f) * tiles + c, at, :] for f in range(3)
    ]
    for f in range(3):
        work[f * tiles + c, at, :] = new[f]
    return new


def update_kernel(peak_ref, work_in, work, next_ref):
    tiles = tiles_of(work)
    row_tiles = work.shape[1] // 8
    strip = strip_at(work)
    ratio = step_ratio(peak_ref)
    lane = lane_ids(8)
    strip_ratio = jnp.where(lane < 2 * HALO * 3, ratio, 0.0)

    def move_strip(at):
        old = work[strip, at, :]
        work[strip, at, :] = old - strip_ratio * pltpu.roll(old, LANES - STRIP_DIFF, 1)

    def one(r, acc):
        at = aligned(r * 8 + TOP, 8)
        active = work[active_at(work), at, :] > 0.5
        for c in range(tiles):
            new = moved(work, c, at, ratio)
            acc = jnp.maximum(acc, jnp.where(active, speed_of(*new), 0.0))
        move_strip(at)
        return acc

    zero = jnp.zeros((8, LANES), jnp.float32)
    acc = lax.fori_loop(0, row_tiles - 2, one, zero, unroll=8)
    for at in (slice(0, 8), slice(8 * row_tiles - 8, 8 * row_tiles)):
        for c in range(tiles):
            moved(work, c, at, ratio)
        move_strip(at)
    spread_peak(acc, next_ref)


def last_kernel(peak_ref, plan_ref, work_in, work, next_ref, best):
    tiles = tiles_of(work)
    blocks = plan_ref.shape[0]
    block_rows = (work.shape[1] - 2 * 8) // blocks
    ratio = step_ratio(peak_ref)

    def one_block(b, carry):
        acc = jnp.zeros((8, LANES), jnp.float32)
        for r in range(0, block_rows, 8):
            at = aligned(b * block_rows + TOP + r, 8)
            for c in range(tiles):
                acc = jnp.maximum(acc, speed_of(*moved(work, c, at, ratio)))
        best[b] = acc
        return carry

    lax.fori_loop(0, blocks, one_block, 0, unroll=4)
    for t in range(next_ref.shape[0]):
        acc = jnp.zeros((8, LANES), jnp.float32)
        for b in range(blocks):
            acc = jnp.maximum(acc, jnp.where(plan_ref[b] == t, best[b], 0.0))
        top = jnp.max(acc, axis=0, keepdims=True)
        next_ref[t] = jnp.broadcast_to(jnp.max(top, axis=1, keepdims=True), (1, LANES))


def store_kernel(work, depth_hbm, mom_hbm, sem):
    rows, cols = depth_hbm.shape
    tiles = cols // LANES
    copies = []
    for k, dst in enumerate([depth_hbm, mom_hbm.at[0], mom_hbm.at[1]]):
        for c in range(tiles):
            copies.append(
                pltpu.make_async_copy(
                    work.at[k * tiles + c, pl.ds(TOP, rows), :],
                    dst.at[:, pl.ds(c * LANES, LANES)],
                    sem.at[k, c],
                )
            )
    for copy in copies:
        copy.start()
    for copy in copies:
        copy.wait()


def exchange(x, axes):
    return lax.all_to_all(x, axes, 0, 0)


def send(x, axis, forward):
    count = lax.axis_size(axis)
    pairs = [(i, i + 1) if forward else (i + 1, i) for i in range(count - 1)]
    return lax.ppermute(x, axis, pairs)


def on_device(water_depth, momentum, wet_mask, helper_plan, breach_cells, breach_rate):
    rows, cols = water_depth.shape
    tile_count = lax.axis_size("tile")
    everyone = tile_count * lax.axis_size("region")
    blocks = wet_mask.shape[0]
    tiles = cols // LANES
    padded = rows + 2 * 8
    f32 = jnp.float32
    cells = breach_cells.reshape(-1)
    rates = breach_rate.reshape(-1)
    nbytes = 4 * 3 * rows * cols
    work_out = vmem_out(FIELDS * tiles + 2, padded, LANES)
    strip_out = vmem_out(SEND, HALO, rows + LANES)
    edge_out = vmem_out(SEND * tiles, HALO, LANES)
    peak_out = vmem_out(everyone, 1, LANES)

    work, plan, up, down = pl.pallas_call(
        start_kernel,
        out_shape=(work_out, pltpu.VMEM((blocks, 1, LANES), jnp.int32), edge_out, edge_out),
        in_specs=[hbm_spec()] * 6,
        out_specs=(vmem_spec(),) * 4,
        scratch_shapes=[
            pltpu.SMEM((blocks,), jnp.int32),
            pltpu.SMEM((blocks,), jnp.int32),
            pltpu.SMEM(cells.shape, jnp.int32),
            pltpu.SMEM(cells.shape, f32),
            pltpu.SemaphoreType.DMA((4,)),
            pltpu.SemaphoreType.DMA((3, tiles)),
        ],
        compiler_params=params(),
        cost_estimate=cost(2 * rows * cols, nbytes),
        name="start",
    )(
        *(
            pltpu.with_memory_space_constraint(x, pltpu.HBM)
            for x in (
                wet_mask.reshape(-1),
                helper_plan.reshape(-1),
                cells,
                rates,
                water_depth,
                momentum,
            )
        )
    )

    above = send(down, "region", True)
    below = send(up, "region", False)

    peak, left, right = pl.pallas_call(
        pack_kernel,
        out_shape=(peak_out, strip_out, strip_out),
        in_specs=[vmem_spec()],
        out_specs=(vmem_spec(),) * 3,
        scratch_shapes=[pltpu.VMEM((rows, LANES), f32)],
        compiler_params=params(),
        cost_estimate=cost(20 * rows * cols, nbytes),
        name="pack",
    )(work)

    work, left, right = pl.pallas_call(
        rows_kernel,
        out_shape=(work_out, strip_out, strip_out),
        in_specs=[vmem_spec()] * 5,
        out_specs=(vmem_spec(),) * 3,
        scratch_shapes=[pltpu.VMEM((LANES, LANES), f32)],
        input_output_aliases={0: 0, 1: 1, 2: 2},
        compiler_params=params(),
        cost_estimate=cost(rows * cols, nbytes // 8),
        name="rows",
    )(work, left, right, above, below)

    from_left = send(right, "tile", True)
    from_right = send(left, "tile", False)
    peaks = exchange(peak, ("region", "tile"))

    work = pl.pallas_call(
        columns_kernel,
        out_shape=work_out,
        in_specs=[vmem_spec()] * 5,
        out_specs=vmem_spec(),
        scratch_shapes=[
            pltpu.VMEM((LANES, rows + LANES), f32),
        ],
        input_output_aliases={0: 0},
        compiler_params=params(),
        cost_estimate=cost(10 * rows * cols, nbytes),
        name="columns",
    )(work, left, right, from_left, from_right)

    for step in range(STEPS):
        work = pl.pallas_call(
            flux_kernel,
            out_shape=work_out,
            in_specs=[vmem_spec()],
            out_specs=vmem_spec(),
            scratch_shapes=[
                pltpu.VMEM((SEND, padded, LANES), f32),
                pltpu.VMEM((3 * (tiles + 1), padded, LANES), f32),
                pltpu.VMEM((3 * (tiles + 1), padded + 8, LANES), f32),
            ],
            input_output_aliases={0: 0},
            compiler_params=params(),
            cost_estimate=cost(150 * rows * cols, 4 * nbytes),
            name="flux",
        )(work)
        if step < STEPS - 1:
            work, peak = pl.pallas_call(
                update_kernel,
                out_shape=(work_out, peak_out),
                in_specs=[vmem_spec()] * 2,
                out_specs=(vmem_spec(),) * 2,
                input_output_aliases={1: 0},
                compiler_params=params(),
                cost_estimate=cost(20 * rows * cols, nbytes),
                name="update",
            )(peaks, work)
            peaks = exchange(peak, ("region", "tile"))

    work, best = pl.pallas_call(
        last_kernel,
        out_shape=(work_out, vmem_out(tile_count, 1, LANES)),
        in_specs=[vmem_spec()] * 3,
        out_specs=(vmem_spec(),) * 2,
        scratch_shapes=[pltpu.VMEM((blocks, 8, LANES), f32)],
        input_output_aliases={2: 0},
        compiler_params=params(),
        cost_estimate=cost(20 * rows * cols, 2 * nbytes),
        name="last",
    )(peaks, plan, work)
    helpers = exchange(best, "tile")
    new_depth, new_momentum = pl.pallas_call(
        store_kernel,
        out_shape=(
            jax.ShapeDtypeStruct((rows, cols), f32),
            jax.ShapeDtypeStruct((2, rows, cols), f32),
        ),
        in_specs=[vmem_spec()],
        out_specs=(hbm_spec(),) * 2,
        scratch_shapes=[pltpu.SemaphoreType.DMA((3, tiles))],
        compiler_params=params(),
        cost_estimate=cost(10 * rows * cols, 2 * nbytes),
        name="store",
    )(work)
    return new_depth, new_momentum, jnp.max(helpers[:, :, :1], axis=0)


def solution(mesh):
    return jax.shard_map(
        on_device,
        mesh=mesh,
        in_specs=(
            P("region", "tile"),
            P(None, "region", "tile"),
            P("region", "tile"),
            P("region", "tile"),
            P("region", "tile", None),
            P("region", "tile", None),
        ),
        out_specs=(P("region", "tile"), P(None, "region", "tile"), P("region", "tile")),
        check_vma=False,
    )
```

```python
import functools

import jax
import jax.numpy as jnp
from jax import lax
from jax.experimental import pallas as pl
from jax.experimental.pallas import tpu as pltpu
from jax.sharding import PartitionSpec as P

STEPS = 4
HALO = 4
LANES = 128
TOP = 8

GRAVITY = 9.81
COURANT = 0.45
SPACING = 1.0

VMEM_LIMIT = 20 << 20
FLUX_UNROLL = 7


SOURCE, DIFF, FIELDS = 3, 4, 7
SEND = 5
ALL, ROWS, REST = range(3)
STRIP_DIFF = 2 * HALO * SEND
STRIP_END = STRIP_DIFF + 2 * HALO * 3


def tiles_of(work):
    return (work.shape[0] - 2) // FIELDS


def active_at(work):
    return work.shape[0] - 2


def strip_at(work):
    return work.shape[0] - 1


def sent_plane(work, k, c):
    tiles = tiles_of(work)
    return (k * tiles + c, active_at(work), SOURCE * tiles + c)[max(k - 2, 0)]


def vmem_spec():
    return pl.BlockSpec(memory_space=pltpu.VMEM)


def hbm_spec():
    return pl.BlockSpec(memory_space=pltpu.HBM)


def vmem_out(*shape):
    return pltpu.VMEM(shape, jnp.float32)


def params():
    return pltpu.CompilerParams(vmem_limit_bytes=VMEM_LIMIT)


def cost(flops, nbytes):
    return pl.CostEstimate(flops=flops, bytes_accessed=nbytes, transcendentals=0)


def lane_ids(rows):
    return lax.broadcasted_iota(jnp.int32, (rows, LANES), 1)


def aligned(start, size):
    return pl.ds(pl.multiple_of(start, 8), size)


def speed_of(depth, along, across):
    root = lax.rsqrt(depth)
    inverse = root * root
    return jnp.maximum(jnp.abs(along), jnp.abs(across)) * inverse + jnp.sqrt(
        jnp.float32(GRAVITY)
    ) * (depth * root)


def spread_peak(acc, out_ref):
    top = jnp.max(jnp.max(acc, axis=0, keepdims=True), axis=1, keepdims=True)
    out_ref[...] = jnp.broadcast_to(top[None], out_ref.shape)


def start_kernel(
    wet_hbm,
    plan_hbm,
    cell_hbm,
    rate_hbm,
    depth_hbm,
    mom_hbm,
    work,
    plan_ref,
    peak_ref,
    up_ref,
    down_ref,
    wet_ref,
    plan_smem,
    cell_ref,
    rate_ref,
    small_sem,
    big_sem,
):
    rows, cols = depth_hbm.shape
    tiles = cols // LANES
    padded = work.shape[1]
    blocks = wet_hbm.shape[0]
    block_rows = rows // blocks
    bottom = TOP + rows
    small = [
        pltpu.make_async_copy(src, dst, small_sem.at[i])
        for i, (src, dst) in enumerate(
            [
                (cell_hbm, cell_ref),
                (rate_hbm, rate_ref),
                (wet_hbm, wet_ref),
                (plan_hbm, plan_smem),
            ]
        )
    ]
    big = []
    for k, src in enumerate([depth_hbm, mom_hbm.at[0], mom_hbm.at[1]]):
        for c in range(tiles):
            big.append(
                pltpu.make_async_copy(
                    src.at[:, pl.ds(c * LANES, LANES)],
                    work.at[k * tiles + c, pl.ds(TOP, rows), :],
                    big_sem.at[k, c],
                )
            )
    for copy in small + big:
        copy.start()
    for k in range(SEND):
        for c in range(tiles):
            plane = sent_plane(work, k, c)
            fill = 1.0 if k == 0 else 0.0
            work[plane, 0:TOP, :] = jnp.full((TOP, LANES), fill, jnp.float32)
            work[plane, bottom:padded, :] = jnp.full((padded - bottom, LANES), fill, jnp.float32)
    for c in range(tiles):
        work[SOURCE * tiles + c, TOP:bottom, :] = jnp.zeros((rows, LANES), jnp.float32)
    for copy in small:
        copy.wait()
    lane = lane_ids(1)

    def add_cell(i, carry):
        cell = cell_ref[i]
        row = lax.div(cell, cols)
        col = cell - row * cols
        c = lax.div(col, LANES)
        at = pl.ds(row + TOP, 1)
        work[SOURCE * tiles + c, at, :] += jnp.where(lane == col - c * LANES, rate_ref[i], 0.0)
        return carry

    lax.fori_loop(0, cell_ref.shape[0], add_cell, 0)
    for b in range(blocks):
        wet = wet_ref[b].astype(jnp.float32)
        at = slice(TOP + b * block_rows, TOP + (b + 1) * block_rows)
        work[active_at(work), at, :] = jnp.full((block_rows, LANES), wet)
        plan_ref[b] = jnp.full((1, LANES), plan_smem[b])
    for copy in big:
        copy.wait()
    for k in range(SEND):
        for c in range(tiles):
            plane = sent_plane(work, k, c)
            up_ref[k * tiles + c] = work[plane, TOP : TOP + HALO, :]
            down_ref[k * tiles + c] = work[plane, bottom - HALO : bottom, :]

    def one(r, acc):
        at = aligned(r * 8 + TOP, 8)
        active = work[active_at(work), at, :] > 0.5
        for c in range(tiles):
            speed = speed_of(*[work[k * tiles + c, at, :] for k in range(3)])
            acc = jnp.maximum(acc, jnp.where(active, speed, 0.0))
        return acc

    acc = lax.fori_loop(0, rows // 8, one, jnp.zeros((8, LANES), jnp.float32), unroll=8)
    spread_peak(acc, peak_ref)


def packed(work, at, lane):
    tiles = tiles_of(work)
    out = None
    for k in range(SEND):
        first, last = sent_plane(work, k, 0), sent_plane(work, k, tiles - 1)
        ends = jnp.where(lane < HALO, work[first, at, :], work[last, at, :])
        ends = pltpu.roll(ends, 2 * HALO * k + HALO, 1)
        out = ends if out is None else jnp.where(lane >= 2 * HALO * k, ends, out)
    return out


def split_packed(turned, left_ref, right_ref, at):
    for k in range(SEND):
        lo = 2 * HALO * k
        right_ref[k, :, at] = turned[lo : lo + HALO, :]
        left_ref[k, :, at] = turned[lo + HALO : lo + 2 * HALO, :]


def pack_kernel(work, left_ref, right_ref, pack):
    rows = pack.shape[0]
    lane = lane_ids(8)

    def one(r, carry):
        pack[aligned(r * 8, 8), :] = packed(work, aligned(r * 8 + TOP, 8), lane)
        return carry

    lax.fori_loop(0, rows // 8, one, 0, unroll=8)
    for q in range(rows // LANES):
        at = slice(q * LANES, (q + 1) * LANES)
        split_packed(pack[at, :].T, left_ref, right_ref, at)


def rows_kernel(
    work_in, left_in, right_in, above_ref, below_ref, work, left_ref, right_ref, pack
):
    tiles = tiles_of(work)
    own = left_ref.shape[2] - LANES
    bottom = TOP + own
    is_top = lax.axis_index("region") == 0
    is_bottom = lax.axis_index("region") == lax.axis_size("region") - 1

    def mirrored(first, step, to):
        for k in range(SEND):
            flip = -1.0 if k == 1 else 1.0
            for c in range(tiles):
                plane = sent_plane(work, k, c)
                for j in range(HALO):
                    work[plane, to - step * (1 + j), :] = work[plane, first + step * j, :] * flip

    def received(ref, lo):
        for k in range(SEND):
            for c in range(tiles):
                work[sent_plane(work, k, c), lo : lo + HALO, :] = ref[k * tiles + c]

    pl.when(is_top)(lambda: mirrored(TOP, 1, TOP))
    pl.when(jnp.logical_not(is_top))(lambda: received(above_ref, TOP - HALO))
    pl.when(is_bottom)(lambda: mirrored(bottom - 1, -1, bottom - 1))
    pl.when(jnp.logical_not(is_bottom))(lambda: received(below_ref, bottom))
    pack[...] = jnp.zeros_like(pack)
    lane = lane_ids(8)
    pack[0:8, :] = packed(work, slice(0, 8), lane)
    pack[8:16, :] = packed(work, slice(bottom, bottom + 8), lane)
    split_packed(pack[...].T, left_ref, right_ref, slice(own, own + LANES))


def columns_kernel(work_in, own_left, own_right, from_left, from_right, work, both):
    own = own_left.shape[2] - LANES
    bottom = TOP + own
    is_left = lax.axis_index("tile") == 0
    is_right = lax.axis_index("tile") == lax.axis_size("tile") - 1

    def mirrored(ref, to):
        for k in range(SEND):
            flip = -1.0 if k == 2 else 1.0
            for j in range(HALO):
                both[2 * HALO * k + to + HALO - 1 - j, :] = ref[k, j, :] * flip

    def received(ref, to):
        for k in range(SEND):
            at = 2 * HALO * k + to
            both[at : at + HALO, :] = ref[k]

    both[STRIP_DIFF:, :] = jnp.zeros((LANES - STRIP_DIFF, own + LANES), jnp.float32)
    pl.when(is_left)(lambda: mirrored(own_left, 0))
    pl.when(jnp.logical_not(is_left))(lambda: received(from_left, 0))
    pl.when(is_right)(lambda: mirrored(own_right, HALO))
    pl.when(jnp.logical_not(is_right))(lambda: received(from_right, HALO))
    strip = strip_at(work)
    for q in range(own // LANES):
        at = slice(q * LANES, (q + 1) * LANES)
        work[strip, TOP + q * LANES : TOP + (q + 1) * LANES, :] = both[:, at].T
    ends = both[:, own : own + LANES].T
    work[strip, 0:8, :] = ends[0:8, :]
    work[strip, bottom : bottom + 8, :] = ends[8:16, :]


def roe(left, right):
    depth_l, normal_l, tangent_l, root_l, sn_l, st_l, press_l, shear_l = left
    depth_r, normal_r, tangent_r, root_r, sn_r, st_r, press_r, shear_r = right
    weight = pl.reciprocal(root_l + root_r, approx=False)
    speed = (sn_l + sn_r) * weight
    drift = (st_l + st_r) * weight
    half = (0.5 * GRAVITY) * (depth_l + depth_r)
    inverse = lax.rsqrt(half)
    celerity = half * inverse
    jump = depth_r - depth_l
    excess = (normal_r - normal_l) - speed * jump
    bend = excess * (0.5 * inverse)
    half_jump = 0.5 * jump
    slow = speed - celerity
    fast = speed + celerity
    wave_one = jnp.abs(slow) * (half_jump - bend)
    wave_three = jnp.abs(fast) * (half_jump + bend)
    wave_two = jnp.abs(speed) * ((tangent_r - tangent_l) - drift * jump)
    both = wave_one + wave_three
    flux_depth = (normal_l + normal_r) - both
    flux_normal = (press_l + press_r) - speed * both - celerity * (wave_three - wave_one)
    flux_tangent = (shear_l + shear_r) - drift * both - wave_two
    return flux_depth, flux_normal, flux_tangent


def side(depth, normal, tangent, root, sn, st):
    press = sn * sn + (0.5 * GRAVITY) * (depth * depth)
    return (depth, normal, tangent, root, sn, st, press, sn * st)


def flux_kernel(part, work_in, work, beside, derived, faces):
    tiles = tiles_of(work)
    count = tiles if part == ROWS else tiles + 1
    padded = work.shape[1]
    row_tiles = padded // 8
    strip, active_rows = strip_at(work), active_at(work)
    lane = lane_ids(8)
    inside = (lane < HALO) | (lane >= LANES - HALO)

    def derive(r, carry):
        for i in range(5):
            at = aligned(r * 40 + i * 8, 8)
            packed_columns = work[strip, at, :]
            for k in range(SEND if part != ROWS else 0):
                out = pltpu.roll(packed_columns, LANES - HALO - 2 * HALO * k, 1)
                beside[k, at, :] = jnp.where(inside, out, 1.0) if k == 0 else out
            for c in range(count):
                state = own_state(c, at)
                inverse = lax.rsqrt(state[0])
                derived[c, at, :] = state[0] * inverse
                derived[tiles + 1 + c, at, :] = state[1] * inverse
                derived[2 * (tiles + 1) + c, at, :] = state[2] * inverse
        return carry

    def own_state(c, at):
        if c == tiles:
            return [beside[k, at, :] for k in range(3)]
        return [work[k * tiles + c, at, :] for k in range(3)]

    lax.fori_loop(0, row_tiles // 5, derive, 0)
    for f in range(3):
        for c in range(tiles + 1):
            faces[f * (tiles + 1) + c, 0:8, :] = jnp.zeros((8, LANES), jnp.float32)

    def load(c, at):
        return own_state(c, at) + [derived[k * (tiles + 1) + c, at, :] for k in range(3)]

    def flip(v):
        return (v[0], v[2], v[1], v[3], v[5], v[4])

    def fluxes(at, wrap):
        here, below = pl.ds(at, 8), pl.ds(at + 1, 8)
        now = [load(c, here) for c in range(count)]
        for c in range(count):
            if part == REST and c < tiles:
                continue
            under = [pltpu.roll(v, 7, 0) for v in now[c]] if wrap else load(c, below)
            flux = roe(side(*now[c]), side(*under))
            for f in range(3):
                faces[f * (tiles + 1) + c, pl.ds(at + 8, 8), :] = flux[f]

        def along_rows(f, c):
            plane = f * (tiles + 1) + c
            return faces[plane, pl.ds(at + 8, 8), :] - faces[plane, pl.ds(at + 7, 8), :]

        if part == ROWS:
            for f in range(3):
                for c in range(tiles):
                    work[(DIFF + f) * tiles + c, here, :] = along_rows(f, c)
            return
        across = []
        for c in range(count):
            right = [
                pltpu.roll(jnp.where(lane == 0, b, a), LANES - 1, 1)
                for a, b in zip(now[c], now[(c + 1) % count])
            ]
            f_depth, f_across, f_along = roe(side(*flip(now[c])), side(*flip(right)))
            across.append((f_depth, f_along, f_across))
        strip_out = work[strip, here, :]
        for c in range(count):
            prev = across[(c - 1) % count]
            own = c < tiles
            active = (work[active_rows, here, :] if own else beside[3, here, :]) > 0.5
            for f in range(3):
                left = pltpu.roll(jnp.where(lane == LANES - 1, prev[f], across[c][f]), 1, 1)
                if own and part == REST:
                    out = (across[c][f] - left) + work[(DIFF + f) * tiles + c, here, :]
                else:
                    out = (across[c][f] - left) + along_rows(f, c)
                if f == 0:
                    source = work[SOURCE * tiles + c, here, :] if own else beside[4, here, :]
                    out = out - 2.0 * source
                out = jnp.where(active, out, 0.0)
                if own:
                    work[(DIFF + f) * tiles + c, here, :] = out
                else:
                    lo = STRIP_DIFF + 2 * HALO * f
                    strip_out = jnp.where(lane >= lo, pltpu.roll(out, lo + HALO, 1), strip_out)
        work[strip, here, :] = strip_out

    def one(r, carry):
        fluxes(pl.multiple_of(r * 8, 8), False)
        return carry

    lax.fori_loop(0, row_tiles - 1, one, 0, unroll=FLUX_UNROLL)
    fluxes(padded - 8, True)


def step_ratio(peak_ref):
    peak = jnp.max(jnp.max(peak_ref[...], axis=0), axis=0, keepdims=True)
    step = (COURANT * SPACING) / peak
    return jnp.broadcast_to((0.5 / SPACING) * step, (8, LANES))


def moved(work, c, at, ratio):
    tiles = tiles_of(work)
    new = [
        work[f * tiles + c, at, :] - ratio * work[(DIFF + f) * tiles + c, at, :] for f in range(3)
    ]
    for f in range(3):
        work[f * tiles + c, at, :] = new[f]
    return new


def update_kernel(peak_ref, work_in, work, next_ref):
    tiles = tiles_of(work)
    row_tiles = work.shape[1] // 8
    strip = strip_at(work)
    ratio = step_ratio(peak_ref)
    lane = lane_ids(8)
    strip_ratio = jnp.where(lane < 2 * HALO * 3, ratio, 0.0)

    def move_strip(at):
        old = work[strip, at, :]
        work[strip, at, :] = old - strip_ratio * pltpu.roll(old, LANES - STRIP_DIFF, 1)

    def one(r, acc):
        at = aligned(r * 8 + TOP, 8)
        active = work[active_at(work), at, :] > 0.5
        for c in range(tiles):
            new = moved(work, c, at, ratio)
            acc = jnp.maximum(acc, jnp.where(active, speed_of(*new), 0.0))
        move_strip(at)
        return acc

    zero = jnp.zeros((8, LANES), jnp.float32)
    acc = lax.fori_loop(0, row_tiles - 2, one, zero, unroll=8)
    for at in (slice(0, 8), slice(8 * row_tiles - 8, 8 * row_tiles)):
        for c in range(tiles):
            moved(work, c, at, ratio)
        move_strip(at)
    spread_peak(acc, next_ref)


def last_kernel(peak_ref, plan_ref, work_in, work, next_ref, best):
    tiles = tiles_of(work)
    blocks = plan_ref.shape[0]
    block_rows = (work.shape[1] - 2 * 8) // blocks
    ratio = step_ratio(peak_ref)

    def one_block(b, carry):
        acc = jnp.zeros((8, LANES), jnp.float32)
        for r in range(0, block_rows, 8):
            at = aligned(b * block_rows + TOP + r, 8)
            for c in range(tiles):
                acc = jnp.maximum(acc, speed_of(*moved(work, c, at, ratio)))
        best[b] = acc
        return carry

    lax.fori_loop(0, blocks, one_block, 0, unroll=4)
    for t in range(next_ref.shape[0]):
        acc = jnp.zeros((8, LANES), jnp.float32)
        for b in range(blocks):
            acc = jnp.maximum(acc, jnp.where(plan_ref[b] == t, best[b], 0.0))
        top = jnp.max(acc, axis=0, keepdims=True)
        next_ref[t] = jnp.broadcast_to(jnp.max(top, axis=1, keepdims=True), (1, LANES))


def store_kernel(work, depth_hbm, mom_hbm, sem):
    rows, cols = depth_hbm.shape
    tiles = cols // LANES
    copies = []
    for k, dst in enumerate([depth_hbm, mom_hbm.at[0], mom_hbm.at[1]]):
        for c in range(tiles):
            copies.append(
                pltpu.make_async_copy(
                    work.at[k * tiles + c, pl.ds(TOP, rows), :],
                    dst.at[:, pl.ds(c * LANES, LANES)],
                    sem.at[k, c],
                )
            )
    for copy in copies:
        copy.start()
    for copy in copies:
        copy.wait()


def exchange(x, axes):
    return lax.all_to_all(x, axes, 0, 0)


def send(x, axis, forward):
    count = lax.axis_size(axis)
    pairs = [(i, i + 1) if forward else (i + 1, i) for i in range(count - 1)]
    return lax.ppermute(x, axis, pairs)


def on_device(water_depth, momentum, wet_mask, helper_plan, breach_cells, breach_rate):
    rows, cols = water_depth.shape
    tile_count = lax.axis_size("tile")
    everyone = tile_count * lax.axis_size("region")
    blocks = wet_mask.shape[0]
    tiles = cols // LANES
    padded = rows + 2 * 8
    f32 = jnp.float32
    cells = breach_cells.reshape(-1)
    rates = breach_rate.reshape(-1)
    nbytes = 4 * 3 * rows * cols
    work_out = vmem_out(FIELDS * tiles + 2, padded, LANES)
    strip_out = vmem_out(SEND, HALO, rows + LANES)
    edge_out = vmem_out(SEND * tiles, HALO, LANES)
    peak_out = vmem_out(everyone, 1, LANES)
    first_out = vmem_out(everyone, 2, LANES)

    work, plan, peak, up, down = pl.pallas_call(
        start_kernel,
        out_shape=(work_out, pltpu.VMEM((blocks, 1, LANES), jnp.int32), first_out, edge_out, edge_out),
        in_specs=[hbm_spec()] * 6,
        out_specs=(vmem_spec(),) * 5,
        scratch_shapes=[
            pltpu.SMEM((blocks,), jnp.int32),
            pltpu.SMEM((blocks,), jnp.int32),
            pltpu.SMEM(cells.shape, jnp.int32),
            pltpu.SMEM(cells.shape, f32),
            pltpu.SemaphoreType.DMA((4,)),
            pltpu.SemaphoreType.DMA((3, tiles)),
        ],
        compiler_params=params(),
        cost_estimate=cost(2 * rows * cols, nbytes),
        name="start",
    )(
        *(
            pltpu.with_memory_space_constraint(x, pltpu.HBM)
            for x in (
                wet_mask.reshape(-1),
                helper_plan.reshape(-1),
                cells,
                rates,
                water_depth,
                momentum,
            )
        )
    )

    peaks = exchange(peak, ("region", "tile"))
    above = send(down, "region", True)
    below = send(up, "region", False)

    left, right = pl.pallas_call(
        pack_kernel,
        out_shape=(strip_out, strip_out),
        in_specs=[vmem_spec()],
        out_specs=(vmem_spec(),) * 2,
        scratch_shapes=[pltpu.VMEM((rows, LANES), f32)],
        compiler_params=params(),
        cost_estimate=cost(20 * rows * cols, nbytes),
        name="pack",
    )(work)

    work, left, right = pl.pallas_call(
        rows_kernel,
        out_shape=(work_out, strip_out, strip_out),
        in_specs=[vmem_spec()] * 5,
        out_specs=(vmem_spec(),) * 3,
        scratch_shapes=[pltpu.VMEM((LANES, LANES), f32)],
        input_output_aliases={0: 0, 1: 1, 2: 2},
        compiler_params=params(),
        cost_estimate=cost(rows * cols, nbytes // 8),
        name="rows",
    )(work, left, right, above, below)

    from_left = send(right, "tile", True)
    from_right = send(left, "tile", False)

    def flux(part, work):
        share = (1.0, 0.35, 0.65)[part]
        return pl.pallas_call(
            functools.partial(flux_kernel, part),
            out_shape=work_out,
            in_specs=[vmem_spec()],
            out_specs=vmem_spec(),
            scratch_shapes=[
                pltpu.VMEM((SEND, padded, LANES), f32),
                pltpu.VMEM((3 * (tiles + 1), padded, LANES), f32),
                pltpu.VMEM((3 * (tiles + 1), padded + 8, LANES), f32),
            ],
            input_output_aliases={0: 0},
            compiler_params=params(),
            cost_estimate=cost(int(share * 150 * rows * cols), int(share * 4 * nbytes)),
            name="flux",
        )(work)

    work = flux(ROWS, work)
    work = pl.pallas_call(
        columns_kernel,
        out_shape=work_out,
        in_specs=[vmem_spec()] * 5,
        out_specs=vmem_spec(),
        scratch_shapes=[
            pltpu.VMEM((LANES, rows + LANES), f32),
        ],
        input_output_aliases={0: 0},
        compiler_params=params(),
        cost_estimate=cost(10 * rows * cols, nbytes),
        name="columns",
    )(work, left, right, from_left, from_right)

    for step in range(STEPS):
        work = flux(ALL if step else REST, work)
        if step < STEPS - 1:
            work, peak = pl.pallas_call(
                update_kernel,
                out_shape=(work_out, peak_out),
                in_specs=[vmem_spec()] * 2,
                out_specs=(vmem_spec(),) * 2,
                input_output_aliases={1: 0},
                compiler_params=params(),
                cost_estimate=cost(20 * rows * cols, nbytes),
                name="update",
            )(peaks, work)
            peaks = exchange(peak, ("region", "tile"))

    work, best = pl.pallas_call(
        last_kernel,
        out_shape=(work_out, vmem_out(tile_count, 1, LANES)),
        in_specs=[vmem_spec()] * 3,
        out_specs=(vmem_spec(),) * 2,
        scratch_shapes=[pltpu.VMEM((blocks, 8, LANES), f32)],
        input_output_aliases={2: 0},
        compiler_params=params(),
        cost_estimate=cost(20 * rows * cols, 2 * nbytes),
        name="last",
    )(peaks, plan, work)
    helpers = exchange(best, "tile")
    new_depth, new_momentum = pl.pallas_call(
        store_kernel,
        out_shape=(
            jax.ShapeDtypeStruct((rows, cols), f32),
            jax.ShapeDtypeStruct((2, rows, cols), f32),
        ),
        in_specs=[vmem_spec()],
        out_specs=(hbm_spec(),) * 2,
        scratch_shapes=[pltpu.SemaphoreType.DMA((3, tiles))],
        compiler_params=params(),
        cost_estimate=cost(10 * rows * cols, 2 * nbytes),
        name="store",
    )(work)
    return new_depth, new_momentum, jnp.max(helpers[:, :, :1], axis=0)


def solution(mesh):
    return jax.shard_map(
        on_device,
        mesh=mesh,
        in_specs=(
            P("region", "tile"),
            P(None, "region", "tile"),
            P("region", "tile"),
            P("region", "tile"),
            P("region", "tile", None),
            P("region", "tile", None),
        ),
        out_specs=(P("region", "tile"), P(None, "region", "tile"), P("region", "tile")),
        check_vma=False,
    )
```

```python
import jax
import jax.numpy as jnp
from jax import lax
from jax.experimental import pallas as pl
from jax.experimental.pallas import tpu as pltpu
from jax.sharding import PartitionSpec as P

STEPS = 4
HALO = 4
LANES = 128
TOP = 8

GRAVITY = 9.81
COURANT = 0.45
SPACING = 1.0

VMEM_LIMIT = 20 << 20
FLUX_UNROLL = 7


SOURCE, DIFF, FIELDS = 3, 4, 7
SEND = 5
STRIP_DIFF = 2 * HALO * SEND
STRIP_END = STRIP_DIFF + 2 * HALO * 3


def tiles_of(work):
    return (work.shape[0] - 2) // FIELDS


def active_at(work):
    return work.shape[0] - 2


def strip_at(work):
    return work.shape[0] - 1


def sent_plane(work, k, c):
    tiles = tiles_of(work)
    return (k * tiles + c, active_at(work), SOURCE * tiles + c)[max(k - 2, 0)]


def vmem_spec():
    return pl.BlockSpec(memory_space=pltpu.VMEM)


def hbm_spec():
    return pl.BlockSpec(memory_space=pltpu.HBM)


def vmem_out(*shape):
    return pltpu.VMEM(shape, jnp.float32)


def params():
    return pltpu.CompilerParams(vmem_limit_bytes=VMEM_LIMIT)


def cost(flops, nbytes):
    return pl.CostEstimate(flops=flops, bytes_accessed=nbytes, transcendentals=0)


def lane_ids(rows):
    return lax.broadcasted_iota(jnp.int32, (rows, LANES), 1)


def aligned(start, size):
    return pl.ds(pl.multiple_of(start, 8), size)


def speed_of(depth, along, across):
    root = lax.rsqrt(depth)
    inverse = root * root
    return jnp.maximum(jnp.abs(along), jnp.abs(across)) * inverse + jnp.sqrt(
        jnp.float32(GRAVITY)
    ) * (depth * root)


def spread_peak(acc, out_ref):
    top = jnp.max(jnp.max(acc, axis=0, keepdims=True), axis=1, keepdims=True)
    out_ref[...] = jnp.broadcast_to(top[None], out_ref.shape)


def start_kernel(
    wet_hbm,
    plan_hbm,
    cell_hbm,
    rate_hbm,
    depth_hbm,
    mom_hbm,
    work,
    plan_ref,
    up_ref,
    down_ref,
    wet_ref,
    plan_smem,
    cell_ref,
    rate_ref,
    small_sem,
    big_sem,
):
    rows, cols = depth_hbm.shape
    tiles = cols // LANES
    padded = work.shape[1]
    blocks = wet_hbm.shape[0]
    block_rows = rows // blocks
    bottom = TOP + rows
    small = [
        pltpu.make_async_copy(src, dst, small_sem.at[i])
        for i, (src, dst) in enumerate(
            [
                (cell_hbm, cell_ref),
                (rate_hbm, rate_ref),
                (wet_hbm, wet_ref),
                (plan_hbm, plan_smem),
            ]
        )
    ]
    big = []
    for k, src in enumerate([depth_hbm, mom_hbm.at[0], mom_hbm.at[1]]):
        for c in range(tiles):
            big.append(
                pltpu.make_async_copy(
                    src.at[:, pl.ds(c * LANES, LANES)],
                    work.at[k * tiles + c, pl.ds(TOP, rows), :],
                    big_sem.at[k, c],
                )
            )
    for copy in small + big:
        copy.start()
    for k in range(SEND):
        for c in range(tiles):
            plane = sent_plane(work, k, c)
            fill = 1.0 if k == 0 else 0.0
            work[plane, 0:TOP, :] = jnp.full((TOP, LANES), fill, jnp.float32)
            work[plane, bottom:padded, :] = jnp.full((padded - bottom, LANES), fill, jnp.float32)
    for c in range(tiles):
        work[SOURCE * tiles + c, TOP:bottom, :] = jnp.zeros((rows, LANES), jnp.float32)
    for copy in small:
        copy.wait()
    lane = lane_ids(1)

    def add_cell(i, carry):
        cell = cell_ref[i]
        row = lax.div(cell, cols)
        col = cell - row * cols
        c = lax.div(col, LANES)
        at = pl.ds(row + TOP, 1)
        work[SOURCE * tiles + c, at, :] += jnp.where(lane == col - c * LANES, rate_ref[i], 0.0)
        return carry

    lax.fori_loop(0, cell_ref.shape[0], add_cell, 0)
    for b in range(blocks):
        wet = wet_ref[b].astype(jnp.float32)
        at = slice(TOP + b * block_rows, TOP + (b + 1) * block_rows)
        work[active_at(work), at, :] = jnp.full((block_rows, LANES), wet)
        plan_ref[b] = jnp.full((1, LANES), plan_smem[b])
    for copy in big:
        copy.wait()
    for k in range(SEND):
        for c in range(tiles):
            plane = sent_plane(work, k, c)
            up_ref[k * tiles + c] = work[plane, TOP : TOP + HALO, :]
            down_ref[k * tiles + c] = work[plane, bottom - HALO : bottom, :]


def packed(work, at, lane):
    tiles = tiles_of(work)
    out = None
    for k in range(SEND):
        first, last = sent_plane(work, k, 0), sent_plane(work, k, tiles - 1)
        ends = jnp.where(lane < HALO, work[first, at, :], work[last, at, :])
        ends = pltpu.roll(ends, 2 * HALO * k + HALO, 1)
        out = ends if out is None else jnp.where(lane >= 2 * HALO * k, ends, out)
    return out


def split_packed(turned, left_ref, right_ref, at):
    for k in range(SEND):
        lo = 2 * HALO * k
        right_ref[k, :, at] = turned[lo : lo + HALO, :]
        left_ref[k, :, at] = turned[lo + HALO : lo + 2 * HALO, :]


def pack_kernel(work, peak_ref, left_ref, right_ref, pack):
    tiles = tiles_of(work)
    rows = pack.shape[0]
    lane = lane_ids(8)

    def one(r, acc):
        at = aligned(r * 8 + TOP, 8)
        pack[aligned(r * 8, 8), :] = packed(work, at, lane)
        active = work[active_at(work), at, :] > 0.5
        for c in range(tiles):
            speed = speed_of(*[work[k * tiles + c, at, :] for k in range(3)])
            acc = jnp.maximum(acc, jnp.where(active, speed, 0.0))
        return acc

    acc = lax.fori_loop(0, rows // 8, one, jnp.zeros((8, LANES), jnp.float32), unroll=8)
    spread_peak(acc, peak_ref)
    for q in range(rows // LANES):
        at = slice(q * LANES, (q + 1) * LANES)
        split_packed(pack[at, :].T, left_ref, right_ref, at)


def rows_kernel(
    work_in, left_in, right_in, above_ref, below_ref, work, left_ref, right_ref, pack
):
    tiles = tiles_of(work)
    own = left_ref.shape[2] - LANES
    bottom = TOP + own
    is_top = lax.axis_index("region") == 0
    is_bottom = lax.axis_index("region") == lax.axis_size("region") - 1

    def mirrored(first, step, to):
        for k in range(SEND):
            flip = -1.0 if k == 1 else 1.0
            for c in range(tiles):
                plane = sent_plane(work, k, c)
                for j in range(HALO):
                    work[plane, to - step * (1 + j), :] = work[plane, first + step * j, :] * flip

    def received(ref, lo):
        for k in range(SEND):
            for c in range(tiles):
                work[sent_plane(work, k, c), lo : lo + HALO, :] = ref[k * tiles + c]

    pl.when(is_top)(lambda: mirrored(TOP, 1, TOP))
    pl.when(jnp.logical_not(is_top))(lambda: received(above_ref, TOP - HALO))
    pl.when(is_bottom)(lambda: mirrored(bottom - 1, -1, bottom - 1))
    pl.when(jnp.logical_not(is_bottom))(lambda: received(below_ref, bottom))
    pack[...] = jnp.zeros_like(pack)
    lane = lane_ids(8)
    pack[0:8, :] = packed(work, slice(0, 8), lane)
    pack[8:16, :] = packed(work, slice(bottom, bottom + 8), lane)
    split_packed(pack[...].T, left_ref, right_ref, slice(own, own + LANES))


def columns_kernel(work_in, own_left, own_right, from_left, from_right, work, both):
    own = own_left.shape[2] - LANES
    bottom = TOP + own
    is_left = lax.axis_index("tile") == 0
    is_right = lax.axis_index("tile") == lax.axis_size("tile") - 1

    def mirrored(ref, to):
        for k in range(SEND):
            flip = -1.0 if k == 2 else 1.0
            for j in range(HALO):
                both[2 * HALO * k + to + HALO - 1 - j, :] = ref[k, j, :] * flip

    def received(ref, to):
        for k in range(SEND):
            at = 2 * HALO * k + to
            both[at : at + HALO, :] = ref[k]

    both[STRIP_DIFF:, :] = jnp.zeros((LANES - STRIP_DIFF, own + LANES), jnp.float32)
    pl.when(is_left)(lambda: mirrored(own_left, 0))
    pl.when(jnp.logical_not(is_left))(lambda: received(from_left, 0))
    pl.when(is_right)(lambda: mirrored(own_right, HALO))
    pl.when(jnp.logical_not(is_right))(lambda: received(from_right, HALO))
    strip = strip_at(work)
    for q in range(own // LANES):
        at = slice(q * LANES, (q + 1) * LANES)
        work[strip, TOP + q * LANES : TOP + (q + 1) * LANES, :] = both[:, at].T
    ends = both[:, own : own + LANES].T
    work[strip, 0:8, :] = ends[0:8, :]
    work[strip, bottom : bottom + 8, :] = ends[8:16, :]


def roe(left, right):
    depth_l, normal_l, tangent_l, root_l, sn_l, st_l, press_l, shear_l = left
    depth_r, normal_r, tangent_r, root_r, sn_r, st_r, press_r, shear_r = right
    weight = pl.reciprocal(root_l + root_r, approx=False)
    speed = (sn_l + sn_r) * weight
    drift = (st_l + st_r) * weight
    half = (0.5 * GRAVITY) * (depth_l + depth_r)
    inverse = lax.rsqrt(half)
    celerity = half * inverse
    jump = depth_r - depth_l
    excess = (normal_r - normal_l) - speed * jump
    bend = excess * (0.5 * inverse)
    half_jump = 0.5 * jump
    slow = speed - celerity
    fast = speed + celerity
    wave_one = jnp.abs(slow) * (half_jump - bend)
    wave_three = jnp.abs(fast) * (half_jump + bend)
    wave_two = jnp.abs(speed) * ((tangent_r - tangent_l) - drift * jump)
    both = wave_one + wave_three
    flux_depth = (normal_l + normal_r) - both
    flux_normal = (press_l + press_r) - speed * both - celerity * (wave_three - wave_one)
    flux_tangent = (shear_l + shear_r) - drift * both - wave_two
    return flux_depth, flux_normal, flux_tangent


def side(depth, normal, tangent, root, sn, st):
    press = sn * sn + (0.5 * GRAVITY) * (depth * depth)
    return (depth, normal, tangent, root, sn, st, press, sn * st)


def flux_kernel(work_in, work, beside, derived, faces):
    tiles = tiles_of(work)
    padded = work.shape[1]
    row_tiles = padded // 8
    strip, active_rows = strip_at(work), active_at(work)
    lane = lane_ids(8)
    inside = (lane < HALO) | (lane >= LANES - HALO)

    def derive(r, carry):
        for i in range(5):
            at = aligned(r * 40 + i * 8, 8)
            packed_columns = work[strip, at, :]
            for k in range(SEND):
                out = pltpu.roll(packed_columns, LANES - HALO - 2 * HALO * k, 1)
                beside[k, at, :] = jnp.where(inside, out, 1.0) if k == 0 else out
            for c in range(tiles + 1):
                state = own_state(c, at)
                inverse = lax.rsqrt(state[0])
                derived[c, at, :] = state[0] * inverse
                derived[tiles + 1 + c, at, :] = state[1] * inverse
                derived[2 * (tiles + 1) + c, at, :] = state[2] * inverse
        return carry

    def own_state(c, at):
        if c == tiles:
            return [beside[k, at, :] for k in range(3)]
        return [work[k * tiles + c, at, :] for k in range(3)]

    lax.fori_loop(0, row_tiles // 5, derive, 0, unroll=5)
    for f in range(3):
        for c in range(tiles + 1):
            faces[f * (tiles + 1) + c, 0:8, :] = jnp.zeros((8, LANES), jnp.float32)

    def load(c, at):
        return own_state(c, at) + [derived[k * (tiles + 1) + c, at, :] for k in range(3)]

    def flip(v):
        return (v[0], v[2], v[1], v[3], v[5], v[4])

    def row_faces(at, wrap):
        here, below = pl.ds(at, 8), pl.ds(at + 1, 8)
        now = [load(c, here) for c in range(tiles + 1)]
        across = []
        for c in range(tiles + 1):
            nxt = now[(c + 1) % (tiles + 1)]
            right = [
                pltpu.roll(jnp.where(lane == 0, b, a), LANES - 1, 1)
                for a, b in zip(now[c], nxt)
            ]
            f_depth, f_across, f_along = roe(side(*flip(now[c])), side(*flip(right)))
            across.append((f_depth, f_along, f_across))
            under = [pltpu.roll(v, 7, 0) for v in now[c]] if wrap else load(c, below)
            flux = roe(side(*now[c]), side(*under))
            for f in range(3):
                faces[f * (tiles + 1) + c, pl.ds(at + 8, 8), :] = flux[f]
        strip_out = work[strip, here, :]
        for c in range(tiles + 1):
            prev = across[(c - 1) % (tiles + 1)]
            own = c < tiles
            active = (work[active_rows, here, :] if own else beside[3, here, :]) > 0.5
            for f in range(3):
                left = pltpu.roll(jnp.where(lane == LANES - 1, prev[f], across[c][f]), 1, 1)
                plane = f * (tiles + 1) + c
                out = (across[c][f] - left) + (
                    faces[plane, pl.ds(at + 8, 8), :] - faces[plane, pl.ds(at + 7, 8), :]
                )
                if f == 0:
                    source = work[SOURCE * tiles + c, here, :] if own else beside[4, here, :]
                    out = out - 2.0 * source
                out = jnp.where(active, out, 0.0)
                if own:
                    work[(DIFF + f) * tiles + c, here, :] = out
                else:
                    lo = STRIP_DIFF + 2 * HALO * f
                    strip_out = jnp.where(lane >= lo, pltpu.roll(out, lo + HALO, 1), strip_out)
        work[strip, here, :] = strip_out

    def one(r, carry):
        row_faces(pl.multiple_of(r * 8, 8), False)
        return carry

    lax.fori_loop(0, row_tiles - 1, one, 0, unroll=FLUX_UNROLL)
    row_faces(padded - 8, True)


def step_ratio(peak_ref):
    peak = jnp.max(jnp.max(peak_ref[...], axis=0), axis=0, keepdims=True)
    step = (COURANT * SPACING) / peak
    return jnp.broadcast_to((0.5 / SPACING) * step, (8, LANES))


def moved(work, c, at, ratio):
    tiles = tiles_of(work)
    return [
        work[f * tiles + c, at, :] - ratio * work[(DIFF + f) * tiles + c, at, :] for f in range(3)
    ]


def move_own(work, at, ratio):
    tiles = tiles_of(work)
    for c in range(tiles):
        for f, new in enumerate(moved(work, c, at, ratio)):
            work[f * tiles + c, at, :] = new


def update_kernel(peak_ref, work_in, work, next_hbm, spread, sem):
    tiles = tiles_of(work)
    row_tiles = work.shape[1] // 8
    strip = strip_at(work)
    ratio = step_ratio(peak_ref)

    def find(r, acc):
        at = aligned(r * 8 + TOP, 8)
        active = work[active_at(work), at, :] > 0.5
        for c in range(tiles):
            acc = jnp.maximum(acc, jnp.where(active, speed_of(*moved(work, c, at, ratio)), 0.0))
        return acc

    zero = jnp.zeros((8, LANES), jnp.float32)
    spread_peak(lax.fori_loop(0, row_tiles - 2, find, zero, unroll=16), spread)
    copy = pltpu.make_async_copy(spread, next_hbm, sem)
    copy.start()
    strip_ratio = jnp.where(lane_ids(8) < 2 * HALO * 3, ratio, 0.0)

    def move(r, carry):
        at = aligned(r * 8, 8)
        move_own(work, at, ratio)
        old = work[strip, at, :]
        work[strip, at, :] = old - strip_ratio * pltpu.roll(old, LANES - STRIP_DIFF, 1)
        return carry

    lax.fori_loop(0, row_tiles, move, 0, unroll=10)
    copy.wait()


def last_kernel(peak_ref, plan_ref, work, next_ref, best):
    tiles = tiles_of(work)
    blocks = plan_ref.shape[0]
    block_rows = (work.shape[1] - 2 * 8) // blocks
    ratio = step_ratio(peak_ref)

    def one_block(b, carry):
        acc = jnp.zeros((8, LANES), jnp.float32)
        for r in range(0, block_rows, 8):
            at = aligned(b * block_rows + TOP + r, 8)
            for c in range(tiles):
                acc = jnp.maximum(acc, speed_of(*moved(work, c, at, ratio)))
        best[b] = acc
        return carry

    lax.fori_loop(0, blocks, one_block, 0, unroll=8)
    for t in range(next_ref.shape[0]):
        acc = jnp.zeros((8, LANES), jnp.float32)
        for b in range(blocks):
            acc = jnp.maximum(acc, jnp.where(plan_ref[b] == t, best[b], 0.0))
        top = jnp.max(acc, axis=0, keepdims=True)
        next_ref[t] = jnp.broadcast_to(jnp.max(top, axis=1, keepdims=True), (1, LANES))


def store_kernel(peak_ref, work_in, work, depth_hbm, mom_hbm, sem):
    rows, cols = depth_hbm.shape
    tiles = cols // LANES
    ratio = step_ratio(peak_ref)

    def move(r, carry):
        move_own(work, aligned(r * 8 + TOP, 8), ratio)
        return carry

    lax.fori_loop(0, rows // 8, move, 0, unroll=8)
    copies = []
    for k, dst in enumerate([depth_hbm, mom_hbm.at[0], mom_hbm.at[1]]):
        for c in range(tiles):
            copies.append(
                pltpu.make_async_copy(
                    work.at[k * tiles + c, pl.ds(TOP, rows), :],
                    dst.at[:, pl.ds(c * LANES, LANES)],
                    sem.at[k, c],
                )
            )
    for copy in copies:
        copy.start()
    for copy in copies:
        copy.wait()


def exchange(x, axes):
    return lax.all_to_all(x, axes, 0, 0)


def send(x, axis, forward):
    count = lax.axis_size(axis)
    pairs = [(i, (i + 1) % count) if forward else ((i + 1) % count, i) for i in range(count)]
    return lax.ppermute(x, axis, pairs)


def on_device(water_depth, momentum, wet_mask, helper_plan, breach_cells, breach_rate):
    rows, cols = water_depth.shape
    tile_count = lax.axis_size("tile")
    everyone = tile_count * lax.axis_size("region")
    blocks = wet_mask.shape[0]
    tiles = cols // LANES
    padded = rows + 2 * 8
    f32 = jnp.float32
    cells = breach_cells.reshape(-1)
    rates = breach_rate.reshape(-1)
    nbytes = 4 * 3 * rows * cols
    work_out = vmem_out(FIELDS * tiles + 2, padded, LANES)
    strip_out = vmem_out(SEND, HALO, rows + LANES)
    edge_out = vmem_out(SEND * tiles, HALO, LANES)
    peak_out = vmem_out(everyone, 1, LANES)

    work, plan, up, down = pl.pallas_call(
        start_kernel,
        out_shape=(work_out, pltpu.VMEM((blocks, 1, LANES), jnp.int32), edge_out, edge_out),
        in_specs=[hbm_spec()] * 6,
        out_specs=(vmem_spec(),) * 4,
        scratch_shapes=[
            pltpu.SMEM((blocks,), jnp.int32),
            pltpu.SMEM((blocks,), jnp.int32),
            pltpu.SMEM(cells.shape, jnp.int32),
            pltpu.SMEM(cells.shape, f32),
            pltpu.SemaphoreType.DMA((4,)),
            pltpu.SemaphoreType.DMA((3, tiles)),
        ],
        compiler_params=params(),
        cost_estimate=cost(2 * rows * cols, nbytes),
        name="start",
    )(
        *(
            pltpu.with_memory_space_constraint(x, pltpu.HBM)
            for x in (
                wet_mask.reshape(-1),
                helper_plan.reshape(-1),
                cells,
                rates,
                water_depth,
                momentum,
            )
        )
    )

    above = send(down, "region", True)
    below = send(up, "region", False)

    peak, left, right = pl.pallas_call(
        pack_kernel,
        out_shape=(peak_out, strip_out, strip_out),
        in_specs=[vmem_spec()],
        out_specs=(vmem_spec(),) * 3,
        scratch_shapes=[pltpu.VMEM((rows, LANES), f32)],
        compiler_params=params(),
        cost_estimate=cost(20 * rows * cols, nbytes),
        name="pack",
    )(work)

    work, left, right = pl.pallas_call(
        rows_kernel,
        out_shape=(work_out, strip_out, strip_out),
        in_specs=[vmem_spec()] * 5,
        out_specs=(vmem_spec(),) * 3,
        scratch_shapes=[pltpu.VMEM((LANES, LANES), f32)],
        input_output_aliases={0: 0, 1: 1, 2: 2},
        compiler_params=params(),
        cost_estimate=cost(rows * cols, nbytes // 8),
        name="rows",
    )(work, left, right, above, below)

    from_left = send(right, "tile", True)
    from_right = send(left, "tile", False)
    peaks = exchange(peak, ("region", "tile"))

    work = pl.pallas_call(
        columns_kernel,
        out_shape=work_out,
        in_specs=[vmem_spec()] * 5,
        out_specs=vmem_spec(),
        scratch_shapes=[
            pltpu.VMEM((LANES, rows + LANES), f32),
        ],
        input_output_aliases={0: 0},
        compiler_params=params(),
        cost_estimate=cost(10 * rows * cols, nbytes),
        name="columns",
    )(work, left, right, from_left, from_right)

    for step in range(STEPS):
        work = pl.pallas_call(
            flux_kernel,
            out_shape=work_out,
            in_specs=[vmem_spec()],
            out_specs=vmem_spec(),
            scratch_shapes=[
                pltpu.VMEM((SEND, padded, LANES), f32),
                pltpu.VMEM((3 * (tiles + 1), padded, LANES), f32),
                pltpu.VMEM((3 * (tiles + 1), padded + 8, LANES), f32),
            ],
            input_output_aliases={0: 0},
            compiler_params=params(),
            cost_estimate=cost(150 * rows * cols, 4 * nbytes),
            name="flux",
        )(work)
        if step < STEPS - 1:
            work, peak = pl.pallas_call(
                update_kernel,
                out_shape=(work_out, jax.ShapeDtypeStruct((everyone, 1, LANES), f32)),
                in_specs=[vmem_spec()] * 2,
                out_specs=(vmem_spec(), hbm_spec()),
                scratch_shapes=[
                    pltpu.VMEM((everyone, 1, LANES), f32),
                    pltpu.SemaphoreType.DMA,
                ],
                input_output_aliases={1: 0},
                compiler_params=params(),
                cost_estimate=cost(20 * rows * cols, nbytes),
                name="update",
            )(peaks, work)
            peaks = exchange(peak, ("region", "tile"))

    best = pl.pallas_call(
        last_kernel,
        out_shape=vmem_out(tile_count, 1, LANES),
        in_specs=[vmem_spec()] * 3,
        out_specs=vmem_spec(),
        scratch_shapes=[pltpu.VMEM((blocks, 8, LANES), f32)],
        compiler_params=params(),
        cost_estimate=cost(20 * rows * cols, 2 * nbytes),
        name="last",
    )(peaks, plan, work)
    helpers = exchange(best, "tile")
    work, new_depth, new_momentum = pl.pallas_call(
        store_kernel,
        out_shape=(
            work_out,
            jax.ShapeDtypeStruct((rows, cols), f32),
            jax.ShapeDtypeStruct((2, rows, cols), f32),
        ),
        in_specs=[vmem_spec()] * 2,
        out_specs=(vmem_spec(), hbm_spec(), hbm_spec()),
        scratch_shapes=[pltpu.SemaphoreType.DMA((3, tiles))],
        input_output_aliases={1: 0},
        compiler_params=params(),
        cost_estimate=cost(10 * rows * cols, 2 * nbytes),
        name="store",
    )(peaks, work)
    return new_depth, new_momentum, jnp.max(helpers[:, :, :1], axis=0)


def solution(mesh):
    return jax.shard_map(
        on_device,
        mesh=mesh,
        in_specs=(
            P("region", "tile"),
            P(None, "region", "tile"),
            P("region", "tile"),
            P("region", "tile"),
            P("region", "tile", None),
            P("region", "tile", None),
        ),
        out_specs=(P("region", "tile"), P(None, "region", "tile"), P("region", "tile")),
        check_vma=False,
    )
```

```python
import functools

import jax
import jax.numpy as jnp
from jax import lax
from jax.experimental import pallas as pl
from jax.experimental.pallas import tpu as pltpu
from jax.sharding import PartitionSpec as P

STEPS = 4
HALO = 4
LANES = 128
TOP = 8

GRAVITY = 9.81
COURANT = 0.45
SPACING = 1.0

VMEM_LIMIT = 20 << 20
FLUX_UNROLL = 7
FLUX_COST = ((150, 4), (150, 4), (20, 1))


SOURCE, DIFF, FIELDS = 3, 4, 7
SEND = 5
STRIP_DIFF, STRIP_FIELDS = 5, 8
ALL, MAIN, EDGE = range(3)


def tiles_of(work):
    return (work.shape[0] - 1) // FIELDS


def active_at(work):
    return work.shape[0] - 1


def sent_plane(work, k, c):
    tiles = tiles_of(work)
    return (k * tiles + c, active_at(work), SOURCE * tiles + c)[max(k - 2, 0)]


def vmem_spec():
    return pl.BlockSpec(memory_space=pltpu.VMEM)


def hbm_spec():
    return pl.BlockSpec(memory_space=pltpu.HBM)


def vmem_out(*shape):
    return pltpu.VMEM(shape, jnp.float32)


def params():
    return pltpu.CompilerParams(vmem_limit_bytes=VMEM_LIMIT)


def cost(flops, nbytes):
    return pl.CostEstimate(flops=flops, bytes_accessed=nbytes, transcendentals=0)


def lane_ids(rows):
    return lax.broadcasted_iota(jnp.int32, (rows, LANES), 1)


def aligned(start, size):
    return pl.ds(pl.multiple_of(start, 8), size)


def speed_of(depth, along, across):
    root = lax.rsqrt(depth)
    inverse = root * root
    return jnp.maximum(jnp.abs(along), jnp.abs(across)) * inverse + jnp.sqrt(
        jnp.float32(GRAVITY)
    ) * (depth * root)


def spread_peak(acc, out_ref):
    top = jnp.max(jnp.max(acc, axis=0, keepdims=True), axis=1, keepdims=True)
    out_ref[...] = jnp.broadcast_to(top[None], out_ref.shape)


def start_kernel(
    wet_hbm,
    plan_hbm,
    cell_hbm,
    rate_hbm,
    depth_hbm,
    mom_hbm,
    work,
    plan_ref,
    up_ref,
    down_ref,
    wet_ref,
    plan_smem,
    cell_ref,
    rate_ref,
    small_sem,
    big_sem,
):
    rows, cols = depth_hbm.shape
    tiles = cols // LANES
    padded = work.shape[1]
    blocks = wet_hbm.shape[0]
    block_rows = rows // blocks
    bottom = TOP + rows
    small = [
        pltpu.make_async_copy(src, dst, small_sem.at[i])
        for i, (src, dst) in enumerate(
            [
                (cell_hbm, cell_ref),
                (rate_hbm, rate_ref),
                (wet_hbm, wet_ref),
                (plan_hbm, plan_smem),
            ]
        )
    ]
    big = []
    for k, src in enumerate([depth_hbm, mom_hbm.at[0], mom_hbm.at[1]]):
        for c in range(tiles):
            big.append(
                pltpu.make_async_copy(
                    src.at[:, pl.ds(c * LANES, LANES)],
                    work.at[k * tiles + c, pl.ds(TOP, rows), :],
                    big_sem.at[k, c],
                )
            )
    for copy in small + big:
        copy.start()
    for k in range(SEND):
        for c in range(tiles):
            plane = sent_plane(work, k, c)
            fill = 1.0 if k == 0 else 0.0
            work[plane, 0:TOP, :] = jnp.full((TOP, LANES), fill, jnp.float32)
            work[plane, bottom:padded, :] = jnp.full((padded - bottom, LANES), fill, jnp.float32)
    for c in range(tiles):
        work[SOURCE * tiles + c, TOP:bottom, :] = jnp.zeros((rows, LANES), jnp.float32)
    for copy in small:
        copy.wait()
    lane = lane_ids(1)

    def add_cell(i, carry):
        cell = cell_ref[i]
        row = lax.div(cell, cols)
        col = cell - row * cols
        c = lax.div(col, LANES)
        at = pl.ds(row + TOP, 1)
        work[SOURCE * tiles + c, at, :] += jnp.where(lane == col - c * LANES, rate_ref[i], 0.0)
        return carry

    lax.fori_loop(0, cell_ref.shape[0], add_cell, 0)
    for b in range(blocks):
        wet = wet_ref[b].astype(jnp.float32)
        at = slice(TOP + b * block_rows, TOP + (b + 1) * block_rows)
        work[active_at(work), at, :] = jnp.full((block_rows, LANES), wet)
        plan_ref[b] = jnp.full((1, LANES), plan_smem[b])
    for copy in big:
        copy.wait()
    for k in range(SEND):
        for c in range(tiles):
            plane = sent_plane(work, k, c)
            up_ref[k * tiles + c] = work[plane, TOP : TOP + HALO, :]
            down_ref[k * tiles + c] = work[plane, bottom - HALO : bottom, :]


def packed(work, at, lane):
    tiles = tiles_of(work)
    out = None
    for k in range(SEND):
        first, last = sent_plane(work, k, 0), sent_plane(work, k, tiles - 1)
        ends = jnp.where(lane < HALO, work[first, at, :], work[last, at, :])
        ends = pltpu.roll(ends, 2 * HALO * k + HALO, 1)
        out = ends if out is None else jnp.where(lane >= 2 * HALO * k, ends, out)
    return out


def split_packed(turned, left_ref, right_ref, at):
    for k in range(SEND):
        lo = 2 * HALO * k
        right_ref[k, :, at] = turned[lo : lo + HALO, :]
        left_ref[k, :, at] = turned[lo + HALO : lo + 2 * HALO, :]


def pack_kernel(work, peak_ref, left_ref, right_ref, pack):
    tiles = tiles_of(work)
    rows = pack.shape[0]
    lane = lane_ids(8)

    def one(r, acc):
        at = aligned(r * 8 + TOP, 8)
        pack[aligned(r * 8, 8), :] = packed(work, at, lane)
        active = work[active_at(work), at, :] > 0.5
        for c in range(tiles):
            speed = speed_of(*[work[k * tiles + c, at, :] for k in range(3)])
            acc = jnp.maximum(acc, jnp.where(active, speed, 0.0))
        return acc

    acc = lax.fori_loop(0, rows // 8, one, jnp.zeros((8, LANES), jnp.float32), unroll=8)
    spread_peak(acc, peak_ref)
    for q in range(rows // LANES):
        at = slice(q * LANES, (q + 1) * LANES)
        split_packed(pack[at, :].T, left_ref, right_ref, at)


def rows_kernel(
    work_in, left_in, right_in, above_ref, below_ref, work, left_ref, right_ref, pack
):
    tiles = tiles_of(work)
    own = left_ref.shape[2] - LANES
    bottom = TOP + own
    is_top = lax.axis_index("region") == 0
    is_bottom = lax.axis_index("region") == lax.axis_size("region") - 1

    def mirrored(first, step, to):
        for k in range(SEND):
            flip = -1.0 if k == 1 else 1.0
            for c in range(tiles):
                plane = sent_plane(work, k, c)
                for j in range(HALO):
                    work[plane, to - step * (1 + j), :] = work[plane, first + step * j, :] * flip

    def received(ref, lo):
        for k in range(SEND):
            for c in range(tiles):
                work[sent_plane(work, k, c), lo : lo + HALO, :] = ref[k * tiles + c]

    pl.when(is_top)(lambda: mirrored(TOP, 1, TOP))
    pl.when(jnp.logical_not(is_top))(lambda: received(above_ref, TOP - HALO))
    pl.when(is_bottom)(lambda: mirrored(bottom - 1, -1, bottom - 1))
    pl.when(jnp.logical_not(is_bottom))(lambda: received(below_ref, bottom))
    pack[...] = jnp.zeros_like(pack)
    lane = lane_ids(8)
    pack[0:8, :] = packed(work, slice(bottom, bottom + 8), lane)
    pack[LANES - 8 :, :] = packed(work, slice(0, 8), lane)
    split_packed(pack[...].T, left_ref, right_ref, slice(own, own + LANES))


def columns_kernel(own_left, own_right, from_left, from_right, strips):
    is_left = lax.axis_index("tile") == 0
    is_right = lax.axis_index("tile") == lax.axis_size("tile") - 1

    def mirrored(ref, side, to):
        for k in range(SEND):
            flip = -1.0 if k == 2 else 1.0
            for j in range(HALO):
                strips[side, k, to + HALO - 1 - j, :] = ref[k, j, :] * flip

    def received(ref, side, to):
        for k in range(SEND):
            strips[side, k, to : to + HALO, :] = ref[k]

    received(own_left, 0, HALO)
    received(own_right, 1, 0)
    pl.when(is_left)(lambda: mirrored(own_left, 0, 0))
    pl.when(jnp.logical_not(is_left))(lambda: received(from_left, 0, 0))
    pl.when(is_right)(lambda: mirrored(own_right, 1, HALO))
    pl.when(jnp.logical_not(is_right))(lambda: received(from_right, 1, HALO))


def roe(left, right):
    depth_l, normal_l, tangent_l, root_l, sn_l, st_l, press_l, shear_l = left
    depth_r, normal_r, tangent_r, root_r, sn_r, st_r, press_r, shear_r = right
    weight = pl.reciprocal(root_l + root_r, approx=False)
    speed = (sn_l + sn_r) * weight
    drift = (st_l + st_r) * weight
    half = (0.5 * GRAVITY) * (depth_l + depth_r)
    inverse = lax.rsqrt(half)
    celerity = half * inverse
    jump = depth_r - depth_l
    excess = (normal_r - normal_l) - speed * jump
    bend = excess * (0.5 * inverse)
    half_jump = 0.5 * jump
    slow = speed - celerity
    fast = speed + celerity
    wave_one = jnp.abs(slow) * (half_jump - bend)
    wave_three = jnp.abs(fast) * (half_jump + bend)
    wave_two = jnp.abs(speed) * ((tangent_r - tangent_l) - drift * jump)
    both = wave_one + wave_three
    flux_depth = (normal_l + normal_r) - both
    flux_normal = (press_l + press_r) - speed * both - celerity * (wave_three - wave_one)
    flux_tangent = (shear_l + shear_r) - drift * both - wave_two
    return flux_depth, flux_normal, flux_tangent


def side(depth, normal, tangent, root, sn, st):
    press = sn * sn + (0.5 * GRAVITY) * (depth * depth)
    return (depth, normal, tangent, root, sn, st, press, sn * st)


def flip(v):
    return (v[0], v[2], v[1], v[3], v[5], v[4])


def with_roots(depth, along, across):
    inverse = lax.rsqrt(depth)
    return [depth, along, across, depth * inverse, along * inverse, across * inverse]


def strip_fluxes(strips, ghost_rows):
    chunks = strips.shape[3] // LANES
    lane = lane_ids(8)
    for s in range(2):
        spans = [slice(q * LANES, (q + 1) * LANES) for q in range(chunks)]
        now = [with_roots(*[strips[s, k, :, at] for k in range(3)]) for at in spans]
        rows = []
        for q in range(chunks):
            below = [
                pltpu.roll(jnp.where(lane == 0, b, a), LANES - 1, 1)
                for a, b in zip(now[q], now[(q + 1) % chunks])
            ]
            rows.append(roe(side(*now[q]), side(*below)))
        for q, at in enumerate(spans):
            right = [pltpu.roll(v, 7, 0) for v in now[q]]
            f_depth, f_across, f_along = roe(side(*flip(now[q])), side(*flip(right)))
            active = strips[s, 3, :, at] > 0.5
            for f, flux in enumerate((f_depth, f_along, f_across)):
                above = jnp.where(lane == LANES - 1, rows[q - 1][f], rows[q][f])
                out = (flux - pltpu.roll(flux, 1, 0)) + (rows[q][f] - pltpu.roll(above, 1, 1))
                if f == 0:
                    out = out - 2.0 * strips[s, 4, :, at]
                strips[s, STRIP_DIFF + f, :, at] = jnp.where(active, out, 0.0)
                ghost_rows[3 * s + f, at] = flux[HALO - 1, :]


def turn_ghosts(ghost_rows, ghost):
    own = ghost_rows.shape[1] - LANES
    for q in range(own // LANES):
        at = slice(q * LANES, (q + 1) * LANES)
        ghost[TOP + q * LANES : TOP + (q + 1) * LANES, :] = ghost_rows[:, at].T
    ends = ghost_rows[:, own : own + LANES].T
    ghost[TOP + own : TOP + own + 8, :] = ends[0:8, :]
    ghost[0:8, :] = ends[LANES - 8 :, :]


def flux_kernel(part, *refs):
    if part == MAIN:
        work_in, work, derived, faces = refs
    elif part == EDGE:
        work_in, strips_in, work, strips, ghost_rows, ghost = refs
    else:
        work_in, strips_in, work, strips, derived, faces, ghost_rows, ghost = refs
    tiles = tiles_of(work)
    padded = work.shape[1]
    row_tiles = padded // 8
    active_rows = active_at(work)
    lane = lane_ids(8)
    first, last = lane == 0, lane == LANES - 1
    if part != MAIN:
        strip_fluxes(strips, ghost_rows)
        turn_ghosts(ghost_rows, ghost)

    def edge_fluxes(at):
        values = ghost[at, :]
        return [pltpu.roll(values, LANES - 1 - i, 1) for i in range(6)]

    if part == EDGE:

        def fix(r, carry):
            at = aligned(r * 8, 8)
            edges = edge_fluxes(at)
            active = work[active_rows, at, :] > 0.5
            for f in range(3):
                left, right = DIFF * tiles + f * tiles, DIFF * tiles + f * tiles + tiles - 1
                gone = jnp.where(active & first, pltpu.roll(edges[f], 1, 1), 0.0)
                work[left, at, :] = work[left, at, :] - gone
                gone = jnp.where(active & last, edges[3 + f], 0.0)
                work[right, at, :] = work[right, at, :] + gone
            return carry

        lax.fori_loop(0, row_tiles, fix, 0, unroll=10)
        return

    def derive(r, carry):
        for i in range(5):
            at = aligned(r * 40 + i * 8, 8)
            for c in range(tiles):
                roots = with_roots(*[work[k * tiles + c, at, :] for k in range(3)])
                for k in range(3):
                    derived[k * tiles + c, at, :] = roots[3 + k]
        return carry

    lax.fori_loop(0, row_tiles // 5, derive, 0, unroll=2)
    for p in range(3 * tiles):
        faces[p, 0:8, :] = jnp.zeros((8, LANES), jnp.float32)

    def load(c, at):
        return [ref[k * tiles + c, at, :] for ref in (work, derived) for k in range(3)]

    def fluxes(at, wrap):
        here, below = pl.ds(at, 8), pl.ds(at + 1, 8)
        now = [load(c, here) for c in range(tiles)]
        across = []
        for c in range(tiles):
            right = [
                pltpu.roll(jnp.where(first, b, a), LANES - 1, 1)
                for a, b in zip(now[c], now[(c + 1) % tiles])
            ]
            f_depth, f_across, f_along = roe(side(*flip(now[c])), side(*flip(right)))
            across.append([f_depth, f_along, f_across])
            under = [pltpu.roll(v, 7, 0) for v in now[c]] if wrap else load(c, below)
            flux = roe(side(*now[c]), side(*under))
            for f in range(3):
                faces[f * tiles + c, pl.ds(at + 8, 8), :] = flux[f]
        if part == ALL:
            edges = edge_fluxes(here)
        else:
            edges = [jnp.zeros((8, LANES), jnp.float32)] * 6
        for f in range(3):
            across[-1][f] = jnp.where(last, edges[3 + f], across[-1][f])
        active = work[active_rows, here, :] > 0.5
        for c in range(tiles):
            prev = across[c - 1] if c else edges
            for f in range(3):
                left = pltpu.roll(jnp.where(last, prev[f], across[c][f]), 1, 1)
                plane = f * tiles + c
                out = (across[c][f] - left) + (
                    faces[plane, pl.ds(at + 8, 8), :] - faces[plane, pl.ds(at + 7, 8), :]
                )
                if f == 0:
                    out = out - 2.0 * work[SOURCE * tiles + c, here, :]
                work[(DIFF + f) * tiles + c, here, :] = jnp.where(active, out, 0.0)

    def one(r, carry):
        fluxes(pl.multiple_of(r * 8, 8), False)
        return carry

    lax.fori_loop(0, row_tiles - 1, one, 0, unroll=FLUX_UNROLL)
    fluxes(padded - 8, True)


def step_ratio(peak_ref):
    peak = jnp.max(jnp.max(peak_ref[...], axis=0), axis=0, keepdims=True)
    step = (COURANT * SPACING) / peak
    return jnp.broadcast_to((0.5 / SPACING) * step, (8, LANES))


def moved(work, c, at, ratio):
    tiles = tiles_of(work)
    return [
        work[f * tiles + c, at, :] - ratio * work[(DIFF + f) * tiles + c, at, :] for f in range(3)
    ]


def move_own(work, at, ratio):
    tiles = tiles_of(work)
    for c in range(tiles):
        for f, new in enumerate(moved(work, c, at, ratio)):
            work[f * tiles + c, at, :] = new


def update_kernel(peak_ref, work_in, strips_in, work, strips, next_hbm, spread, sem):
    tiles = tiles_of(work)
    row_tiles = work.shape[1] // 8
    ratio = step_ratio(peak_ref)

    def find(r, acc):
        at = aligned(r * 8 + TOP, 8)
        active = work[active_at(work), at, :] > 0.5
        for c in range(tiles):
            acc = jnp.maximum(acc, jnp.where(active, speed_of(*moved(work, c, at, ratio)), 0.0))
        return acc

    zero = jnp.zeros((8, LANES), jnp.float32)
    spread_peak(lax.fori_loop(0, row_tiles - 2, find, zero, unroll=16), spread)
    copy = pltpu.make_async_copy(spread, next_hbm, sem)
    copy.start()
    for q in range(strips.shape[3] // LANES):
        span = slice(q * LANES, (q + 1) * LANES)
        for k in range(3):
            for s in range(2):
                strips[s, k, :, span] -= ratio * strips[s, STRIP_DIFF + k, :, span]

    def move(r, carry):
        move_own(work, aligned(r * 8, 8), ratio)
        return carry

    lax.fori_loop(0, row_tiles, move, 0, unroll=10)
    copy.wait()


def last_kernel(peak_ref, plan_ref, work, next_ref, best):
    tiles = tiles_of(work)
    blocks = plan_ref.shape[0]
    block_rows = (work.shape[1] - 2 * 8) // blocks
    ratio = step_ratio(peak_ref)

    def one_block(b, carry):
        acc = jnp.zeros((8, LANES), jnp.float32)
        for r in range(0, block_rows, 8):
            at = aligned(b * block_rows + TOP + r, 8)
            for c in range(tiles):
                acc = jnp.maximum(acc, speed_of(*moved(work, c, at, ratio)))
        best[b] = acc
        return carry

    lax.fori_loop(0, blocks, one_block, 0, unroll=8)
    for t in range(next_ref.shape[0]):
        acc = jnp.zeros((8, LANES), jnp.float32)
        for b in range(blocks):
            acc = jnp.maximum(acc, jnp.where(plan_ref[b] == t, best[b], 0.0))
        top = jnp.max(acc, axis=0, keepdims=True)
        next_ref[t] = jnp.broadcast_to(jnp.max(top, axis=1, keepdims=True), (1, LANES))


def store_kernel(peak_ref, work_in, work, depth_hbm, mom_hbm, sem):
    rows, cols = depth_hbm.shape
    tiles = cols // LANES
    ratio = step_ratio(peak_ref)

    def move(r, carry):
        move_own(work, aligned(r * 8 + TOP, 8), ratio)
        return carry

    lax.fori_loop(0, rows // 8, move, 0, unroll=8)
    copies = []
    for k, dst in enumerate([depth_hbm, mom_hbm.at[0], mom_hbm.at[1]]):
        for c in range(tiles):
            copies.append(
                pltpu.make_async_copy(
                    work.at[k * tiles + c, pl.ds(TOP, rows), :],
                    dst.at[:, pl.ds(c * LANES, LANES)],
                    sem.at[k, c],
                )
            )
    for copy in copies:
        copy.start()
    for copy in copies:
        copy.wait()


def exchange(x, axes):
    return lax.all_to_all(x, axes, 0, 0)


def send(x, axis, forward):
    count = lax.axis_size(axis)
    pairs = [(i, (i + 1) % count) if forward else ((i + 1) % count, i) for i in range(count)]
    return lax.ppermute(x, axis, pairs)


def on_device(water_depth, momentum, wet_mask, helper_plan, breach_cells, breach_rate):
    rows, cols = water_depth.shape
    tile_count = lax.axis_size("tile")
    everyone = tile_count * lax.axis_size("region")
    blocks = wet_mask.shape[0]
    tiles = cols // LANES
    padded = rows + 2 * 8
    f32 = jnp.float32
    cells = breach_cells.reshape(-1)
    rates = breach_rate.reshape(-1)
    nbytes = 4 * 3 * rows * cols
    work_out = vmem_out(FIELDS * tiles + 1, padded, LANES)
    strips_out = vmem_out(2, STRIP_FIELDS, 2 * HALO, rows + LANES)
    strip_out = vmem_out(SEND, HALO, rows + LANES)
    edge_out = vmem_out(SEND * tiles, HALO, LANES)
    peak_out = vmem_out(everyone, 1, LANES)

    work, plan, up, down = pl.pallas_call(
        start_kernel,
        out_shape=(work_out, pltpu.VMEM((blocks, 1, LANES), jnp.int32), edge_out, edge_out),
        in_specs=[hbm_spec()] * 6,
        out_specs=(vmem_spec(),) * 4,
        scratch_shapes=[
            pltpu.SMEM((blocks,), jnp.int32),
            pltpu.SMEM((blocks,), jnp.int32),
            pltpu.SMEM(cells.shape, jnp.int32),
            pltpu.SMEM(cells.shape, f32),
            pltpu.SemaphoreType.DMA((4,)),
            pltpu.SemaphoreType.DMA((3, tiles)),
        ],
        compiler_params=params(),
        cost_estimate=cost(2 * rows * cols, nbytes),
        name="start",
    )(
        *(
            pltpu.with_memory_space_constraint(x, pltpu.HBM)
            for x in (
                wet_mask.reshape(-1),
                helper_plan.reshape(-1),
                cells,
                rates,
                water_depth,
                momentum,
            )
        )
    )

    above = send(down, "region", True)
    below = send(up, "region", False)

    peak, left, right = pl.pallas_call(
        pack_kernel,
        out_shape=(peak_out, strip_out, strip_out),
        in_specs=[vmem_spec()],
        out_specs=(vmem_spec(),) * 3,
        scratch_shapes=[pltpu.VMEM((rows, LANES), f32)],
        compiler_params=params(),
        cost_estimate=cost(20 * rows * cols, nbytes),
        name="pack",
    )(work)

    work, left, right = pl.pallas_call(
        rows_kernel,
        out_shape=(work_out, strip_out, strip_out),
        in_specs=[vmem_spec()] * 5,
        out_specs=(vmem_spec(),) * 3,
        scratch_shapes=[pltpu.VMEM((LANES, LANES), f32)],
        input_output_aliases={0: 0, 1: 1, 2: 2},
        compiler_params=params(),
        cost_estimate=cost(rows * cols, nbytes // 8),
        name="rows",
    )(work, left, right, above, below)

    from_left = send(right, "tile", True)
    from_right = send(left, "tile", False)
    peaks = exchange(peak, ("region", "tile"))

    def flux(part, work, *strips):
        outs = (work_out, strips_out)[: 1 + len(strips)]
        main = [
            pltpu.VMEM((3 * tiles, padded, LANES), f32),
            pltpu.VMEM((3 * tiles, padded + 8, LANES), f32),
        ]
        edge = [pltpu.VMEM((LANES, rows + LANES), f32), pltpu.VMEM((padded, LANES), f32)]
        flops, moved_bytes = FLUX_COST[part]
        return pl.pallas_call(
            functools.partial(flux_kernel, part),
            out_shape=outs,
            in_specs=[vmem_spec()] * len(outs),
            out_specs=(vmem_spec(),) * len(outs),
            scratch_shapes=(main + edge, main, edge)[part],
            input_output_aliases={i: i for i in range(len(outs))},
            compiler_params=params(),
            cost_estimate=cost(int(flops * rows * cols), int(moved_bytes * nbytes)),
            name=("flux", "main", "edge")[part],
        )(work, *strips)

    (work,) = flux(MAIN, work)
    strips = pl.pallas_call(
        columns_kernel,
        out_shape=strips_out,
        in_specs=[vmem_spec()] * 4,
        out_specs=vmem_spec(),
        compiler_params=params(),
        cost_estimate=cost(rows * cols, nbytes // 8),
        name="columns",
    )(left, right, from_left, from_right)

    for step in range(STEPS):
        work, strips = flux(ALL if step else EDGE, work, strips)
        if step < STEPS - 1:
            work, strips, peak = pl.pallas_call(
                update_kernel,
                out_shape=(
                    work_out,
                    strips_out,
                    jax.ShapeDtypeStruct((everyone, 1, LANES), f32),
                ),
                in_specs=[vmem_spec()] * 3,
                out_specs=(vmem_spec(), vmem_spec(), hbm_spec()),
                scratch_shapes=[
                    pltpu.VMEM((everyone, 1, LANES), f32),
                    pltpu.SemaphoreType.DMA,
                ],
                input_output_aliases={1: 0, 2: 1},
                compiler_params=params(),
                cost_estimate=cost(20 * rows * cols, nbytes),
                name="update",
            )(peaks, work, strips)
            peaks = exchange(peak, ("region", "tile"))

    best = pl.pallas_call(
        last_kernel,
        out_shape=vmem_out(tile_count, 1, LANES),
        in_specs=[vmem_spec()] * 3,
        out_specs=vmem_spec(),
        scratch_shapes=[pltpu.VMEM((blocks, 8, LANES), f32)],
        compiler_params=params(),
        cost_estimate=cost(20 * rows * cols, 2 * nbytes),
        name="last",
    )(peaks, plan, work)
    helpers = exchange(best, "tile")
    work, new_depth, new_momentum = pl.pallas_call(
        store_kernel,
        out_shape=(
            work_out,
            jax.ShapeDtypeStruct((rows, cols), f32),
            jax.ShapeDtypeStruct((2, rows, cols), f32),
        ),
        in_specs=[vmem_spec()] * 2,
        out_specs=(vmem_spec(), hbm_spec(), hbm_spec()),
        scratch_shapes=[pltpu.SemaphoreType.DMA((3, tiles))],
        input_output_aliases={1: 0},
        compiler_params=params(),
        cost_estimate=cost(10 * rows * cols, 2 * nbytes),
        name="store",
    )(peaks, work)
    return new_depth, new_momentum, jnp.max(helpers[:, :, :1], axis=0)


def solution(mesh):
    return jax.shard_map(
        on_device,
        mesh=mesh,
        in_specs=(
            P("region", "tile"),
            P(None, "region", "tile"),
            P("region", "tile"),
            P("region", "tile"),
            P("region", "tile", None),
            P("region", "tile", None),
        ),
        out_specs=(P("region", "tile"), P(None, "region", "tile"), P("region", "tile")),
        check_vma=False,
    )
```

```python
import functools

import jax
import jax.numpy as jnp
from jax import lax
from jax.experimental import pallas as pl
from jax.experimental.pallas import tpu as pltpu
from jax.sharding import PartitionSpec as P

STEPS = 4
HALO = 4
LANES = 128
TOP = 8

GRAVITY = 9.81
COURANT = 0.45
SPACING = 1.0

VMEM_LIMIT = 20 << 20
FLUX_UNROLL = 7
FIRST = 2
FLUX_COST = ((150, 4), (150, 4), (500, 20))


SOURCE, DIFF, FIELDS = 3, 4, 7
SEND = 5
STRIP_DIFF, STRIP_FIELDS = 5, 8
ALL, MAIN, EDGE = range(3)


def tiles_of(work):
    return (work.shape[0] - 1) // FIELDS


def active_at(work):
    return work.shape[0] - 1


def sent_plane(work, k, c):
    tiles = tiles_of(work)
    return (k * tiles + c, active_at(work), SOURCE * tiles + c)[max(k - 2, 0)]


def vmem_spec():
    return pl.BlockSpec(memory_space=pltpu.VMEM)


def hbm_spec():
    return pl.BlockSpec(memory_space=pltpu.HBM)


def vmem_out(*shape):
    return pltpu.VMEM(shape, jnp.float32)


def params():
    return pltpu.CompilerParams(vmem_limit_bytes=VMEM_LIMIT)


def cost(flops, nbytes):
    return pl.CostEstimate(flops=flops, bytes_accessed=nbytes, transcendentals=0)


def lane_ids(rows):
    return lax.broadcasted_iota(jnp.int32, (rows, LANES), 1)


def aligned(start, size):
    return pl.ds(pl.multiple_of(start, 8), size)


def speed_of(depth, along, across):
    root = lax.rsqrt(depth)
    inverse = root * root
    return jnp.maximum(jnp.abs(along), jnp.abs(across)) * inverse + jnp.sqrt(
        jnp.float32(GRAVITY)
    ) * (depth * root)


def spread_peak(acc, out_ref):
    top = jnp.max(jnp.max(acc, axis=0, keepdims=True), axis=1, keepdims=True)
    out_ref[...] = jnp.broadcast_to(top[None], out_ref.shape)


def start_kernel(
    wet_hbm,
    plan_hbm,
    cell_hbm,
    rate_hbm,
    depth_hbm,
    mom_hbm,
    work,
    plan_ref,
    up_ref,
    down_ref,
    wet_ref,
    plan_smem,
    cell_ref,
    rate_ref,
    small_sem,
    big_sem,
):
    rows, cols = depth_hbm.shape
    tiles = cols // LANES
    padded = work.shape[1]
    blocks = wet_hbm.shape[0]
    block_rows = rows // blocks
    bottom = TOP + rows
    small = [
        pltpu.make_async_copy(src, dst, small_sem.at[i])
        for i, (src, dst) in enumerate(
            [
                (cell_hbm, cell_ref),
                (rate_hbm, rate_ref),
                (wet_hbm, wet_ref),
                (plan_hbm, plan_smem),
            ]
        )
    ]
    big = []
    for k, src in enumerate([depth_hbm, mom_hbm.at[0], mom_hbm.at[1]]):
        for c in range(tiles):
            big.append(
                pltpu.make_async_copy(
                    src.at[:, pl.ds(c * LANES, LANES)],
                    work.at[k * tiles + c, pl.ds(TOP, rows), :],
                    big_sem.at[k, c],
                )
            )
    for copy in small + big:
        copy.start()
    for k in range(SEND):
        for c in range(tiles):
            plane = sent_plane(work, k, c)
            fill = 1.0 if k == 0 else 0.0
            work[plane, 0:TOP, :] = jnp.full((TOP, LANES), fill, jnp.float32)
            work[plane, bottom:padded, :] = jnp.full((padded - bottom, LANES), fill, jnp.float32)
    for c in range(tiles):
        work[SOURCE * tiles + c, TOP:bottom, :] = jnp.zeros((rows, LANES), jnp.float32)
    for copy in small:
        copy.wait()
    lane = lane_ids(1)

    def add_cell(i, carry):
        cell = cell_ref[i]
        row = lax.div(cell, cols)
        col = cell - row * cols
        c = lax.div(col, LANES)
        at = pl.ds(row + TOP, 1)
        work[SOURCE * tiles + c, at, :] += jnp.where(lane == col - c * LANES, rate_ref[i], 0.0)
        return carry

    lax.fori_loop(0, cell_ref.shape[0], add_cell, 0)
    for b in range(blocks):
        wet = wet_ref[b].astype(jnp.float32)
        at = slice(TOP + b * block_rows, TOP + (b + 1) * block_rows)
        work[active_at(work), at, :] = jnp.full((block_rows, LANES), wet)
        plan_ref[b] = jnp.full((1, LANES), plan_smem[b])
    for copy in big:
        copy.wait()
    for k in range(SEND):
        for c in range(tiles):
            plane = sent_plane(work, k, c)
            up_ref[k * tiles + c] = work[plane, TOP : TOP + HALO, :]
            down_ref[k * tiles + c] = work[plane, bottom - HALO : bottom, :]


def packed(work, at, lane):
    tiles = tiles_of(work)
    out = None
    for k in range(SEND):
        first, last = sent_plane(work, k, 0), sent_plane(work, k, tiles - 1)
        ends = jnp.where(lane < HALO, work[first, at, :], work[last, at, :])
        ends = pltpu.roll(ends, 2 * HALO * k + HALO, 1)
        out = ends if out is None else jnp.where(lane >= 2 * HALO * k, ends, out)
    return out


def split_packed(turned, left_ref, right_ref, at):
    for k in range(SEND):
        lo = 2 * HALO * k
        right_ref[k, :, at] = turned[lo : lo + HALO, :]
        left_ref[k, :, at] = turned[lo + HALO : lo + 2 * HALO, :]


def pack_kernel(work, peak_hbm, left_ref, right_ref, pack, spread, sem):
    tiles = tiles_of(work)
    rows = pack.shape[0]
    lane = lane_ids(8)

    def find(r, acc):
        at = aligned(r * 8 + TOP, 8)
        active = work[active_at(work), at, :] > 0.5
        for c in range(tiles):
            speed = speed_of(*[work[k * tiles + c, at, :] for k in range(3)])
            acc = jnp.maximum(acc, jnp.where(active, speed, 0.0))
        return acc

    zero = jnp.zeros((8, LANES), jnp.float32)
    spread_peak(lax.fori_loop(0, rows // 8, find, zero, unroll=16), spread)
    copy = pltpu.make_async_copy(spread, peak_hbm, sem)
    copy.start()

    def one(r, carry):
        pack[aligned(r * 8, 8), :] = packed(work, aligned(r * 8 + TOP, 8), lane)
        return carry

    lax.fori_loop(0, rows // 8, one, 0, unroll=8)
    for q in range(rows // LANES):
        at = slice(q * LANES, (q + 1) * LANES)
        split_packed(pack[at, :].T, left_ref, right_ref, at)
    copy.wait()


def rows_kernel(
    work_in, left_in, right_in, above_ref, below_ref, work, left_ref, right_ref, pack
):
    tiles = tiles_of(work)
    own = left_ref.shape[2] - LANES
    bottom = TOP + own
    is_top = lax.axis_index("region") == 0
    is_bottom = lax.axis_index("region") == lax.axis_size("region") - 1

    def mirrored(first, step, to):
        for k in range(SEND):
            flip = -1.0 if k == 1 else 1.0
            for c in range(tiles):
                plane = sent_plane(work, k, c)
                for j in range(HALO):
                    work[plane, to - step * (1 + j), :] = work[plane, first + step * j, :] * flip

    def received(ref, lo):
        for k in range(SEND):
            for c in range(tiles):
                work[sent_plane(work, k, c), lo : lo + HALO, :] = ref[k * tiles + c]

    pl.when(is_top)(lambda: mirrored(TOP, 1, TOP))
    pl.when(jnp.logical_not(is_top))(lambda: received(above_ref, TOP - HALO))
    pl.when(is_bottom)(lambda: mirrored(bottom - 1, -1, bottom - 1))
    pl.when(jnp.logical_not(is_bottom))(lambda: received(below_ref, bottom))
    pack[...] = jnp.zeros_like(pack)
    lane = lane_ids(8)
    pack[0:8, :] = packed(work, slice(bottom, bottom + 8), lane)
    pack[LANES - 8 :, :] = packed(work, slice(0, 8), lane)
    split_packed(pack[...].T, left_ref, right_ref, slice(own, own + LANES))


def columns_kernel(own_left, own_right, from_left, from_right, strips):
    is_left = lax.axis_index("tile") == 0
    is_right = lax.axis_index("tile") == lax.axis_size("tile") - 1

    def mirrored(ref, side, to):
        for k in range(SEND):
            flip = -1.0 if k == 2 else 1.0
            for j in range(HALO):
                strips[side, k, to + HALO - 1 - j, :] = ref[k, j, :] * flip

    def received(ref, side, to):
        for k in range(SEND):
            strips[side, k, to : to + HALO, :] = ref[k]

    received(own_left, 0, HALO)
    received(own_right, 1, 0)
    pl.when(is_left)(lambda: mirrored(own_left, 0, 0))
    pl.when(jnp.logical_not(is_left))(lambda: received(from_left, 0, 0))
    pl.when(is_right)(lambda: mirrored(own_right, 1, HALO))
    pl.when(jnp.logical_not(is_right))(lambda: received(from_right, 1, HALO))


def roe(left, right):
    depth_l, normal_l, tangent_l, root_l, sn_l, st_l, press_l, shear_l = left
    depth_r, normal_r, tangent_r, root_r, sn_r, st_r, press_r, shear_r = right
    weight = pl.reciprocal(root_l + root_r, approx=False)
    speed = (sn_l + sn_r) * weight
    drift = (st_l + st_r) * weight
    half = (0.5 * GRAVITY) * (depth_l + depth_r)
    inverse = lax.rsqrt(half)
    celerity = half * inverse
    jump = depth_r - depth_l
    excess = (normal_r - normal_l) - speed * jump
    bend = excess * (0.5 * inverse)
    half_jump = 0.5 * jump
    slow = speed - celerity
    fast = speed + celerity
    wave_one = jnp.abs(slow) * (half_jump - bend)
    wave_three = jnp.abs(fast) * (half_jump + bend)
    wave_two = jnp.abs(speed) * ((tangent_r - tangent_l) - drift * jump)
    both = wave_one + wave_three
    flux_depth = (normal_l + normal_r) - both
    flux_normal = (press_l + press_r) - speed * both - celerity * (wave_three - wave_one)
    flux_tangent = (shear_l + shear_r) - drift * both - wave_two
    return flux_depth, flux_normal, flux_tangent


def side(depth, normal, tangent, root, sn, st):
    press = sn * sn + (0.5 * GRAVITY) * (depth * depth)
    return (depth, normal, tangent, root, sn, st, press, sn * st)


def flip(v):
    return (v[0], v[2], v[1], v[3], v[5], v[4])


def with_roots(depth, along, across):
    inverse = lax.rsqrt(depth)
    return [depth, along, across, depth * inverse, along * inverse, across * inverse]


def strip_fluxes(strips, ghost_rows):
    chunks = strips.shape[3] // LANES
    lane = lane_ids(8)
    for s in range(2):
        spans = [slice(q * LANES, (q + 1) * LANES) for q in range(chunks)]
        now = [with_roots(*[strips[s, k, :, at] for k in range(3)]) for at in spans]
        rows = []
        for q in range(chunks):
            below = [
                pltpu.roll(jnp.where(lane == 0, b, a), LANES - 1, 1)
                for a, b in zip(now[q], now[(q + 1) % chunks])
            ]
            rows.append(roe(side(*now[q]), side(*below)))
        for q, at in enumerate(spans):
            right = [pltpu.roll(v, 7, 0) for v in now[q]]
            f_depth, f_across, f_along = roe(side(*flip(now[q])), side(*flip(right)))
            active = strips[s, 3, :, at] > 0.5
            for f, flux in enumerate((f_depth, f_along, f_across)):
                above = jnp.where(lane == LANES - 1, rows[q - 1][f], rows[q][f])
                out = (flux - pltpu.roll(flux, 1, 0)) + (rows[q][f] - pltpu.roll(above, 1, 1))
                if f == 0:
                    out = out - 2.0 * strips[s, 4, :, at]
                strips[s, STRIP_DIFF + f, :, at] = jnp.where(active, out, 0.0)
                ghost_rows[(2 * f - s) % LANES, at] = flux[HALO - 1, :]


def turn_ghosts(ghost_rows, ghost):
    own = ghost_rows.shape[1] - LANES
    for q in range(own // LANES):
        at = slice(q * LANES, (q + 1) * LANES)
        ghost[TOP + q * LANES : TOP + (q + 1) * LANES, :] = ghost_rows[:, at].T
    ends = ghost_rows[:, own : own + LANES].T
    ghost[TOP + own : TOP + own + 8, :] = ends[0:8, :]
    ghost[0:8, :] = ends[LANES - 8 :, :]


def flux_kernel(part, *refs):
    if part == MAIN:
        work_in, work, derived, faces = refs
    elif part == EDGE:
        work_in, strips_in, work, strips, ghost_rows, ghost = refs
    else:
        work_in, strips_in, work, strips, derived, faces, ghost_rows, ghost = refs
    tiles = tiles_of(work)
    padded = work.shape[1]
    row_tiles = padded // 8
    active_rows = active_at(work)
    lane = lane_ids(8)
    first, last = lane == 0, lane == LANES - 1
    if part != MAIN:
        strip_fluxes(strips, ghost_rows)
        turn_ghosts(ghost_rows, ghost)

    def edge_fluxes(at):
        values = ghost[at, :]
        return [values] + [pltpu.roll(values, LANES - 2 * f, 1) for f in (1, 2)]

    if part == EDGE:

        def fix(r, carry):
            at = aligned(r * 8, 8)
            edges = edge_fluxes(at)
            active = work[active_rows, at, :] > 0.5
            for f in range(3):
                left, right = DIFF * tiles + f * tiles, DIFF * tiles + f * tiles + tiles - 1
                work[left, at, :] -= jnp.where(active & first, edges[f], 0.0)
                work[right, at, :] += jnp.where(active & last, edges[f], 0.0)
            return carry

        lax.fori_loop(0, row_tiles, fix, 0, unroll=10)
        return

    def derive(r, carry):
        for i in range(5):
            at = aligned(r * 40 + i * 8, 8)
            for c in range(tiles):
                roots = with_roots(*[work[k * tiles + c, at, :] for k in range(3)])
                for k in range(3):
                    derived[k * tiles + c, at, :] = roots[3 + k]
        return carry

    lax.fori_loop(0, row_tiles // 5, derive, 0, unroll=2)
    for p in range(3 * tiles):
        faces[p, 0:8, :] = jnp.zeros((8, LANES), jnp.float32)

    def load(c, at):
        return [ref[k * tiles + c, at, :] for ref in (work, derived) for k in range(3)]

    def fluxes(at, wrap):
        here, below = pl.ds(at, 8), pl.ds(at + 1, 8)
        now = [load(c, here) for c in range(tiles)]
        across = []
        for c in range(tiles):
            right = [
                pltpu.roll(jnp.where(first, b, a), LANES - 1, 1)
                for a, b in zip(now[c], now[(c + 1) % tiles])
            ]
            f_depth, f_across, f_along = roe(side(*flip(now[c])), side(*flip(right)))
            across.append([f_depth, f_along, f_across])
            under = [pltpu.roll(v, 7, 0) for v in now[c]] if wrap else load(c, below)
            flux = roe(side(*now[c]), side(*under))
            for f in range(3):
                faces[f * tiles + c, pl.ds(at + 8, 8), :] = flux[f]
        if part == ALL:
            edges = edge_fluxes(here)
        else:
            edges = [jnp.zeros((8, LANES), jnp.float32)] * 3
        for f in range(3):
            across[-1][f] = jnp.where(last, edges[f], across[-1][f])
        active = work[active_rows, here, :] > 0.5
        for c in range(tiles):
            for f in range(3):
                if c:
                    left = pltpu.roll(jnp.where(last, across[c - 1][f], across[c][f]), 1, 1)
                else:
                    left = jnp.where(first, edges[f], pltpu.roll(across[c][f], 1, 1))
                plane = f * tiles + c
                out = (across[c][f] - left) + (
                    faces[plane, pl.ds(at + 8, 8), :] - faces[plane, pl.ds(at + 7, 8), :]
                )
                if f == 0:
                    out = out - 2.0 * work[SOURCE * tiles + c, here, :]
                work[(DIFF + f) * tiles + c, here, :] = jnp.where(active, out, 0.0)

    def one(r, carry):
        fluxes(pl.multiple_of(r * 8, 8), False)
        return carry

    lax.fori_loop(0, row_tiles - 1, one, 0, unroll=FLUX_UNROLL)
    fluxes(padded - 8, True)


def step_ratio(peak_ref):
    peak = jnp.max(jnp.max(peak_ref[...], axis=0), axis=0, keepdims=True)
    step = (COURANT * SPACING) / peak
    return jnp.broadcast_to((0.5 / SPACING) * step, (8, LANES))


def moved(work, c, at, ratio):
    tiles = tiles_of(work)
    return [
        work[f * tiles + c, at, :] - ratio * work[(DIFF + f) * tiles + c, at, :] for f in range(3)
    ]


def move_own(work, at, ratio):
    tiles = tiles_of(work)
    for c in range(tiles):
        for f, new in enumerate(moved(work, c, at, ratio)):
            work[f * tiles + c, at, :] = new


def update_kernel(peak_ref, work_in, strips_in, work, strips, next_hbm, spread, sem):
    tiles = tiles_of(work)
    row_tiles = work.shape[1] // 8
    ratio = step_ratio(peak_ref)

    def find(r, acc):
        at = aligned(r * 8 + TOP, 8)
        active = work[active_at(work), at, :] > 0.5
        for c in range(tiles):
            acc = jnp.maximum(acc, jnp.where(active, speed_of(*moved(work, c, at, ratio)), 0.0))
        return acc

    zero = jnp.zeros((8, LANES), jnp.float32)
    spread_peak(lax.fori_loop(0, row_tiles - 2, find, zero, unroll=16), spread)
    copy = pltpu.make_async_copy(spread, next_hbm, sem)
    copy.start()
    for q in range(strips.shape[3] // LANES):
        span = slice(q * LANES, (q + 1) * LANES)
        for k in range(3):
            for s in range(2):
                strips[s, k, :, span] -= ratio * strips[s, STRIP_DIFF + k, :, span]

    def move(r, carry):
        move_own(work, aligned(r * 8, 8), ratio)
        return carry

    lax.fori_loop(0, row_tiles, move, 0, unroll=10)
    copy.wait()


def last_kernel(peak_ref, plan_ref, work, next_ref, best):
    tiles = tiles_of(work)
    blocks = plan_ref.shape[0]
    block_rows = (work.shape[1] - 2 * 8) // blocks
    ratio = step_ratio(peak_ref)

    def one_block(b, carry):
        acc = jnp.zeros((8, LANES), jnp.float32)
        for r in range(0, block_rows, 8):
            at = aligned(b * block_rows + TOP + r, 8)
            for c in range(tiles):
                acc = jnp.maximum(acc, speed_of(*moved(work, c, at, ratio)))
        best[b] = acc
        return carry

    lax.fori_loop(0, blocks, one_block, 0, unroll=8)
    for t in range(next_ref.shape[0]):
        acc = jnp.zeros((8, LANES), jnp.float32)
        for b in range(blocks):
            acc = jnp.maximum(acc, jnp.where(plan_ref[b] == t, best[b], 0.0))
        top = jnp.max(acc, axis=0, keepdims=True)
        next_ref[t] = jnp.broadcast_to(jnp.max(top, axis=1, keepdims=True), (1, LANES))


def store_kernel(peak_ref, work_in, work, depth_hbm, mom_hbm, sem):
    rows, cols = depth_hbm.shape
    tiles = cols // LANES
    ratio = step_ratio(peak_ref)

    def move(r, carry):
        move_own(work, aligned(r * 8 + TOP, 8), ratio)
        return carry

    lax.fori_loop(0, rows // 8, move, 0, unroll=8)
    copies = []
    for k, dst in enumerate([depth_hbm, mom_hbm.at[0], mom_hbm.at[1]]):
        for c in range(tiles):
            copies.append(
                pltpu.make_async_copy(
                    work.at[k * tiles + c, pl.ds(TOP, rows), :],
                    dst.at[:, pl.ds(c * LANES, LANES)],
                    sem.at[k, c],
                )
            )
    for copy in copies:
        copy.start()
    for copy in copies:
        copy.wait()


def exchange(x, axes):
    return lax.all_to_all(x, axes, 0, 0)


def send(x, axis, forward):
    count = lax.axis_size(axis)
    pairs = [(i, (i + 1) % count) if forward else ((i + 1) % count, i) for i in range(count)]
    return lax.ppermute(x, axis, pairs)


def on_device(water_depth, momentum, wet_mask, helper_plan, breach_cells, breach_rate):
    rows, cols = water_depth.shape
    tile_count = lax.axis_size("tile")
    everyone = tile_count * lax.axis_size("region")
    blocks = wet_mask.shape[0]
    tiles = cols // LANES
    padded = rows + 2 * 8
    f32 = jnp.float32
    cells = breach_cells.reshape(-1)
    rates = breach_rate.reshape(-1)
    nbytes = 4 * 3 * rows * cols
    work_out = vmem_out(FIELDS * tiles + 1, padded, LANES)
    strips_out = vmem_out(2, STRIP_FIELDS, 2 * HALO, rows + LANES)
    strip_out = vmem_out(SEND, HALO, rows + LANES)
    edge_out = vmem_out(SEND * tiles, HALO, LANES)
    peak_out = jax.ShapeDtypeStruct((everyone, 1, LANES), f32)
    first_out = jax.ShapeDtypeStruct((everyone, FIRST, LANES), f32)

    work, plan, up, down = pl.pallas_call(
        start_kernel,
        out_shape=(work_out, pltpu.VMEM((blocks, 1, LANES), jnp.int32), edge_out, edge_out),
        in_specs=[hbm_spec()] * 6,
        out_specs=(vmem_spec(),) * 4,
        scratch_shapes=[
            pltpu.SMEM((blocks,), jnp.int32),
            pltpu.SMEM((blocks,), jnp.int32),
            pltpu.SMEM(cells.shape, jnp.int32),
            pltpu.SMEM(cells.shape, f32),
            pltpu.SemaphoreType.DMA((4,)),
            pltpu.SemaphoreType.DMA((3, tiles)),
        ],
        compiler_params=params(),
        cost_estimate=cost(2 * rows * cols, nbytes),
        name="start",
    )(
        *(
            pltpu.with_memory_space_constraint(x, pltpu.HBM)
            for x in (
                wet_mask.reshape(-1),
                helper_plan.reshape(-1),
                cells,
                rates,
                water_depth,
                momentum,
            )
        )
    )

    above = send(down, "region", True)
    below = send(up, "region", False)

    peak, left, right = pl.pallas_call(
        pack_kernel,
        out_shape=(first_out, strip_out, strip_out),
        in_specs=[vmem_spec()],
        out_specs=(hbm_spec(), vmem_spec(), vmem_spec()),
        scratch_shapes=[
            pltpu.VMEM((rows, LANES), f32),
            pltpu.VMEM(first_out.shape, f32),
            pltpu.SemaphoreType.DMA,
        ],
        compiler_params=params(),
        cost_estimate=cost(20 * rows * cols, nbytes),
        name="pack",
    )(work)

    work, left, right = pl.pallas_call(
        rows_kernel,
        out_shape=(work_out, strip_out, strip_out),
        in_specs=[vmem_spec()] * 5,
        out_specs=(vmem_spec(),) * 3,
        scratch_shapes=[pltpu.VMEM((LANES, LANES), f32)],
        input_output_aliases={0: 0, 1: 1, 2: 2},
        compiler_params=params(),
        cost_estimate=cost(rows * cols, nbytes // 8),
        name="rows",
    )(work, left, right, above, below)

    from_left = send(right, "tile", True)
    from_right = send(left, "tile", False)
    peaks = exchange(peak, ("region", "tile"))

    def flux(part, work, *strips):
        outs = (work_out, strips_out)[: 1 + len(strips)]
        main = [
            pltpu.VMEM((3 * tiles, padded, LANES), f32),
            pltpu.VMEM((3 * tiles, padded + 8, LANES), f32),
        ]
        edge = [pltpu.VMEM((LANES, rows + LANES), f32), pltpu.VMEM((padded, LANES), f32)]
        flops, moved_bytes = FLUX_COST[part]
        return pl.pallas_call(
            functools.partial(flux_kernel, part),
            out_shape=outs,
            in_specs=[vmem_spec()] * len(outs),
            out_specs=(vmem_spec(),) * len(outs),
            scratch_shapes=(main + edge, main, edge)[part],
            input_output_aliases={i: i for i in range(len(outs))},
            compiler_params=params(),
            cost_estimate=cost(int(flops * rows * cols), int(moved_bytes * nbytes)),
            name=("flux", "main", "edge")[part],
        )(work, *strips)

    (work,) = flux(MAIN, work)
    strips = pl.pallas_call(
        columns_kernel,
        out_shape=strips_out,
        in_specs=[vmem_spec()] * 4,
        out_specs=vmem_spec(),
        compiler_params=params(),
        cost_estimate=cost(rows * cols, nbytes // 8),
        name="columns",
    )(left, right, from_left, from_right)

    for step in range(STEPS):
        work, strips = flux(ALL if step else EDGE, work, strips)
        if step < STEPS - 1:
            work, strips, peak = pl.pallas_call(
                update_kernel,
                out_shape=(
                    work_out,
                    strips_out,
                    peak_out,
                ),
                in_specs=[vmem_spec()] * 3,
                out_specs=(vmem_spec(), vmem_spec(), hbm_spec()),
                scratch_shapes=[
                    pltpu.VMEM((everyone, 1, LANES), f32),
                    pltpu.SemaphoreType.DMA,
                ],
                input_output_aliases={1: 0, 2: 1},
                compiler_params=params(),
                cost_estimate=cost(20 * rows * cols, nbytes),
                name="update",
            )(peaks, work, strips)
            peaks = exchange(peak, ("region", "tile"))

    best = pl.pallas_call(
        last_kernel,
        out_shape=vmem_out(tile_count, 1, LANES),
        in_specs=[vmem_spec()] * 3,
        out_specs=vmem_spec(),
        scratch_shapes=[pltpu.VMEM((blocks, 8, LANES), f32)],
        compiler_params=params(),
        cost_estimate=cost(20 * rows * cols, 2 * nbytes),
        name="last",
    )(peaks, plan, work)
    helpers = exchange(best, "tile")
    work, new_depth, new_momentum = pl.pallas_call(
        store_kernel,
        out_shape=(
            work_out,
            jax.ShapeDtypeStruct((rows, cols), f32),
            jax.ShapeDtypeStruct((2, rows, cols), f32),
        ),
        in_specs=[vmem_spec()] * 2,
        out_specs=(vmem_spec(), hbm_spec(), hbm_spec()),
        scratch_shapes=[pltpu.SemaphoreType.DMA((3, tiles))],
        input_output_aliases={1: 0},
        compiler_params=params(),
        cost_estimate=cost(10 * rows * cols, 2 * nbytes),
        name="store",
    )(peaks, work)
    return new_depth, new_momentum, jnp.max(helpers[:, :, :1], axis=0)


def solution(mesh):
    return jax.shard_map(
        on_device,
        mesh=mesh,
        in_specs=(
            P("region", "tile"),
            P(None, "region", "tile"),
            P("region", "tile"),
            P("region", "tile"),
            P("region", "tile", None),
            P("region", "tile", None),
        ),
        out_specs=(P("region", "tile"), P(None, "region", "tile"), P("region", "tile")),
        check_vma=False,
    )
```

```python
import functools

import jax
import jax.numpy as jnp
from jax import lax
from jax.experimental import pallas as pl
from jax.experimental.pallas import tpu as pltpu
from jax.sharding import PartitionSpec as P

STEPS = 4
HALO = 4
LANES = 128
TOP = 8

GRAVITY = 9.81
COURANT = 0.45
SPACING = 1.0

VMEM_LIMIT = 20 << 20
FLUX_UNROLL = 7
FIRST = 2
FLUX_COST = ((150, 4), (150, 4), (500, 20))


SOURCE, DIFF, FIELDS = 3, 4, 7
SEND = 5
STRIP_DIFF, STRIP_FIELDS = 5, 8
ALL, MAIN, EDGE = range(3)


def tiles_of(work):
    return (work.shape[0] - 1) // FIELDS


def active_at(work):
    return work.shape[0] - 1


def sent_plane(work, k, c):
    tiles = tiles_of(work)
    return (k * tiles + c, active_at(work), SOURCE * tiles + c)[max(k - 2, 0)]


def vmem_spec():
    return pl.BlockSpec(memory_space=pltpu.VMEM)


def hbm_spec():
    return pl.BlockSpec(memory_space=pltpu.HBM)


def vmem_out(*shape):
    return pltpu.VMEM(shape, jnp.float32)


def params():
    return pltpu.CompilerParams(vmem_limit_bytes=VMEM_LIMIT)


def cost(flops, nbytes):
    return pl.CostEstimate(flops=flops, bytes_accessed=nbytes, transcendentals=0)


def lane_ids(rows):
    return lax.broadcasted_iota(jnp.int32, (rows, LANES), 1)


def aligned(start, size):
    return pl.ds(pl.multiple_of(start, 8), size)


def speed_of(depth, along, across):
    root = lax.rsqrt(depth)
    inverse = root * root
    return jnp.maximum(jnp.abs(along), jnp.abs(across)) * inverse + jnp.sqrt(
        jnp.float32(GRAVITY)
    ) * (depth * root)


def spread_peak(acc, out_ref):
    top = jnp.max(jnp.max(acc, axis=0, keepdims=True), axis=1, keepdims=True)
    out_ref[...] = jnp.broadcast_to(top[None], out_ref.shape)


def start_kernel(
    wet_hbm,
    plan_hbm,
    cell_hbm,
    rate_hbm,
    depth_hbm,
    mom_hbm,
    work,
    plan_ref,
    up_ref,
    down_ref,
    wet_ref,
    plan_smem,
    cell_ref,
    rate_ref,
    small_sem,
    big_sem,
):
    rows, cols = depth_hbm.shape
    tiles = cols // LANES
    padded = work.shape[1]
    blocks = wet_hbm.shape[0]
    block_rows = rows // blocks
    bottom = TOP + rows
    small = [
        pltpu.make_async_copy(src, dst, small_sem.at[i])
        for i, (src, dst) in enumerate(
            [
                (cell_hbm, cell_ref),
                (rate_hbm, rate_ref),
                (wet_hbm, wet_ref),
                (plan_hbm, plan_smem),
            ]
        )
    ]
    big = []
    for k, src in enumerate([depth_hbm, mom_hbm.at[0], mom_hbm.at[1]]):
        for c in range(tiles):
            big.append(
                pltpu.make_async_copy(
                    src.at[:, pl.ds(c * LANES, LANES)],
                    work.at[k * tiles + c, pl.ds(TOP, rows), :],
                    big_sem.at[k, c],
                )
            )
    for copy in small + big:
        copy.start()
    for k in range(SEND):
        for c in range(tiles):
            plane = sent_plane(work, k, c)
            fill = 1.0 if k == 0 else 0.0
            work[plane, 0:TOP, :] = jnp.full((TOP, LANES), fill, jnp.float32)
            work[plane, bottom:padded, :] = jnp.full((padded - bottom, LANES), fill, jnp.float32)
    for c in range(tiles):
        work[SOURCE * tiles + c, TOP:bottom, :] = jnp.zeros((rows, LANES), jnp.float32)
    for copy in small:
        copy.wait()
    lane = lane_ids(1)

    for i in range(cell_ref.shape[0]):
        cell = cell_ref[i]
        row = lax.div(cell, cols)
        col = cell - row * cols
        c = lax.div(col, LANES)
        at = pl.ds(row + TOP, 1)
        work[SOURCE * tiles + c, at, :] += jnp.where(lane == col - c * LANES, rate_ref[i], 0.0)
    for b in range(blocks):
        wet = wet_ref[b].astype(jnp.float32)
        at = slice(TOP + b * block_rows, TOP + (b + 1) * block_rows)
        work[active_at(work), at, :] = jnp.full((block_rows, LANES), wet)
        plan_ref[b] = jnp.full((1, LANES), plan_smem[b])
    for copy in big:
        copy.wait()
    for k in range(SEND):
        for c in range(tiles):
            plane = sent_plane(work, k, c)
            up_ref[k * tiles + c] = work[plane, TOP : TOP + HALO, :]
            down_ref[k * tiles + c] = work[plane, bottom - HALO : bottom, :]


def packed(work, at, lane):
    tiles = tiles_of(work)
    out = None
    for k in range(SEND):
        first, last = sent_plane(work, k, 0), sent_plane(work, k, tiles - 1)
        ends = jnp.where(lane < HALO, work[first, at, :], work[last, at, :])
        ends = pltpu.roll(ends, 2 * HALO * k + HALO, 1)
        out = ends if out is None else jnp.where(lane >= 2 * HALO * k, ends, out)
    return out


def split_packed(turned, left_ref, right_ref, at):
    for k in range(SEND):
        lo = 2 * HALO * k
        right_ref[k, :, at] = turned[lo : lo + HALO, :]
        left_ref[k, :, at] = turned[lo + HALO : lo + 2 * HALO, :]


def pack_kernel(work, peak_hbm, left_ref, right_ref, pack, spread, sem):
    tiles = tiles_of(work)
    rows = pack.shape[0]
    lane = lane_ids(8)

    def find(r, acc):
        at = aligned(r * 8 + TOP, 8)
        active = work[active_at(work), at, :] > 0.5
        for c in range(tiles):
            speed = speed_of(*[work[k * tiles + c, at, :] for k in range(3)])
            acc = jnp.maximum(acc, jnp.where(active, speed, 0.0))
        return acc

    zero = jnp.zeros((8, LANES), jnp.float32)
    spread_peak(lax.fori_loop(0, rows // 8, find, zero, unroll=16), spread)
    copy = pltpu.make_async_copy(spread, peak_hbm, sem)
    copy.start()

    def one(r, carry):
        pack[aligned(r * 8, 8), :] = packed(work, aligned(r * 8 + TOP, 8), lane)
        return carry

    lax.fori_loop(0, rows // 8, one, 0, unroll=8)
    for q in range(rows // LANES):
        at = slice(q * LANES, (q + 1) * LANES)
        split_packed(pack[at, :].T, left_ref, right_ref, at)
    copy.wait()


def rows_kernel(
    work_in, left_in, right_in, above_ref, below_ref, work, left_ref, right_ref, pack
):
    tiles = tiles_of(work)
    own = left_ref.shape[2] - LANES
    bottom = TOP + own
    is_top = lax.axis_index("region") == 0
    is_bottom = lax.axis_index("region") == lax.axis_size("region") - 1

    def mirrored(first, step, to):
        for k in range(SEND):
            flip = -1.0 if k == 1 else 1.0
            for c in range(tiles):
                plane = sent_plane(work, k, c)
                for j in range(HALO):
                    work[plane, to - step * (1 + j), :] = work[plane, first + step * j, :] * flip

    def received(ref, lo):
        for k in range(SEND):
            for c in range(tiles):
                work[sent_plane(work, k, c), lo : lo + HALO, :] = ref[k * tiles + c]

    pl.when(is_top)(lambda: mirrored(TOP, 1, TOP))
    pl.when(jnp.logical_not(is_top))(lambda: received(above_ref, TOP - HALO))
    pl.when(is_bottom)(lambda: mirrored(bottom - 1, -1, bottom - 1))
    pl.when(jnp.logical_not(is_bottom))(lambda: received(below_ref, bottom))
    pack[...] = jnp.zeros_like(pack)
    lane = lane_ids(8)
    pack[0:8, :] = packed(work, slice(bottom, bottom + 8), lane)
    pack[LANES - 8 :, :] = packed(work, slice(0, 8), lane)
    split_packed(pack[...].T, left_ref, right_ref, slice(own, own + LANES))


def columns_kernel(own_left, own_right, from_left, from_right, strips):
    is_left = lax.axis_index("tile") == 0
    is_right = lax.axis_index("tile") == lax.axis_size("tile") - 1

    def mirrored(ref, side, to):
        for k in range(SEND):
            flip = -1.0 if k == 2 else 1.0
            for j in range(HALO):
                strips[side, k, to + HALO - 1 - j, :] = ref[k, j, :] * flip

    def received(ref, side, to):
        for k in range(SEND):
            strips[side, k, to : to + HALO, :] = ref[k]

    received(own_left, 0, HALO)
    received(own_right, 1, 0)
    pl.when(is_left)(lambda: mirrored(own_left, 0, 0))
    pl.when(jnp.logical_not(is_left))(lambda: received(from_left, 0, 0))
    pl.when(is_right)(lambda: mirrored(own_right, 1, HALO))
    pl.when(jnp.logical_not(is_right))(lambda: received(from_right, 1, HALO))


def roe(left, right):
    depth_l, normal_l, tangent_l, root_l, sn_l, st_l, press_l, shear_l = left
    depth_r, normal_r, tangent_r, root_r, sn_r, st_r, press_r, shear_r = right
    weight = pl.reciprocal(root_l + root_r, approx=False)
    speed = (sn_l + sn_r) * weight
    drift = (st_l + st_r) * weight
    half = (0.5 * GRAVITY) * (depth_l + depth_r)
    inverse = lax.rsqrt(half)
    celerity = half * inverse
    jump = depth_r - depth_l
    excess = (normal_r - normal_l) - speed * jump
    bend = excess * (0.5 * inverse)
    half_jump = 0.5 * jump
    slow = speed - celerity
    fast = speed + celerity
    wave_one = jnp.abs(slow) * (half_jump - bend)
    wave_three = jnp.abs(fast) * (half_jump + bend)
    wave_two = jnp.abs(speed) * ((tangent_r - tangent_l) - drift * jump)
    both = wave_one + wave_three
    flux_depth = (normal_l + normal_r) - both
    flux_normal = (press_l + press_r) - speed * both - celerity * (wave_three - wave_one)
    flux_tangent = (shear_l + shear_r) - drift * both - wave_two
    return flux_depth, flux_normal, flux_tangent


def side(depth, normal, tangent, root, sn, st):
    press = sn * sn + (0.5 * GRAVITY) * (depth * depth)
    return (depth, normal, tangent, root, sn, st, press, sn * st)


def flip(v):
    return (v[0], v[2], v[1], v[3], v[5], v[4])


def with_roots(depth, along, across):
    inverse = lax.rsqrt(depth)
    return [depth, along, across, depth * inverse, along * inverse, across * inverse]


def strip_fluxes(strips, ghost_rows):
    chunks = strips.shape[3] // LANES
    lane = lane_ids(8)
    for s in range(2):
        spans = [slice(q * LANES, (q + 1) * LANES) for q in range(chunks)]
        now = [with_roots(*[strips[s, k, :, at] for k in range(3)]) for at in spans]
        rows = []
        for q in range(chunks):
            below = [
                pltpu.roll(jnp.where(lane == 0, b, a), LANES - 1, 1)
                for a, b in zip(now[q], now[(q + 1) % chunks])
            ]
            rows.append(roe(side(*now[q]), side(*below)))
        for q, at in enumerate(spans):
            right = [pltpu.roll(v, 7, 0) for v in now[q]]
            f_depth, f_across, f_along = roe(side(*flip(now[q])), side(*flip(right)))
            active = strips[s, 3, :, at] > 0.5
            for f, flux in enumerate((f_depth, f_along, f_across)):
                above = jnp.where(lane == LANES - 1, rows[q - 1][f], rows[q][f])
                out = (flux - pltpu.roll(flux, 1, 0)) + (rows[q][f] - pltpu.roll(above, 1, 1))
                if f == 0:
                    out = out - 2.0 * strips[s, 4, :, at]
                strips[s, STRIP_DIFF + f, :, at] = jnp.where(active, out, 0.0)
                ghost_rows[(2 * f - s) % LANES, at] = flux[HALO - 1, :]


def turn_ghosts(ghost_rows, ghost):
    own = ghost_rows.shape[1] - LANES
    for q in range(own // LANES):
        at = slice(q * LANES, (q + 1) * LANES)
        ghost[TOP + q * LANES : TOP + (q + 1) * LANES, :] = ghost_rows[:, at].T
    ends = ghost_rows[:, own : own + LANES].T
    ghost[TOP + own : TOP + own + 8, :] = ends[0:8, :]
    ghost[0:8, :] = ends[LANES - 8 :, :]


def flux_kernel(part, *refs):
    if part == MAIN:
        work_in, work, derived, faces = refs
    elif part == EDGE:
        work_in, strips_in, work, strips, ghost_rows, ghost = refs
    else:
        work_in, strips_in, work, strips, derived, faces, ghost_rows, ghost = refs
    tiles = tiles_of(work)
    padded = work.shape[1]
    row_tiles = padded // 8
    active_rows = active_at(work)
    lane = lane_ids(8)
    first, last = lane == 0, lane == LANES - 1
    if part != MAIN:
        strip_fluxes(strips, ghost_rows)
        turn_ghosts(ghost_rows, ghost)

    def edge_fluxes(at):
        values = ghost[at, :]
        return [values] + [pltpu.roll(values, LANES - 2 * f, 1) for f in (1, 2)]

    if part == EDGE:

        def fix(r, carry):
            at = aligned(r * 8, 8)
            edges = edge_fluxes(at)
            active = work[active_rows, at, :] > 0.5
            for f in range(3):
                left, right = DIFF * tiles + f * tiles, DIFF * tiles + f * tiles + tiles - 1
                work[left, at, :] -= jnp.where(active & first, edges[f], 0.0)
                work[right, at, :] += jnp.where(active & last, edges[f], 0.0)
            return carry

        lax.fori_loop(0, row_tiles, fix, 0, unroll=10)
        return

    def derive(r, carry):
        for i in range(5):
            at = aligned(r * 40 + i * 8, 8)
            for c in range(tiles):
                roots = with_roots(*[work[k * tiles + c, at, :] for k in range(3)])
                for k in range(3):
                    derived[k * tiles + c, at, :] = roots[3 + k]
        return carry

    lax.fori_loop(0, row_tiles // 5, derive, 0, unroll=2)
    for p in range(3 * tiles):
        faces[p, 0:8, :] = jnp.zeros((8, LANES), jnp.float32)

    def load(c, at):
        return [ref[k * tiles + c, at, :] for ref in (work, derived) for k in range(3)]

    def fluxes(at, wrap):
        here, below = pl.ds(at, 8), pl.ds(at + 1, 8)
        now = [load(c, here) for c in range(tiles)]
        across = []
        for c in range(tiles):
            right = [
                pltpu.roll(jnp.where(first, b, a), LANES - 1, 1)
                for a, b in zip(now[c], now[(c + 1) % tiles])
            ]
            f_depth, f_across, f_along = roe(side(*flip(now[c])), side(*flip(right)))
            across.append([f_depth, f_along, f_across])
            under = [pltpu.roll(v, 7, 0) for v in now[c]] if wrap else load(c, below)
            flux = roe(side(*now[c]), side(*under))
            for f in range(3):
                faces[f * tiles + c, pl.ds(at + 8, 8), :] = flux[f]
        if part == ALL:
            edges = edge_fluxes(here)
        else:
            edges = [jnp.zeros((8, LANES), jnp.float32)] * 3
        for f in range(3):
            across[-1][f] = jnp.where(last, edges[f], across[-1][f])
        active = work[active_rows, here, :] > 0.5
        for c in range(tiles):
            for f in range(3):
                if c:
                    left = pltpu.roll(jnp.where(last, across[c - 1][f], across[c][f]), 1, 1)
                else:
                    left = jnp.where(first, edges[f], pltpu.roll(across[c][f], 1, 1))
                plane = f * tiles + c
                out = (across[c][f] - left) + (
                    faces[plane, pl.ds(at + 8, 8), :] - faces[plane, pl.ds(at + 7, 8), :]
                )
                if f == 0:
                    out = out - 2.0 * work[SOURCE * tiles + c, here, :]
                work[(DIFF + f) * tiles + c, here, :] = jnp.where(active, out, 0.0)

    def one(r, carry):
        fluxes(pl.multiple_of(r * 8, 8), False)
        return carry

    lax.fori_loop(0, row_tiles - 1, one, 0, unroll=FLUX_UNROLL)
    fluxes(padded - 8, True)


def step_ratio(peak_ref):
    peak = jnp.max(jnp.max(peak_ref[...], axis=0), axis=0, keepdims=True)
    step = (COURANT * SPACING) / peak
    return jnp.broadcast_to((0.5 / SPACING) * step, (8, LANES))


def moved(work, c, at, ratio):
    tiles = tiles_of(work)
    return [
        work[f * tiles + c, at, :] - ratio * work[(DIFF + f) * tiles + c, at, :] for f in range(3)
    ]


def move_own(work, at, ratio):
    tiles = tiles_of(work)
    for c in range(tiles):
        for f, new in enumerate(moved(work, c, at, ratio)):
            work[f * tiles + c, at, :] = new


def update_kernel(peak_ref, work_in, strips_in, work, strips, next_hbm, spread, sem):
    tiles = tiles_of(work)
    row_tiles = work.shape[1] // 8
    ratio = step_ratio(peak_ref)

    def find(r, acc):
        at = aligned(r * 8 + TOP, 8)
        active = work[active_at(work), at, :] > 0.5
        for c in range(tiles):
            acc = jnp.maximum(acc, jnp.where(active, speed_of(*moved(work, c, at, ratio)), 0.0))
        return acc

    zero = jnp.zeros((8, LANES), jnp.float32)
    spread_peak(lax.fori_loop(0, row_tiles - 2, find, zero, unroll=16), spread)
    copy = pltpu.make_async_copy(spread, next_hbm, sem)
    copy.start()
    for q in range(strips.shape[3] // LANES):
        span = slice(q * LANES, (q + 1) * LANES)
        for k in range(3):
            for s in range(2):
                strips[s, k, :, span] -= ratio * strips[s, STRIP_DIFF + k, :, span]

    def move(r, carry):
        move_own(work, aligned(r * 8, 8), ratio)
        return carry

    lax.fori_loop(0, row_tiles, move, 0, unroll=10)
    copy.wait()


def last_kernel(peak_ref, plan_ref, work, mine_ref, theirs_ref, best):
    tiles = tiles_of(work)
    blocks = plan_ref.shape[0]
    block_rows = (work.shape[1] - 2 * 8) // blocks
    ratio = step_ratio(peak_ref)

    def one_block(b, carry):
        acc = jnp.zeros((8, LANES), jnp.float32)
        for r in range(0, block_rows, 8):
            at = aligned(b * block_rows + TOP + r, 8)
            for c in range(tiles):
                acc = jnp.maximum(acc, speed_of(*moved(work, c, at, ratio)))
        best[b] = acc
        return carry

    lax.fori_loop(0, blocks, one_block, 0, unroll=8)
    is_odd = lax.rem(lax.axis_index("tile"), 2) == 1
    for j in range(mine_ref.shape[0]):
        pair = []
        for t in (2 * j, 2 * j + 1):
            acc = jnp.zeros((8, LANES), jnp.float32)
            for b in range(blocks):
                acc = jnp.maximum(acc, jnp.where(plan_ref[b] == t, best[b], 0.0))
            top = jnp.max(acc, axis=0, keepdims=True)
            pair.append(jnp.broadcast_to(jnp.max(top, axis=1, keepdims=True), (1, LANES)))
        mine_ref[j] = jnp.where(is_odd, pair[1], pair[0])
        theirs_ref[j] = jnp.where(is_odd, pair[0], pair[1])


def chip_kernel(mine_ref, other_ref, *out_refs):
    here = lax.div(lax.axis_index("tile"), 2)
    for x, out_ref in enumerate(out_refs):
        there = jnp.bitwise_xor(here, x)
        out_ref[...] = jnp.maximum(mine_ref[there], other_ref[there])


def helper_kernel(*refs):
    value = refs[0][...]
    for ref in refs[1:-1]:
        value = jnp.maximum(value, ref[...])
    refs[-1][...] = value[:, :1]


def store_kernel(peak_ref, work_in, work, depth_hbm, mom_hbm, sem):
    rows, cols = depth_hbm.shape
    tiles = cols // LANES
    ratio = step_ratio(peak_ref)

    def move(r, carry):
        move_own(work, aligned(r * 8 + TOP, 8), ratio)
        return carry

    lax.fori_loop(0, rows // 8, move, 0, unroll=8)
    copies = []
    for k, dst in enumerate([depth_hbm, mom_hbm.at[0], mom_hbm.at[1]]):
        for c in range(tiles):
            copies.append(
                pltpu.make_async_copy(
                    work.at[k * tiles + c, pl.ds(TOP, rows), :],
                    dst.at[:, pl.ds(c * LANES, LANES)],
                    sem.at[k, c],
                )
            )
    for copy in copies:
        copy.start()
    for copy in copies:
        copy.wait()


def exchange(x, axes):
    return lax.all_to_all(x, axes, 0, 0)


def swap(x, axis, apart):
    return lax.ppermute(x, axis, [(i, i ^ apart) for i in range(lax.axis_size(axis))])


def send(x, axis, forward):
    count = lax.axis_size(axis)
    pairs = [(i, (i + 1) % count) if forward else ((i + 1) % count, i) for i in range(count)]
    return lax.ppermute(x, axis, pairs)


def on_device(water_depth, momentum, wet_mask, helper_plan, breach_cells, breach_rate):
    rows, cols = water_depth.shape
    tile_count = lax.axis_size("tile")
    everyone = tile_count * lax.axis_size("region")
    blocks = wet_mask.shape[0]
    tiles = cols // LANES
    padded = rows + 2 * 8
    f32 = jnp.float32
    cells = breach_cells.reshape(-1)
    rates = breach_rate.reshape(-1)
    nbytes = 4 * 3 * rows * cols
    work_out = vmem_out(FIELDS * tiles + 1, padded, LANES)
    strips_out = vmem_out(2, STRIP_FIELDS, 2 * HALO, rows + LANES)
    strip_out = vmem_out(SEND, HALO, rows + LANES)
    edge_out = vmem_out(SEND * tiles, HALO, LANES)
    peak_out = jax.ShapeDtypeStruct((everyone, 1, LANES), f32)
    first_out = jax.ShapeDtypeStruct((everyone, FIRST, LANES), f32)

    work, plan, up, down = pl.pallas_call(
        start_kernel,
        out_shape=(work_out, pltpu.VMEM((blocks, 1, LANES), jnp.int32), edge_out, edge_out),
        in_specs=[hbm_spec()] * 6,
        out_specs=(vmem_spec(),) * 4,
        scratch_shapes=[
            pltpu.SMEM((blocks,), jnp.int32),
            pltpu.SMEM((blocks,), jnp.int32),
            pltpu.SMEM(cells.shape, jnp.int32),
            pltpu.SMEM(cells.shape, f32),
            pltpu.SemaphoreType.DMA((4,)),
            pltpu.SemaphoreType.DMA((3, tiles)),
        ],
        compiler_params=params(),
        cost_estimate=cost(2 * rows * cols, nbytes),
        name="start",
    )(
        *(
            pltpu.with_memory_space_constraint(x, pltpu.HBM)
            for x in (
                wet_mask.reshape(-1),
                helper_plan.reshape(-1),
                cells,
                rates,
                water_depth,
                momentum,
            )
        )
    )

    above = send(down, "region", True)
    below = send(up, "region", False)

    peak, left, right = pl.pallas_call(
        pack_kernel,
        out_shape=(first_out, strip_out, strip_out),
        in_specs=[vmem_spec()],
        out_specs=(hbm_spec(), vmem_spec(), vmem_spec()),
        scratch_shapes=[
            pltpu.VMEM((rows, LANES), f32),
            pltpu.VMEM(first_out.shape, f32),
            pltpu.SemaphoreType.DMA,
        ],
        compiler_params=params(),
        cost_estimate=cost(20 * rows * cols, nbytes),
        name="pack",
    )(work)

    work, left, right = pl.pallas_call(
        rows_kernel,
        out_shape=(work_out, strip_out, strip_out),
        in_specs=[vmem_spec()] * 5,
        out_specs=(vmem_spec(),) * 3,
        scratch_shapes=[pltpu.VMEM((LANES, LANES), f32)],
        input_output_aliases={0: 0, 1: 1, 2: 2},
        compiler_params=params(),
        cost_estimate=cost(rows * cols, nbytes // 8),
        name="rows",
    )(work, left, right, above, below)

    from_left = send(right, "tile", True)
    from_right = send(left, "tile", False)
    peaks = exchange(peak, ("region", "tile"))

    def flux(part, work, *strips):
        outs = (work_out, strips_out)[: 1 + len(strips)]
        main = [
            pltpu.VMEM((3 * tiles, padded, LANES), f32),
            pltpu.VMEM((3 * tiles, padded + 8, LANES), f32),
        ]
        edge = [pltpu.VMEM((LANES, rows + LANES), f32), pltpu.VMEM((padded, LANES), f32)]
        flops, moved_bytes = FLUX_COST[part]
        return pl.pallas_call(
            functools.partial(flux_kernel, part),
            out_shape=outs,
            in_specs=[vmem_spec()] * len(outs),
            out_specs=(vmem_spec(),) * len(outs),
            scratch_shapes=(main + edge, main, edge)[part],
            input_output_aliases={i: i for i in range(len(outs))},
            compiler_params=params(),
            cost_estimate=cost(int(flops * rows * cols), int(moved_bytes * nbytes)),
            name=("flux", "main", "edge")[part],
        )(work, *strips)

    (work,) = flux(MAIN, work)
    strips = pl.pallas_call(
        columns_kernel,
        out_shape=strips_out,
        in_specs=[vmem_spec()] * 4,
        out_specs=vmem_spec(),
        compiler_params=params(),
        cost_estimate=cost(rows * cols, nbytes // 8),
        name="columns",
    )(left, right, from_left, from_right)

    for step in range(STEPS):
        work, strips = flux(ALL if step else EDGE, work, strips)
        if step < STEPS - 1:
            work, strips, peak = pl.pallas_call(
                update_kernel,
                out_shape=(
                    work_out,
                    strips_out,
                    peak_out,
                ),
                in_specs=[vmem_spec()] * 3,
                out_specs=(vmem_spec(), vmem_spec(), hbm_spec()),
                scratch_shapes=[
                    pltpu.VMEM((everyone, 1, LANES), f32),
                    pltpu.SemaphoreType.DMA,
                ],
                input_output_aliases={1: 0, 2: 1},
                compiler_params=params(),
                cost_estimate=cost(20 * rows * cols, nbytes),
                name="update",
            )(peaks, work, strips)
            peaks = exchange(peak, ("region", "tile"))

    chips = tile_count // 2
    mine, theirs = pl.pallas_call(
        last_kernel,
        out_shape=(vmem_out(chips, 1, LANES),) * 2,
        in_specs=[vmem_spec()] * 3,
        out_specs=(vmem_spec(),) * 2,
        scratch_shapes=[pltpu.VMEM((blocks, 8, LANES), f32)],
        compiler_params=params(),
        cost_estimate=cost(20 * rows * cols, 2 * nbytes),
        name="last",
    )(peaks, plan, work)
    other = swap(theirs, "tile", 1)
    known = pl.pallas_call(
        chip_kernel,
        out_shape=(vmem_out(1, LANES),) * chips,
        in_specs=[vmem_spec()] * 2,
        out_specs=(vmem_spec(),) * chips,
        compiler_params=params(),
        cost_estimate=cost(tile_count, 4 * LANES * tile_count),
        name="chip",
    )(mine, other)
    known = [known[0]] + [swap(known[x], "tile", 2 * x) for x in range(1, chips)]
    work, new_depth, new_momentum = pl.pallas_call(
        store_kernel,
        out_shape=(
            work_out,
            jax.ShapeDtypeStruct((rows, cols), f32),
            jax.ShapeDtypeStruct((2, rows, cols), f32),
        ),
        in_specs=[vmem_spec()] * 2,
        out_specs=(vmem_spec(), hbm_spec(), hbm_spec()),
        scratch_shapes=[pltpu.SemaphoreType.DMA((3, tiles))],
        input_output_aliases={1: 0},
        compiler_params=params(),
        cost_estimate=cost(10 * rows * cols, 2 * nbytes),
        name="store",
    )(peaks, work)
    helper = pl.pallas_call(
        helper_kernel,
        out_shape=jax.ShapeDtypeStruct((1, 1), f32),
        in_specs=[vmem_spec()] * chips,
        out_specs=vmem_spec(),
        compiler_params=params(),
        cost_estimate=cost(tile_count, 4 * LANES * tile_count),
        name="helper",
    )(*known)
    return new_depth, new_momentum, helper


def solution(mesh):
    return jax.shard_map(
        on_device,
        mesh=mesh,
        in_specs=(
            P("region", "tile"),
            P(None, "region", "tile"),
            P("region", "tile"),
            P("region", "tile"),
            P("region", "tile", None),
            P("region", "tile", None),
        ),
        out_specs=(P("region", "tile"), P(None, "region", "tile"), P("region", "tile")),
        check_vma=False,
    )
```

```python
import functools

import jax
import jax.numpy as jnp
from jax import lax
from jax.experimental import pallas as pl
from jax.experimental.pallas import tpu as pltpu
from jax.sharding import PartitionSpec as P

STEPS = 4
HALO = 4
LANES = 128
TOP = 8

GRAVITY = 9.81
COURANT = 0.45
SPACING = 1.0

VMEM_LIMIT = 20 << 20
FLUX_UNROLL = 7
FIRST = 2
FLUX_COST = ((150, 4), (150, 4), (500, 20))


SOURCE, DIFF, FIELDS = 3, 4, 7
SEND = 5
STRIP_DIFF, STRIP_FIELDS = 5, 8
ALL, MAIN, EDGE = range(3)


def tiles_of(work):
    return (work.shape[0] - 1) // FIELDS


def active_at(work):
    return work.shape[0] - 1


def sent_plane(work, k, c):
    tiles = tiles_of(work)
    return (k * tiles + c, active_at(work), SOURCE * tiles + c)[max(k - 2, 0)]


def vmem_spec():
    return pl.BlockSpec(memory_space=pltpu.VMEM)


def hbm_spec():
    return pl.BlockSpec(memory_space=pltpu.HBM)


def vmem_out(*shape):
    return pltpu.VMEM(shape, jnp.float32)


def params():
    return pltpu.CompilerParams(vmem_limit_bytes=VMEM_LIMIT)


def cost(flops, nbytes):
    return pl.CostEstimate(flops=flops, bytes_accessed=nbytes, transcendentals=0)


def lane_ids(rows):
    return lax.broadcasted_iota(jnp.int32, (rows, LANES), 1)


def aligned(start, size):
    return pl.ds(pl.multiple_of(start, 8), size)


def speed_of(depth, along, across):
    root = lax.rsqrt(depth)
    inverse = root * root
    return jnp.maximum(jnp.abs(along), jnp.abs(across)) * inverse + jnp.sqrt(
        jnp.float32(GRAVITY)
    ) * (depth * root)


def spread_peak(acc, out_ref):
    top = jnp.max(jnp.max(acc, axis=0, keepdims=True), axis=1, keepdims=True)
    out_ref[...] = jnp.broadcast_to(top[None], out_ref.shape)


def start_kernel(
    wet_hbm,
    plan_hbm,
    cell_hbm,
    rate_hbm,
    depth_hbm,
    mom_hbm,
    work,
    plan_ref,
    up_ref,
    down_ref,
    wet_ref,
    plan_smem,
    cell_ref,
    rate_ref,
    small_sem,
    big_sem,
):
    rows, cols = depth_hbm.shape
    tiles = cols // LANES
    padded = work.shape[1]
    blocks = wet_hbm.shape[0]
    block_rows = rows // blocks
    bottom = TOP + rows
    small = [
        pltpu.make_async_copy(src, dst, small_sem.at[i])
        for i, (src, dst) in enumerate(
            [
                (cell_hbm, cell_ref),
                (rate_hbm, rate_ref),
                (wet_hbm, wet_ref),
                (plan_hbm, plan_smem),
            ]
        )
    ]
    big = []
    for k, src in enumerate([depth_hbm, mom_hbm.at[0], mom_hbm.at[1]]):
        for c in range(tiles):
            big.append(
                pltpu.make_async_copy(
                    src.at[:, pl.ds(c * LANES, LANES)],
                    work.at[k * tiles + c, pl.ds(TOP, rows), :],
                    big_sem.at[k, c],
                )
            )
    for copy in small + big:
        copy.start()
    for k in range(SEND):
        for c in range(tiles):
            plane = sent_plane(work, k, c)
            fill = 1.0 if k == 0 else 0.0
            work[plane, 0:TOP, :] = jnp.full((TOP, LANES), fill, jnp.float32)
            work[plane, bottom:padded, :] = jnp.full((padded - bottom, LANES), fill, jnp.float32)
    for c in range(tiles):
        work[SOURCE * tiles + c, TOP:bottom, :] = jnp.zeros((rows, LANES), jnp.float32)
    for copy in small:
        copy.wait()
    lane = lane_ids(1)

    for i in range(cell_ref.shape[0]):
        cell = cell_ref[i]
        row = lax.div(cell, cols)
        col = cell - row * cols
        c = lax.div(col, LANES)
        at = pl.ds(row + TOP, 1)
        work[SOURCE * tiles + c, at, :] += jnp.where(lane == col - c * LANES, rate_ref[i], 0.0)
    for b in range(blocks):
        wet = wet_ref[b].astype(jnp.float32)
        at = slice(TOP + b * block_rows, TOP + (b + 1) * block_rows)
        work[active_at(work), at, :] = jnp.full((block_rows, LANES), wet)
        plan_ref[b] = jnp.full((1, LANES), plan_smem[b])
    for copy in big:
        copy.wait()
    for k in range(SEND):
        for c in range(tiles):
            plane = sent_plane(work, k, c)
            up_ref[k * tiles + c] = work[plane, TOP : TOP + HALO, :]
            down_ref[k * tiles + c] = work[plane, bottom - HALO : bottom, :]


def packed(work, at, lane):
    tiles = tiles_of(work)
    out = None
    for k in range(SEND):
        first, last = sent_plane(work, k, 0), sent_plane(work, k, tiles - 1)
        ends = jnp.where(lane < HALO, work[first, at, :], work[last, at, :])
        ends = pltpu.roll(ends, 2 * HALO * k + HALO, 1)
        out = ends if out is None else jnp.where(lane >= 2 * HALO * k, ends, out)
    return out


def split_packed(turned, left_ref, right_ref, at):
    for k in range(SEND):
        lo = 2 * HALO * k
        right_ref[k, :, at] = turned[lo : lo + HALO, :]
        left_ref[k, :, at] = turned[lo + HALO : lo + 2 * HALO, :]


def pack_kernel(work, peak_hbm, left_ref, right_ref, pack, spread, sem):
    tiles = tiles_of(work)
    rows = pack.shape[0]
    lane = lane_ids(8)

    def find(r, acc):
        at = aligned(r * 8 + TOP, 8)
        active = work[active_at(work), at, :] > 0.5
        for c in range(tiles):
            speed = speed_of(*[work[k * tiles + c, at, :] for k in range(3)])
            acc = jnp.maximum(acc, jnp.where(active, speed, 0.0))
        return acc

    zero = jnp.zeros((8, LANES), jnp.float32)
    spread_peak(lax.fori_loop(0, rows // 8, find, zero, unroll=48), spread)
    copy = pltpu.make_async_copy(spread, peak_hbm, sem)
    copy.start()

    def one(r, carry):
        pack[aligned(r * 8, 8), :] = packed(work, aligned(r * 8 + TOP, 8), lane)
        return carry

    lax.fori_loop(0, rows // 8, one, 0, unroll=8)
    for q in range(rows // LANES):
        at = slice(q * LANES, (q + 1) * LANES)
        split_packed(pack[at, :].T, left_ref, right_ref, at)
    copy.wait()


def rows_kernel(
    work_in, left_in, right_in, above_ref, below_ref, work, left_ref, right_ref, pack
):
    tiles = tiles_of(work)
    own = left_ref.shape[2] - LANES
    bottom = TOP + own
    is_top = lax.axis_index("region") == 0
    is_bottom = lax.axis_index("region") == lax.axis_size("region") - 1

    def mirrored(first, step, to):
        for k in range(SEND):
            flip = -1.0 if k == 1 else 1.0
            for c in range(tiles):
                plane = sent_plane(work, k, c)
                for j in range(HALO):
                    work[plane, to - step * (1 + j), :] = work[plane, first + step * j, :] * flip

    def received(ref, lo):
        for k in range(SEND):
            for c in range(tiles):
                work[sent_plane(work, k, c), lo : lo + HALO, :] = ref[k * tiles + c]

    pl.when(is_top)(lambda: mirrored(TOP, 1, TOP))
    pl.when(jnp.logical_not(is_top))(lambda: received(above_ref, TOP - HALO))
    pl.when(is_bottom)(lambda: mirrored(bottom - 1, -1, bottom - 1))
    pl.when(jnp.logical_not(is_bottom))(lambda: received(below_ref, bottom))
    pack[...] = jnp.zeros_like(pack)
    lane = lane_ids(8)
    pack[0:8, :] = packed(work, slice(bottom, bottom + 8), lane)
    pack[LANES - 8 :, :] = packed(work, slice(0, 8), lane)
    split_packed(pack[...].T, left_ref, right_ref, slice(own, own + LANES))


def columns_kernel(own_left, own_right, from_left, from_right, strips):
    is_left = lax.axis_index("tile") == 0
    is_right = lax.axis_index("tile") == lax.axis_size("tile") - 1

    def mirrored(ref, side, to):
        for k in range(SEND):
            flip = -1.0 if k == 2 else 1.0
            for j in range(HALO):
                strips[side, k, to + HALO - 1 - j, :] = ref[k, j, :] * flip

    def received(ref, side, to):
        for k in range(SEND):
            strips[side, k, to : to + HALO, :] = ref[k]

    received(own_left, 0, HALO)
    received(own_right, 1, 0)
    pl.when(is_left)(lambda: mirrored(own_left, 0, 0))
    pl.when(jnp.logical_not(is_left))(lambda: received(from_left, 0, 0))
    pl.when(is_right)(lambda: mirrored(own_right, 1, HALO))
    pl.when(jnp.logical_not(is_right))(lambda: received(from_right, 1, HALO))


def roe(left, right):
    depth_l, normal_l, tangent_l, root_l, sn_l, st_l, press_l, shear_l = left
    depth_r, normal_r, tangent_r, root_r, sn_r, st_r, press_r, shear_r = right
    weight = pl.reciprocal(root_l + root_r, approx=False)
    speed = (sn_l + sn_r) * weight
    drift = (st_l + st_r) * weight
    half = (0.5 * GRAVITY) * (depth_l + depth_r)
    inverse = lax.rsqrt(half)
    celerity = half * inverse
    jump = depth_r - depth_l
    excess = (normal_r - normal_l) - speed * jump
    bend = excess * (0.5 * inverse)
    half_jump = 0.5 * jump
    slow = speed - celerity
    fast = speed + celerity
    wave_one = jnp.abs(slow) * (half_jump - bend)
    wave_three = jnp.abs(fast) * (half_jump + bend)
    wave_two = jnp.abs(speed) * ((tangent_r - tangent_l) - drift * jump)
    both = wave_one + wave_three
    flux_depth = (normal_l + normal_r) - both
    flux_normal = (press_l + press_r) - speed * both - celerity * (wave_three - wave_one)
    flux_tangent = (shear_l + shear_r) - drift * both - wave_two
    return flux_depth, flux_normal, flux_tangent


def side(depth, normal, tangent, root, sn, st):
    press = sn * sn + (0.5 * GRAVITY) * (depth * depth)
    return (depth, normal, tangent, root, sn, st, press, sn * st)


def flip(v):
    return (v[0], v[2], v[1], v[3], v[5], v[4])


def with_roots(depth, along, across):
    inverse = lax.rsqrt(depth)
    return [depth, along, across, depth * inverse, along * inverse, across * inverse]


def strip_fluxes(strips, ghost_rows):
    chunks = strips.shape[3] // LANES
    lane = lane_ids(8)
    for s in range(2):
        spans = [slice(q * LANES, (q + 1) * LANES) for q in range(chunks)]
        now = [with_roots(*[strips[s, k, :, at] for k in range(3)]) for at in spans]
        rows = []
        for q in range(chunks):
            below = [
                pltpu.roll(jnp.where(lane == 0, b, a), LANES - 1, 1)
                for a, b in zip(now[q], now[(q + 1) % chunks])
            ]
            rows.append(roe(side(*now[q]), side(*below)))
        for q, at in enumerate(spans):
            right = [pltpu.roll(v, 7, 0) for v in now[q]]
            f_depth, f_across, f_along = roe(side(*flip(now[q])), side(*flip(right)))
            active = strips[s, 3, :, at] > 0.5
            for f, flux in enumerate((f_depth, f_along, f_across)):
                above = jnp.where(lane == LANES - 1, rows[q - 1][f], rows[q][f])
                out = (flux - pltpu.roll(flux, 1, 0)) + (rows[q][f] - pltpu.roll(above, 1, 1))
                if f == 0:
                    out = out - 2.0 * strips[s, 4, :, at]
                strips[s, STRIP_DIFF + f, :, at] = jnp.where(active, out, 0.0)
                ghost_rows[(2 * f - s) % LANES, at] = flux[HALO - 1, :]


def turn_ghosts(ghost_rows, ghost):
    own = ghost_rows.shape[1] - LANES
    for q in range(own // LANES):
        at = slice(q * LANES, (q + 1) * LANES)
        ghost[TOP + q * LANES : TOP + (q + 1) * LANES, :] = ghost_rows[:, at].T
    ends = ghost_rows[:, own : own + LANES].T
    ghost[TOP + own : TOP + own + 8, :] = ends[0:8, :]
    ghost[0:8, :] = ends[LANES - 8 :, :]


def flux_kernel(part, *refs):
    if part == MAIN:
        work_in, work, derived, faces = refs
    elif part == EDGE:
        work_in, strips_in, work, strips, ghost_rows, ghost = refs
    else:
        work_in, strips_in, work, strips, derived, faces, ghost_rows, ghost = refs
    tiles = tiles_of(work)
    padded = work.shape[1]
    row_tiles = padded // 8
    active_rows = active_at(work)
    lane = lane_ids(8)
    first, last = lane == 0, lane == LANES - 1
    if part != MAIN:
        strip_fluxes(strips, ghost_rows)
        turn_ghosts(ghost_rows, ghost)

    def edge_fluxes(at):
        values = ghost[at, :]
        return [values] + [pltpu.roll(values, LANES - 2 * f, 1) for f in (1, 2)]

    if part == EDGE:

        def fix(r, carry):
            at = aligned(r * 8, 8)
            edges = edge_fluxes(at)
            active = work[active_rows, at, :] > 0.5
            for f in range(3):
                left, right = DIFF * tiles + f * tiles, DIFF * tiles + f * tiles + tiles - 1
                work[left, at, :] -= jnp.where(active & first, edges[f], 0.0)
                work[right, at, :] += jnp.where(active & last, edges[f], 0.0)
            return carry

        lax.fori_loop(0, row_tiles, fix, 0, unroll=10)
        return

    def derive(r, carry):
        for i in range(5):
            at = aligned(r * 40 + i * 8, 8)
            for c in range(tiles):
                roots = with_roots(*[work[k * tiles + c, at, :] for k in range(3)])
                for k in range(3):
                    derived[k * tiles + c, at, :] = roots[3 + k]
        return carry

    lax.fori_loop(0, row_tiles // 5, derive, 0, unroll=2)
    for p in range(3 * tiles):
        faces[p, 0:8, :] = jnp.zeros((8, LANES), jnp.float32)

    def load(c, at):
        return [ref[k * tiles + c, at, :] for ref in (work, derived) for k in range(3)]

    def fluxes(at, wrap):
        here, below = pl.ds(at, 8), pl.ds(at + 1, 8)
        now = [load(c, here) for c in range(tiles)]
        across = []
        for c in range(tiles):
            right = [
                pltpu.roll(jnp.where(first, b, a), LANES - 1, 1)
                for a, b in zip(now[c], now[(c + 1) % tiles])
            ]
            f_depth, f_across, f_along = roe(side(*flip(now[c])), side(*flip(right)))
            across.append([f_depth, f_along, f_across])
            under = [pltpu.roll(v, 7, 0) for v in now[c]] if wrap else load(c, below)
            flux = roe(side(*now[c]), side(*under))
            for f in range(3):
                faces[f * tiles + c, pl.ds(at + 8, 8), :] = flux[f]
        if part == ALL:
            edges = edge_fluxes(here)
        else:
            edges = [jnp.zeros((8, LANES), jnp.float32)] * 3
        for f in range(3):
            across[-1][f] = jnp.where(last, edges[f], across[-1][f])
        active = work[active_rows, here, :] > 0.5
        for c in range(tiles):
            for f in range(3):
                if c:
                    left = pltpu.roll(jnp.where(last, across[c - 1][f], across[c][f]), 1, 1)
                else:
                    left = jnp.where(first, edges[f], pltpu.roll(across[c][f], 1, 1))
                plane = f * tiles + c
                out = (across[c][f] - left) + (
                    faces[plane, pl.ds(at + 8, 8), :] - faces[plane, pl.ds(at + 7, 8), :]
                )
                if f == 0:
                    out = out - 2.0 * work[SOURCE * tiles + c, here, :]
                work[(DIFF + f) * tiles + c, here, :] = jnp.where(active, out, 0.0)

    def one(r, carry):
        fluxes(pl.multiple_of(r * 8, 8), False)
        return carry

    lax.fori_loop(0, row_tiles - 1, one, 0, unroll=FLUX_UNROLL)
    fluxes(padded - 8, True)


def step_ratio(peak_ref):
    peak = jnp.max(jnp.max(peak_ref[...], axis=0), axis=0, keepdims=True)
    step = (COURANT * SPACING) / peak
    return jnp.broadcast_to((0.5 / SPACING) * step, (8, LANES))


def moved(work, c, at, ratio):
    tiles = tiles_of(work)
    return [
        work[f * tiles + c, at, :] - ratio * work[(DIFF + f) * tiles + c, at, :] for f in range(3)
    ]


def move_own(work, at, ratio):
    tiles = tiles_of(work)
    for c in range(tiles):
        for f, new in enumerate(moved(work, c, at, ratio)):
            work[f * tiles + c, at, :] = new


def update_kernel(peak_ref, work_in, strips_in, work, strips, next_hbm, spread, sem):
    tiles = tiles_of(work)
    row_tiles = work.shape[1] // 8
    ratio = step_ratio(peak_ref)

    def find(r, acc):
        at = aligned(r * 8 + TOP, 8)
        active = work[active_at(work), at, :] > 0.5
        for c in range(tiles):
            acc = jnp.maximum(acc, jnp.where(active, speed_of(*moved(work, c, at, ratio)), 0.0))
        return acc

    zero = jnp.zeros((8, LANES), jnp.float32)
    spread_peak(lax.fori_loop(0, row_tiles - 2, find, zero, unroll=48), spread)
    copy = pltpu.make_async_copy(spread, next_hbm, sem)
    copy.start()
    for q in range(strips.shape[3] // LANES):
        span = slice(q * LANES, (q + 1) * LANES)
        for k in range(3):
            for s in range(2):
                strips[s, k, :, span] -= ratio * strips[s, STRIP_DIFF + k, :, span]

    def move(r, carry):
        move_own(work, aligned(r * 8, 8), ratio)
        return carry

    lax.fori_loop(0, row_tiles, move, 0, unroll=10)
    copy.wait()


def last_kernel(peak_ref, plan_ref, work, mine_ref, theirs_ref, best):
    tiles = tiles_of(work)
    blocks = plan_ref.shape[0]
    block_rows = (work.shape[1] - 2 * 8) // blocks
    ratio = step_ratio(peak_ref)

    def one_block(b, carry):
        acc = jnp.zeros((8, LANES), jnp.float32)
        for r in range(0, block_rows, 8):
            at = aligned(b * block_rows + TOP + r, 8)
            for c in range(tiles):
                acc = jnp.maximum(acc, speed_of(*moved(work, c, at, ratio)))
        best[b] = acc
        return carry

    lax.fori_loop(0, blocks, one_block, 0, unroll=8)
    is_odd = lax.rem(lax.axis_index("tile"), 2) == 1
    for j in range(mine_ref.shape[0]):
        pair = []
        for t in (2 * j, 2 * j + 1):
            acc = jnp.zeros((8, LANES), jnp.float32)
            for b in range(blocks):
                acc = jnp.maximum(acc, jnp.where(plan_ref[b] == t, best[b], 0.0))
            top = jnp.max(acc, axis=0, keepdims=True)
            pair.append(jnp.broadcast_to(jnp.max(top, axis=1, keepdims=True), (1, LANES)))
        mine_ref[j] = jnp.where(is_odd, pair[1], pair[0])
        theirs_ref[j] = jnp.where(is_odd, pair[0], pair[1])


def chip_kernel(mine_ref, other_ref, *out_refs):
    here = lax.div(lax.axis_index("tile"), 2)
    for x, out_ref in enumerate(out_refs):
        there = jnp.bitwise_xor(here, x)
        out_ref[...] = jnp.maximum(mine_ref[there], other_ref[there])


def helper_kernel(*refs):
    value = refs[0][...]
    for ref in refs[1:-1]:
        value = jnp.maximum(value, ref[...])
    refs[-1][...] = value[:, :1]


def store_kernel(peak_ref, work_in, work, depth_hbm, mom_hbm, sem):
    rows, cols = depth_hbm.shape
    tiles = cols // LANES
    ratio = step_ratio(peak_ref)

    def move(r, carry):
        move_own(work, aligned(r * 8 + TOP, 8), ratio)
        return carry

    lax.fori_loop(0, rows // 8, move, 0, unroll=8)
    copies = []
    for k, dst in enumerate([depth_hbm, mom_hbm.at[0], mom_hbm.at[1]]):
        for c in range(tiles):
            copies.append(
                pltpu.make_async_copy(
                    work.at[k * tiles + c, pl.ds(TOP, rows), :],
                    dst.at[:, pl.ds(c * LANES, LANES)],
                    sem.at[k, c],
                )
            )
    for copy in copies:
        copy.start()
    for copy in copies:
        copy.wait()


def exchange(x, axes):
    return lax.all_to_all(x, axes, 0, 0)


def swap(x, axis, apart):
    return lax.ppermute(x, axis, [(i, i ^ apart) for i in range(lax.axis_size(axis))])


def send(x, axis, forward):
    count = lax.axis_size(axis)
    pairs = [(i, (i + 1) % count) if forward else ((i + 1) % count, i) for i in range(count)]
    return lax.ppermute(x, axis, pairs)


def on_device(water_depth, momentum, wet_mask, helper_plan, breach_cells, breach_rate):
    rows, cols = water_depth.shape
    tile_count = lax.axis_size("tile")
    everyone = tile_count * lax.axis_size("region")
    blocks = wet_mask.shape[0]
    tiles = cols // LANES
    padded = rows + 2 * 8
    f32 = jnp.float32
    cells = breach_cells.reshape(-1)
    rates = breach_rate.reshape(-1)
    nbytes = 4 * 3 * rows * cols
    work_out = vmem_out(FIELDS * tiles + 1, padded, LANES)
    strips_out = vmem_out(2, STRIP_FIELDS, 2 * HALO, rows + LANES)
    strip_out = vmem_out(SEND, HALO, rows + LANES)
    edge_out = vmem_out(SEND * tiles, HALO, LANES)
    peak_out = jax.ShapeDtypeStruct((everyone, 1, LANES), f32)
    first_out = jax.ShapeDtypeStruct((everyone, FIRST, LANES), f32)

    work, plan, up, down = pl.pallas_call(
        start_kernel,
        out_shape=(work_out, pltpu.VMEM((blocks, 1, LANES), jnp.int32), edge_out, edge_out),
        in_specs=[hbm_spec()] * 6,
        out_specs=(vmem_spec(),) * 4,
        scratch_shapes=[
            pltpu.SMEM((blocks,), jnp.int32),
            pltpu.SMEM((blocks,), jnp.int32),
            pltpu.SMEM(cells.shape, jnp.int32),
            pltpu.SMEM(cells.shape, f32),
            pltpu.SemaphoreType.DMA((4,)),
            pltpu.SemaphoreType.DMA((3, tiles)),
        ],
        compiler_params=params(),
        cost_estimate=cost(2 * rows * cols, nbytes),
        name="start",
    )(
        *(
            pltpu.with_memory_space_constraint(x, pltpu.HBM)
            for x in (
                wet_mask.reshape(-1),
                helper_plan.reshape(-1),
                cells,
                rates,
                water_depth,
                momentum,
            )
        )
    )

    above = send(down, "region", True)
    below = send(up, "region", False)

    peak, left, right = pl.pallas_call(
        pack_kernel,
        out_shape=(first_out, strip_out, strip_out),
        in_specs=[vmem_spec()],
        out_specs=(hbm_spec(), vmem_spec(), vmem_spec()),
        scratch_shapes=[
            pltpu.VMEM((rows, LANES), f32),
            pltpu.VMEM(first_out.shape, f32),
            pltpu.SemaphoreType.DMA,
        ],
        compiler_params=params(),
        cost_estimate=cost(20 * rows * cols, nbytes),
        name="pack",
    )(work)

    work, left, right = pl.pallas_call(
        rows_kernel,
        out_shape=(work_out, strip_out, strip_out),
        in_specs=[vmem_spec()] * 5,
        out_specs=(vmem_spec(),) * 3,
        scratch_shapes=[pltpu.VMEM((LANES, LANES), f32)],
        input_output_aliases={0: 0, 1: 1, 2: 2},
        compiler_params=params(),
        cost_estimate=cost(rows * cols, nbytes // 8),
        name="rows",
    )(work, left, right, above, below)

    from_left = send(right, "tile", True)
    from_right = send(left, "tile", False)
    peaks = exchange(peak, ("region", "tile"))

    def flux(part, work, *strips):
        outs = (work_out, strips_out)[: 1 + len(strips)]
        main = [
            pltpu.VMEM((3 * tiles, padded, LANES), f32),
            pltpu.VMEM((3 * tiles, padded + 8, LANES), f32),
        ]
        edge = [pltpu.VMEM((LANES, rows + LANES), f32), pltpu.VMEM((padded, LANES), f32)]
        flops, moved_bytes = FLUX_COST[part]
        return pl.pallas_call(
            functools.partial(flux_kernel, part),
            out_shape=outs,
            in_specs=[vmem_spec()] * len(outs),
            out_specs=(vmem_spec(),) * len(outs),
            scratch_shapes=(main + edge, main, edge)[part],
            input_output_aliases={i: i for i in range(len(outs))},
            compiler_params=params(),
            cost_estimate=cost(int(flops * rows * cols), int(moved_bytes * nbytes)),
            name=("flux", "main", "edge")[part],
        )(work, *strips)

    (work,) = flux(MAIN, work)
    strips = pl.pallas_call(
        columns_kernel,
        out_shape=strips_out,
        in_specs=[vmem_spec()] * 4,
        out_specs=vmem_spec(),
        compiler_params=params(),
        cost_estimate=cost(rows * cols, nbytes // 8),
        name="columns",
    )(left, right, from_left, from_right)

    for step in range(STEPS):
        work, strips = flux(ALL if step else EDGE, work, strips)
        if step < STEPS - 1:
            work, strips, peak = pl.pallas_call(
                update_kernel,
                out_shape=(
                    work_out,
                    strips_out,
                    peak_out,
                ),
                in_specs=[vmem_spec()] * 3,
                out_specs=(vmem_spec(), vmem_spec(), hbm_spec()),
                scratch_shapes=[
                    pltpu.VMEM((everyone, 1, LANES), f32),
                    pltpu.SemaphoreType.DMA,
                ],
                input_output_aliases={1: 0, 2: 1},
                compiler_params=params(),
                cost_estimate=cost(20 * rows * cols, nbytes),
                name="update",
            )(peaks, work, strips)
            peaks = exchange(peak, ("region", "tile"))

    chips = tile_count // 2
    mine, theirs = pl.pallas_call(
        last_kernel,
        out_shape=(vmem_out(chips, 1, LANES),) * 2,
        in_specs=[vmem_spec()] * 3,
        out_specs=(vmem_spec(),) * 2,
        scratch_shapes=[pltpu.VMEM((blocks, 8, LANES), f32)],
        compiler_params=params(),
        cost_estimate=cost(20 * rows * cols, 2 * nbytes),
        name="last",
    )(peaks, plan, work)
    other = swap(theirs, "tile", 1)
    known = pl.pallas_call(
        chip_kernel,
        out_shape=(vmem_out(1, LANES),) * chips,
        in_specs=[vmem_spec()] * 2,
        out_specs=(vmem_spec(),) * chips,
        compiler_params=params(),
        cost_estimate=cost(tile_count, 4 * LANES * tile_count),
        name="chip",
    )(mine, other)
    known = [swap(known[x], "tile", 2 * x) for x in range(chips - 1, 0, -1)] + [known[0]]
    work, new_depth, new_momentum = pl.pallas_call(
        store_kernel,
        out_shape=(
            work_out,
            jax.ShapeDtypeStruct((rows, cols), f32),
            jax.ShapeDtypeStruct((2, rows, cols), f32),
        ),
        in_specs=[vmem_spec()] * 2,
        out_specs=(vmem_spec(), hbm_spec(), hbm_spec()),
        scratch_shapes=[pltpu.SemaphoreType.DMA((3, tiles))],
        input_output_aliases={1: 0},
        compiler_params=params(),
        cost_estimate=cost(10 * rows * cols, 2 * nbytes),
        name="store",
    )(peaks, work)
    helper = pl.pallas_call(
        helper_kernel,
        out_shape=jax.ShapeDtypeStruct((1, 1), f32),
        in_specs=[vmem_spec()] * chips,
        out_specs=vmem_spec(),
        compiler_params=params(),
        cost_estimate=cost(tile_count, 4 * LANES * tile_count),
        name="helper",
    )(*known)
    return new_depth, new_momentum, helper


def solution(mesh):
    return jax.shard_map(
        on_device,
        mesh=mesh,
        in_specs=(
            P("region", "tile"),
            P(None, "region", "tile"),
            P("region", "tile"),
            P("region", "tile"),
            P("region", "tile", None),
            P("region", "tile", None),
        ),
        out_specs=(P("region", "tile"), P(None, "region", "tile"), P("region", "tile")),
        check_vma=False,
    )
```

```python
import functools

import jax
import jax.numpy as jnp
from jax import lax
from jax.experimental import pallas as pl
from jax.experimental.pallas import tpu as pltpu
from jax.sharding import PartitionSpec as P

STEPS = 4
HALO = 4
LANES = 128
TOP = 8

GRAVITY = 9.81
COURANT = 0.45
SPACING = 1.0

VMEM_LIMIT = 20 << 20
FLUX_UNROLL = 7
FIRST = 2
FLUX_COST = ((150, 4), (150, 4), (500, 20))


SOURCE, DIFF, FIELDS = 3, 4, 7
SEND = 5
STRIP_DIFF, STRIP_FIELDS = 5, 8
ALL, MAIN, EDGE = range(3)


def tiles_of(work):
    return (work.shape[0] - 1) // FIELDS


def active_at(work):
    return work.shape[0] - 1


def sent_plane(work, k, c):
    tiles = tiles_of(work)
    return (k * tiles + c, active_at(work), SOURCE * tiles + c)[max(k - 2, 0)]


def vmem_spec():
    return pl.BlockSpec(memory_space=pltpu.VMEM)


def hbm_spec():
    return pl.BlockSpec(memory_space=pltpu.HBM)


def vmem_out(*shape):
    return pltpu.VMEM(shape, jnp.float32)


def params():
    return pltpu.CompilerParams(vmem_limit_bytes=VMEM_LIMIT)


def cost(flops, nbytes):
    return pl.CostEstimate(flops=flops, bytes_accessed=nbytes, transcendentals=0)


def lane_ids(rows):
    return lax.broadcasted_iota(jnp.int32, (rows, LANES), 1)


def aligned(start, size):
    return pl.ds(pl.multiple_of(start, 8), size)


def speed_of(depth, along, across):
    root = lax.rsqrt(depth)
    inverse = root * root
    return jnp.maximum(jnp.abs(along), jnp.abs(across)) * inverse + jnp.sqrt(
        jnp.float32(GRAVITY)
    ) * (depth * root)


def spread_peak(acc, out_ref):
    top = jnp.max(jnp.max(acc, axis=0, keepdims=True), axis=1, keepdims=True)
    out_ref[...] = jnp.broadcast_to(top[None], out_ref.shape)


def start_kernel(
    wet_hbm,
    plan_hbm,
    cell_hbm,
    rate_hbm,
    depth_hbm,
    mom_hbm,
    work,
    plan_ref,
    up_ref,
    down_ref,
    wet_ref,
    plan_smem,
    cell_ref,
    rate_ref,
    small_sem,
    big_sem,
):
    rows, cols = depth_hbm.shape
    tiles = cols // LANES
    padded = work.shape[1]
    blocks = wet_hbm.shape[0]
    block_rows = rows // blocks
    bottom = TOP + rows
    small = [
        pltpu.make_async_copy(src, dst, small_sem.at[i])
        for i, (src, dst) in enumerate(
            [
                (cell_hbm, cell_ref),
                (rate_hbm, rate_ref),
                (wet_hbm, wet_ref),
                (plan_hbm, plan_smem),
            ]
        )
    ]
    big = []
    for k, src in enumerate([depth_hbm, mom_hbm.at[0], mom_hbm.at[1]]):
        for c in range(tiles):
            big.append(
                pltpu.make_async_copy(
                    src.at[:, pl.ds(c * LANES, LANES)],
                    work.at[k * tiles + c, pl.ds(TOP, rows), :],
                    big_sem.at[k, c],
                )
            )
    for copy in small + big:
        copy.start()
    for k in range(SEND):
        for c in range(tiles):
            plane = sent_plane(work, k, c)
            fill = 1.0 if k == 0 else 0.0
            work[plane, 0:TOP, :] = jnp.full((TOP, LANES), fill, jnp.float32)
            work[plane, bottom:padded, :] = jnp.full((padded - bottom, LANES), fill, jnp.float32)
    for c in range(tiles):
        work[SOURCE * tiles + c, TOP:bottom, :] = jnp.zeros((rows, LANES), jnp.float32)
    for copy in small:
        copy.wait()
    lane = lane_ids(1)

    for i in range(cell_ref.shape[0]):
        cell = cell_ref[i]
        row = lax.div(cell, cols)
        col = cell - row * cols
        c = lax.div(col, LANES)
        at = pl.ds(row + TOP, 1)
        work[SOURCE * tiles + c, at, :] += jnp.where(lane == col - c * LANES, rate_ref[i], 0.0)
    for b in range(blocks):
        wet = wet_ref[b].astype(jnp.float32)
        at = slice(TOP + b * block_rows, TOP + (b + 1) * block_rows)
        work[active_at(work), at, :] = jnp.full((block_rows, LANES), wet)
        plan_ref[b] = jnp.full((1, LANES), plan_smem[b])
    for copy in big:
        copy.wait()
    for k in range(SEND):
        for c in range(tiles):
            plane = sent_plane(work, k, c)
            up_ref[k * tiles + c] = work[plane, TOP : TOP + HALO, :]
            down_ref[k * tiles + c] = work[plane, bottom - HALO : bottom, :]


def packed(work, at, lane):
    tiles = tiles_of(work)
    out = None
    for k in range(SEND):
        first, last = sent_plane(work, k, 0), sent_plane(work, k, tiles - 1)
        ends = jnp.where(lane < HALO, work[first, at, :], work[last, at, :])
        ends = pltpu.roll(ends, 2 * HALO * k + HALO, 1)
        out = ends if out is None else jnp.where(lane >= 2 * HALO * k, ends, out)
    return out


def split_packed(turned, left_ref, right_ref, at):
    for k in range(SEND):
        lo = 2 * HALO * k
        right_ref[k, :, at] = turned[lo : lo + HALO, :]
        left_ref[k, :, at] = turned[lo + HALO : lo + 2 * HALO, :]


def pack_kernel(work, peak_hbm, left_ref, right_ref, pack, spread, sem):
    tiles = tiles_of(work)
    rows = pack.shape[0]
    lane = lane_ids(8)

    def find(r, acc):
        at = aligned(r * 8 + TOP, 8)
        active = work[active_at(work), at, :] > 0.5
        for c in range(tiles):
            speed = speed_of(*[work[k * tiles + c, at, :] for k in range(3)])
            acc = jnp.maximum(acc, jnp.where(active, speed, 0.0))
        return acc

    zero = jnp.zeros((8, LANES), jnp.float32)
    spread_peak(lax.fori_loop(0, rows // 8, find, zero, unroll=48), spread)
    copy = pltpu.make_async_copy(spread, peak_hbm, sem)
    copy.start()

    def one(r, carry):
        pack[aligned(r * 8, 8), :] = packed(work, aligned(r * 8 + TOP, 8), lane)
        return carry

    lax.fori_loop(0, rows // 8, one, 0, unroll=24)
    for q in range(rows // LANES):
        at = slice(q * LANES, (q + 1) * LANES)
        split_packed(pack[at, :].T, left_ref, right_ref, at)
    copy.wait()


def rows_kernel(
    work_in, left_in, right_in, above_ref, below_ref, work, left_ref, right_ref, pack
):
    tiles = tiles_of(work)
    own = left_ref.shape[2] - LANES
    bottom = TOP + own
    is_top = lax.axis_index("region") == 0
    is_bottom = lax.axis_index("region") == lax.axis_size("region") - 1

    def mirrored(first, step, to):
        for k in range(SEND):
            flip = -1.0 if k == 1 else 1.0
            for c in range(tiles):
                plane = sent_plane(work, k, c)
                for j in range(HALO):
                    work[plane, to - step * (1 + j), :] = work[plane, first + step * j, :] * flip

    def received(ref, lo):
        for k in range(SEND):
            for c in range(tiles):
                work[sent_plane(work, k, c), lo : lo + HALO, :] = ref[k * tiles + c]

    pl.when(is_top)(lambda: mirrored(TOP, 1, TOP))
    pl.when(jnp.logical_not(is_top))(lambda: received(above_ref, TOP - HALO))
    pl.when(is_bottom)(lambda: mirrored(bottom - 1, -1, bottom - 1))
    pl.when(jnp.logical_not(is_bottom))(lambda: received(below_ref, bottom))
    pack[...] = jnp.zeros_like(pack)
    lane = lane_ids(8)
    pack[0:8, :] = packed(work, slice(bottom, bottom + 8), lane)
    pack[LANES - 8 :, :] = packed(work, slice(0, 8), lane)
    split_packed(pack[...].T, left_ref, right_ref, slice(own, own + LANES))


def columns_kernel(own_left, own_right, from_left, from_right, strips):
    is_left = lax.axis_index("tile") == 0
    is_right = lax.axis_index("tile") == lax.axis_size("tile") - 1

    def mirrored(ref, side, to):
        for k in range(SEND):
            flip = -1.0 if k == 2 else 1.0
            for j in range(HALO):
                strips[side, k, to + HALO - 1 - j, :] = ref[k, j, :] * flip

    def received(ref, side, to):
        for k in range(SEND):
            strips[side, k, to : to + HALO, :] = ref[k]

    received(own_left, 0, HALO)
    received(own_right, 1, 0)
    pl.when(is_left)(lambda: mirrored(own_left, 0, 0))
    pl.when(jnp.logical_not(is_left))(lambda: received(from_left, 0, 0))
    pl.when(is_right)(lambda: mirrored(own_right, 1, HALO))
    pl.when(jnp.logical_not(is_right))(lambda: received(from_right, 1, HALO))


def roe(left, right):
    depth_l, normal_l, tangent_l, root_l, sn_l, st_l, press_l, shear_l = left
    depth_r, normal_r, tangent_r, root_r, sn_r, st_r, press_r, shear_r = right
    weight = pl.reciprocal(root_l + root_r, approx=False)
    speed = (sn_l + sn_r) * weight
    drift = (st_l + st_r) * weight
    half = (0.5 * GRAVITY) * (depth_l + depth_r)
    inverse = lax.rsqrt(half)
    celerity = half * inverse
    jump = depth_r - depth_l
    excess = (normal_r - normal_l) - speed * jump
    bend = excess * (0.5 * inverse)
    half_jump = 0.5 * jump
    slow = speed - celerity
    fast = speed + celerity
    wave_one = jnp.abs(slow) * (half_jump - bend)
    wave_three = jnp.abs(fast) * (half_jump + bend)
    wave_two = jnp.abs(speed) * ((tangent_r - tangent_l) - drift * jump)
    both = wave_one + wave_three
    flux_depth = (normal_l + normal_r) - both
    flux_normal = (press_l + press_r) - speed * both - celerity * (wave_three - wave_one)
    flux_tangent = (shear_l + shear_r) - drift * both - wave_two
    return flux_depth, flux_normal, flux_tangent


def side(depth, normal, tangent, root, sn, st):
    press = sn * sn + (0.5 * GRAVITY) * (depth * depth)
    return (depth, normal, tangent, root, sn, st, press, sn * st)


def flip(v):
    return (v[0], v[2], v[1], v[3], v[5], v[4])


def with_roots(depth, along, across):
    inverse = lax.rsqrt(depth)
    return [depth, along, across, depth * inverse, along * inverse, across * inverse]


def strip_fluxes(strips, ghost_rows):
    chunks = strips.shape[3] // LANES
    lane = lane_ids(8)
    for s in range(2):
        spans = [slice(q * LANES, (q + 1) * LANES) for q in range(chunks)]
        now = [with_roots(*[strips[s, k, :, at] for k in range(3)]) for at in spans]
        rows = []
        for q in range(chunks):
            below = [
                pltpu.roll(jnp.where(lane == 0, b, a), LANES - 1, 1)
                for a, b in zip(now[q], now[(q + 1) % chunks])
            ]
            rows.append(roe(side(*now[q]), side(*below)))
        for q, at in enumerate(spans):
            right = [pltpu.roll(v, 7, 0) for v in now[q]]
            f_depth, f_across, f_along = roe(side(*flip(now[q])), side(*flip(right)))
            active = strips[s, 3, :, at] > 0.5
            for f, flux in enumerate((f_depth, f_along, f_across)):
                above = jnp.where(lane == LANES - 1, rows[q - 1][f], rows[q][f])
                out = (flux - pltpu.roll(flux, 1, 0)) + (rows[q][f] - pltpu.roll(above, 1, 1))
                if f == 0:
                    out = out - 2.0 * strips[s, 4, :, at]
                strips[s, STRIP_DIFF + f, :, at] = jnp.where(active, out, 0.0)
                ghost_rows[(2 * f - s) % LANES, at] = flux[HALO - 1, :]


def turn_ghosts(ghost_rows, ghost):
    own = ghost_rows.shape[1] - LANES
    for q in range(own // LANES):
        at = slice(q * LANES, (q + 1) * LANES)
        ghost[TOP + q * LANES : TOP + (q + 1) * LANES, :] = ghost_rows[:, at].T
    ends = ghost_rows[:, own : own + LANES].T
    ghost[TOP + own : TOP + own + 8, :] = ends[0:8, :]
    ghost[0:8, :] = ends[LANES - 8 :, :]


def flux_kernel(part, *refs):
    if part == MAIN:
        work_in, work, derived, faces = refs
    elif part == EDGE:
        work_in, strips_in, work, strips, ghost_rows, ghost = refs
    else:
        work_in, strips_in, work, strips, derived, faces, ghost_rows, ghost = refs
    tiles = tiles_of(work)
    padded = work.shape[1]
    row_tiles = padded // 8
    active_rows = active_at(work)
    lane = lane_ids(8)
    first, last = lane == 0, lane == LANES - 1
    if part != MAIN:
        strip_fluxes(strips, ghost_rows)
        turn_ghosts(ghost_rows, ghost)

    def edge_fluxes(at):
        values = ghost[at, :]
        return [values] + [pltpu.roll(values, LANES - 2 * f, 1) for f in (1, 2)]

    if part == EDGE:

        def fix(r, carry):
            at = aligned(r * 8, 8)
            edges = edge_fluxes(at)
            active = work[active_rows, at, :] > 0.5
            for f in range(3):
                left, right = DIFF * tiles + f * tiles, DIFF * tiles + f * tiles + tiles - 1
                work[left, at, :] -= jnp.where(active & first, edges[f], 0.0)
                work[right, at, :] += jnp.where(active & last, edges[f], 0.0)
            return carry

        lax.fori_loop(0, row_tiles, fix, 0, unroll=25)
        return

    def derive(r, carry):
        for i in range(5):
            at = aligned(r * 40 + i * 8, 8)
            for c in range(tiles):
                roots = with_roots(*[work[k * tiles + c, at, :] for k in range(3)])
                for k in range(3):
                    derived[k * tiles + c, at, :] = roots[3 + k]
        return carry

    lax.fori_loop(0, row_tiles // 5, derive, 0, unroll=5)
    for p in range(3 * tiles):
        faces[p, 0:8, :] = jnp.zeros((8, LANES), jnp.float32)

    def load(c, at):
        return [ref[k * tiles + c, at, :] for ref in (work, derived) for k in range(3)]

    def fluxes(at, wrap):
        here, below = pl.ds(at, 8), pl.ds(at + 1, 8)
        now = [load(c, here) for c in range(tiles)]
        across = []
        for c in range(tiles):
            right = [
                pltpu.roll(jnp.where(first, b, a), LANES - 1, 1)
                for a, b in zip(now[c], now[(c + 1) % tiles])
            ]
            f_depth, f_across, f_along = roe(side(*flip(now[c])), side(*flip(right)))
            across.append([f_depth, f_along, f_across])
            under = [pltpu.roll(v, 7, 0) for v in now[c]] if wrap else load(c, below)
            flux = roe(side(*now[c]), side(*under))
            for f in range(3):
                faces[f * tiles + c, pl.ds(at + 8, 8), :] = flux[f]
        if part == ALL:
            edges = edge_fluxes(here)
        else:
            edges = [jnp.zeros((8, LANES), jnp.float32)] * 3
        for f in range(3):
            across[-1][f] = jnp.where(last, edges[f], across[-1][f])
        active = work[active_rows, here, :] > 0.5
        for c in range(tiles):
            for f in range(3):
                if c:
                    left = pltpu.roll(jnp.where(last, across[c - 1][f], across[c][f]), 1, 1)
                else:
                    left = jnp.where(first, edges[f], pltpu.roll(across[c][f], 1, 1))
                plane = f * tiles + c
                out = (across[c][f] - left) + (
                    faces[plane, pl.ds(at + 8, 8), :] - faces[plane, pl.ds(at + 7, 8), :]
                )
                if f == 0:
                    out = out - 2.0 * work[SOURCE * tiles + c, here, :]
                work[(DIFF + f) * tiles + c, here, :] = jnp.where(active, out, 0.0)

    def one(r, carry):
        fluxes(pl.multiple_of(r * 8, 8), False)
        return carry

    lax.fori_loop(0, row_tiles - 1, one, 0, unroll=FLUX_UNROLL)
    fluxes(padded - 8, True)


def step_ratio(peak_ref):
    peak = jnp.max(jnp.max(peak_ref[...], axis=0), axis=0, keepdims=True)
    step = (COURANT * SPACING) / peak
    return jnp.broadcast_to((0.5 / SPACING) * step, (8, LANES))


def moved(work, c, at, ratio):
    tiles = tiles_of(work)
    return [
        work[f * tiles + c, at, :] - ratio * work[(DIFF + f) * tiles + c, at, :] for f in range(3)
    ]


def move_own(work, at, ratio):
    tiles = tiles_of(work)
    for c in range(tiles):
        for f, new in enumerate(moved(work, c, at, ratio)):
            work[f * tiles + c, at, :] = new


def update_kernel(peak_ref, work_in, strips_in, work, strips, next_hbm, spread, sem):
    tiles = tiles_of(work)
    row_tiles = work.shape[1] // 8
    ratio = step_ratio(peak_ref)

    def find(r, acc):
        at = aligned(r * 8 + TOP, 8)
        active = work[active_at(work), at, :] > 0.5
        for c in range(tiles):
            acc = jnp.maximum(acc, jnp.where(active, speed_of(*moved(work, c, at, ratio)), 0.0))
        return acc

    zero = jnp.zeros((8, LANES), jnp.float32)
    spread_peak(lax.fori_loop(0, row_tiles - 2, find, zero, unroll=48), spread)
    copy = pltpu.make_async_copy(spread, next_hbm, sem)
    copy.start()
    for q in range(strips.shape[3] // LANES):
        span = slice(q * LANES, (q + 1) * LANES)
        for k in range(3):
            for s in range(2):
                strips[s, k, :, span] -= ratio * strips[s, STRIP_DIFF + k, :, span]

    def move(r, carry):
        move_own(work, aligned(r * 8, 8), ratio)
        return carry

    lax.fori_loop(0, row_tiles, move, 0, unroll=10)
    copy.wait()


def last_kernel(peak_ref, plan_ref, work, mine_ref, theirs_ref, best):
    tiles = tiles_of(work)
    blocks = plan_ref.shape[0]
    block_rows = (work.shape[1] - 2 * 8) // blocks
    ratio = step_ratio(peak_ref)

    def one_block(b, carry):
        acc = jnp.zeros((8, LANES), jnp.float32)
        for r in range(0, block_rows, 8):
            at = aligned(b * block_rows + TOP + r, 8)
            for c in range(tiles):
                acc = jnp.maximum(acc, speed_of(*moved(work, c, at, ratio)))
        best[b] = acc
        return carry

    lax.fori_loop(0, blocks, one_block, 0, unroll=8)
    is_odd = lax.rem(lax.axis_index("tile"), 2) == 1
    for j in range(mine_ref.shape[0]):
        pair = []
        for t in (2 * j, 2 * j + 1):
            acc = jnp.zeros((8, LANES), jnp.float32)
            for b in range(blocks):
                acc = jnp.maximum(acc, jnp.where(plan_ref[b] == t, best[b], 0.0))
            top = jnp.max(acc, axis=0, keepdims=True)
            pair.append(jnp.broadcast_to(jnp.max(top, axis=1, keepdims=True), (1, LANES)))
        mine_ref[j] = jnp.where(is_odd, pair[1], pair[0])
        theirs_ref[j] = jnp.where(is_odd, pair[0], pair[1])


def chip_kernel(mine_ref, other_ref, *out_refs):
    here = lax.div(lax.axis_index("tile"), 2)
    for x, out_ref in enumerate(out_refs):
        there = jnp.bitwise_xor(here, x)
        out_ref[...] = jnp.maximum(mine_ref[there], other_ref[there])


def helper_kernel(*refs):
    value = refs[0][...]
    for ref in refs[1:-1]:
        value = jnp.maximum(value, ref[...])
    refs[-1][...] = value[:, :1]


def store_kernel(peak_ref, work_in, work, depth_hbm, mom_hbm, sem):
    rows, cols = depth_hbm.shape
    tiles = cols // LANES
    ratio = step_ratio(peak_ref)

    def move(r, carry):
        move_own(work, aligned(r * 8 + TOP, 8), ratio)
        return carry

    lax.fori_loop(0, rows // 8, move, 0, unroll=8)
    copies = []
    for k, dst in enumerate([depth_hbm, mom_hbm.at[0], mom_hbm.at[1]]):
        for c in range(tiles):
            copies.append(
                pltpu.make_async_copy(
                    work.at[k * tiles + c, pl.ds(TOP, rows), :],
                    dst.at[:, pl.ds(c * LANES, LANES)],
                    sem.at[k, c],
                )
            )
    for copy in copies:
        copy.start()
    for copy in copies:
        copy.wait()


def exchange(x, axes):
    return lax.all_to_all(x, axes, 0, 0)


def swap(x, axis, apart):
    return lax.ppermute(x, axis, [(i, i ^ apart) for i in range(lax.axis_size(axis))])


def send(x, axis, forward):
    count = lax.axis_size(axis)
    pairs = [(i, (i + 1) % count) if forward else ((i + 1) % count, i) for i in range(count)]
    return lax.ppermute(x, axis, pairs)


def on_device(water_depth, momentum, wet_mask, helper_plan, breach_cells, breach_rate):
    rows, cols = water_depth.shape
    tile_count = lax.axis_size("tile")
    everyone = tile_count * lax.axis_size("region")
    blocks = wet_mask.shape[0]
    tiles = cols // LANES
    padded = rows + 2 * 8
    f32 = jnp.float32
    cells = breach_cells.reshape(-1)
    rates = breach_rate.reshape(-1)
    nbytes = 4 * 3 * rows * cols
    work_out = vmem_out(FIELDS * tiles + 1, padded, LANES)
    strips_out = vmem_out(2, STRIP_FIELDS, 2 * HALO, rows + LANES)
    strip_out = vmem_out(SEND, HALO, rows + LANES)
    edge_out = vmem_out(SEND * tiles, HALO, LANES)
    peak_out = jax.ShapeDtypeStruct((everyone, 1, LANES), f32)
    first_out = jax.ShapeDtypeStruct((everyone, FIRST, LANES), f32)

    work, plan, up, down = pl.pallas_call(
        start_kernel,
        out_shape=(work_out, pltpu.VMEM((blocks, 1, LANES), jnp.int32), edge_out, edge_out),
        in_specs=[hbm_spec()] * 6,
        out_specs=(vmem_spec(),) * 4,
        scratch_shapes=[
            pltpu.SMEM((blocks,), jnp.int32),
            pltpu.SMEM((blocks,), jnp.int32),
            pltpu.SMEM(cells.shape, jnp.int32),
            pltpu.SMEM(cells.shape, f32),
            pltpu.SemaphoreType.DMA((4,)),
            pltpu.SemaphoreType.DMA((3, tiles)),
        ],
        compiler_params=params(),
        cost_estimate=cost(2 * rows * cols, nbytes),
        name="start",
    )(
        *(
            pltpu.with_memory_space_constraint(x, pltpu.HBM)
            for x in (
                wet_mask.reshape(-1),
                helper_plan.reshape(-1),
                cells,
                rates,
                water_depth,
                momentum,
            )
        )
    )

    above = send(down, "region", True)
    below = send(up, "region", False)

    peak, left, right = pl.pallas_call(
        pack_kernel,
        out_shape=(first_out, strip_out, strip_out),
        in_specs=[vmem_spec()],
        out_specs=(hbm_spec(), vmem_spec(), vmem_spec()),
        scratch_shapes=[
            pltpu.VMEM((rows, LANES), f32),
            pltpu.VMEM(first_out.shape, f32),
            pltpu.SemaphoreType.DMA,
        ],
        compiler_params=params(),
        cost_estimate=cost(20 * rows * cols, nbytes),
        name="pack",
    )(work)

    work, left, right = pl.pallas_call(
        rows_kernel,
        out_shape=(work_out, strip_out, strip_out),
        in_specs=[vmem_spec()] * 5,
        out_specs=(vmem_spec(),) * 3,
        scratch_shapes=[pltpu.VMEM((LANES, LANES), f32)],
        input_output_aliases={0: 0, 1: 1, 2: 2},
        compiler_params=params(),
        cost_estimate=cost(rows * cols, nbytes // 8),
        name="rows",
    )(work, left, right, above, below)

    from_left = send(right, "tile", True)
    from_right = send(left, "tile", False)
    peaks = exchange(peak, ("region", "tile"))

    def flux(part, work, *strips):
        outs = (work_out, strips_out)[: 1 + len(strips)]
        main = [
            pltpu.VMEM((3 * tiles, padded, LANES), f32),
            pltpu.VMEM((3 * tiles, padded + 8, LANES), f32),
        ]
        edge = [pltpu.VMEM((LANES, rows + LANES), f32), pltpu.VMEM((padded, LANES), f32)]
        flops, moved_bytes = FLUX_COST[part]
        return pl.pallas_call(
            functools.partial(flux_kernel, part),
            out_shape=outs,
            in_specs=[vmem_spec()] * len(outs),
            out_specs=(vmem_spec(),) * len(outs),
            scratch_shapes=(main + edge, main, edge)[part],
            input_output_aliases={i: i for i in range(len(outs))},
            compiler_params=params(),
            cost_estimate=cost(int(flops * rows * cols), int(moved_bytes * nbytes)),
            name=("flux", "main", "edge")[part],
        )(work, *strips)

    (work,) = flux(MAIN, work)
    strips = pl.pallas_call(
        columns_kernel,
        out_shape=strips_out,
        in_specs=[vmem_spec()] * 4,
        out_specs=vmem_spec(),
        compiler_params=params(),
        cost_estimate=cost(rows * cols, nbytes // 8),
        name="columns",
    )(left, right, from_left, from_right)

    for step in range(STEPS):
        work, strips = flux(ALL if step else EDGE, work, strips)
        if step < STEPS - 1:
            work, strips, peak = pl.pallas_call(
                update_kernel,
                out_shape=(
                    work_out,
                    strips_out,
                    peak_out,
                ),
                in_specs=[vmem_spec()] * 3,
                out_specs=(vmem_spec(), vmem_spec(), hbm_spec()),
                scratch_shapes=[
                    pltpu.VMEM((everyone, 1, LANES), f32),
                    pltpu.SemaphoreType.DMA,
                ],
                input_output_aliases={1: 0, 2: 1},
                compiler_params=params(),
                cost_estimate=cost(20 * rows * cols, nbytes),
                name="update",
            )(peaks, work, strips)
            peaks = exchange(peak, ("region", "tile"))

    chips = tile_count // 2
    mine, theirs = pl.pallas_call(
        last_kernel,
        out_shape=(vmem_out(chips, 1, LANES),) * 2,
        in_specs=[vmem_spec()] * 3,
        out_specs=(vmem_spec(),) * 2,
        scratch_shapes=[pltpu.VMEM((blocks, 8, LANES), f32)],
        compiler_params=params(),
        cost_estimate=cost(20 * rows * cols, 2 * nbytes),
        name="last",
    )(peaks, plan, work)
    other = swap(theirs, "tile", 1)
    known = pl.pallas_call(
        chip_kernel,
        out_shape=(vmem_out(1, LANES),) * chips,
        in_specs=[vmem_spec()] * 2,
        out_specs=(vmem_spec(),) * chips,
        compiler_params=params(),
        cost_estimate=cost(tile_count, 4 * LANES * tile_count),
        name="chip",
    )(mine, other)
    known = [swap(known[x], "tile", 2 * x) for x in range(chips - 1, 0, -1)] + [known[0]]
    work, new_depth, new_momentum = pl.pallas_call(
        store_kernel,
        out_shape=(
            work_out,
            jax.ShapeDtypeStruct((rows, cols), f32),
            jax.ShapeDtypeStruct((2, rows, cols), f32),
        ),
        in_specs=[vmem_spec()] * 2,
        out_specs=(vmem_spec(), hbm_spec(), hbm_spec()),
        scratch_shapes=[pltpu.SemaphoreType.DMA((3, tiles))],
        input_output_aliases={1: 0},
        compiler_params=params(),
        cost_estimate=cost(10 * rows * cols, 2 * nbytes),
        name="store",
    )(peaks, work)
    helper = pl.pallas_call(
        helper_kernel,
        out_shape=jax.ShapeDtypeStruct((1, 1), f32),
        in_specs=[vmem_spec()] * chips,
        out_specs=vmem_spec(),
        compiler_params=params(),
        cost_estimate=cost(tile_count, 4 * LANES * tile_count),
        name="helper",
    )(*known)
    return new_depth, new_momentum, helper


def solution(mesh):
    return jax.shard_map(
        on_device,
        mesh=mesh,
        in_specs=(
            P("region", "tile"),
            P(None, "region", "tile"),
            P("region", "tile"),
            P("region", "tile"),
            P("region", "tile", None),
            P("region", "tile", None),
        ),
        out_specs=(P("region", "tile"), P(None, "region", "tile"), P("region", "tile")),
        check_vma=False,
    )
```

```python
import functools

import jax
import jax.numpy as jnp
from jax import lax
from jax.experimental import pallas as pl
from jax.experimental.pallas import tpu as pltpu
from jax.sharding import PartitionSpec as P

STEPS = 4
HALO = 4
LANES = 128
TOP = 8

GRAVITY = 9.81
COURANT = 0.45
SPACING = 1.0

VMEM_LIMIT = 20 << 20
FLUX_UNROLL = 7
FIRST = 2
FLUX_COST = ((150, 4), (150, 4), (500, 20))


SOURCE, DIFF, FIELDS = 3, 4, 7
SEND = 5
STRIP_DIFF, STRIP_FIELDS = 5, 8
ALL, MAIN, EDGE = range(3)


def tiles_of(work):
    return (work.shape[0] - 1) // FIELDS


def active_at(work):
    return work.shape[0] - 1


def sent_plane(work, k, c):
    tiles = tiles_of(work)
    return (k * tiles + c, active_at(work), SOURCE * tiles + c)[max(k - 2, 0)]


def vmem_spec():
    return pl.BlockSpec(memory_space=pltpu.VMEM)


def hbm_spec():
    return pl.BlockSpec(memory_space=pltpu.HBM)


def vmem_out(*shape):
    return pltpu.VMEM(shape, jnp.float32)


def params():
    return pltpu.CompilerParams(vmem_limit_bytes=VMEM_LIMIT)


def cost(flops, nbytes):
    return pl.CostEstimate(flops=flops, bytes_accessed=nbytes, transcendentals=0)


def lane_ids(rows):
    return lax.broadcasted_iota(jnp.int32, (rows, LANES), 1)


def aligned(start, size):
    return pl.ds(pl.multiple_of(start, 8), size)


def speed_of(depth, along, across):
    root = lax.rsqrt(depth)
    inverse = root * root
    return jnp.maximum(jnp.abs(along), jnp.abs(across)) * inverse + jnp.sqrt(
        jnp.float32(GRAVITY)
    ) * (depth * root)


def spread_peak(acc, out_ref):
    top = jnp.max(jnp.max(acc, axis=0, keepdims=True), axis=1, keepdims=True)
    out_ref[...] = jnp.broadcast_to(top[None], out_ref.shape)


def start_kernel(
    wet_hbm,
    plan_hbm,
    cell_hbm,
    rate_hbm,
    depth_hbm,
    mom_hbm,
    work,
    plan_ref,
    up_ref,
    down_ref,
    wet_ref,
    plan_smem,
    cell_ref,
    rate_ref,
    small_sem,
    big_sem,
):
    rows, cols = depth_hbm.shape
    tiles = cols // LANES
    padded = work.shape[1]
    blocks = wet_hbm.shape[0]
    block_rows = rows // blocks
    bottom = TOP + rows
    small = [
        pltpu.make_async_copy(src, dst, small_sem.at[i])
        for i, (src, dst) in enumerate(
            [
                (cell_hbm, cell_ref),
                (rate_hbm, rate_ref),
                (wet_hbm, wet_ref),
                (plan_hbm, plan_smem),
            ]
        )
    ]
    big = []
    for k, src in enumerate([depth_hbm, mom_hbm.at[0], mom_hbm.at[1]]):
        for c in range(tiles):
            big.append(
                pltpu.make_async_copy(
                    src.at[:, pl.ds(c * LANES, LANES)],
                    work.at[k * tiles + c, pl.ds(TOP, rows), :],
                    big_sem.at[k, c],
                )
            )
    for copy in small + big:
        copy.start()
    for k in range(SEND):
        for c in range(tiles):
            plane = sent_plane(work, k, c)
            fill = 1.0 if k == 0 else 0.0
            work[plane, 0:TOP, :] = jnp.full((TOP, LANES), fill, jnp.float32)
            work[plane, bottom:padded, :] = jnp.full((padded - bottom, LANES), fill, jnp.float32)
    for c in range(tiles):
        work[SOURCE * tiles + c, TOP:bottom, :] = jnp.zeros((rows, LANES), jnp.float32)
    for copy in small:
        copy.wait()
    lane = lane_ids(1)

    for i in range(cell_ref.shape[0]):
        cell = cell_ref[i]
        row = lax.div(cell, cols)
        col = cell - row * cols
        c = lax.div(col, LANES)
        at = pl.ds(row + TOP, 1)
        work[SOURCE * tiles + c, at, :] += jnp.where(lane == col - c * LANES, rate_ref[i], 0.0)
    for b in range(blocks):
        wet = wet_ref[b].astype(jnp.float32)
        at = slice(TOP + b * block_rows, TOP + (b + 1) * block_rows)
        work[active_at(work), at, :] = jnp.full((block_rows, LANES), wet)
        plan_ref[b] = jnp.full((1, LANES), plan_smem[b])
    for copy in big:
        copy.wait()
    for k in range(SEND):
        for c in range(tiles):
            plane = sent_plane(work, k, c)
            up_ref[k * tiles + c] = work[plane, TOP : TOP + HALO, :]
            down_ref[k * tiles + c] = work[plane, bottom - HALO : bottom, :]


def packed(work, at, lane):
    tiles = tiles_of(work)
    out = None
    for k in range(SEND):
        first, last = sent_plane(work, k, 0), sent_plane(work, k, tiles - 1)
        ends = jnp.where(lane < HALO, work[first, at, :], work[last, at, :])
        ends = pltpu.roll(ends, 2 * HALO * k + HALO, 1)
        out = ends if out is None else jnp.where(lane >= 2 * HALO * k, ends, out)
    return out


def split_packed(turned, left_ref, right_ref, at):
    for k in range(SEND):
        lo = 2 * HALO * k
        right_ref[k, :, at] = turned[lo : lo + HALO, :]
        left_ref[k, :, at] = turned[lo + HALO : lo + 2 * HALO, :]


def pack_kernel(work, peak_hbm, left_ref, right_ref, pack, spread, sem):
    tiles = tiles_of(work)
    rows = pack.shape[0]
    lane = lane_ids(8)

    def find(r, acc):
        at = aligned(r * 8 + TOP, 8)
        active = work[active_at(work), at, :] > 0.5
        for c in range(tiles):
            speed = speed_of(*[work[k * tiles + c, at, :] for k in range(3)])
            acc = jnp.maximum(acc, jnp.where(active, speed, 0.0))
        return acc

    zero = jnp.zeros((8, LANES), jnp.float32)
    spread_peak(lax.fori_loop(0, rows // 8, find, zero, unroll=48), spread)
    copy = pltpu.make_async_copy(spread, peak_hbm, sem)
    copy.start()

    def one(r, carry):
        pack[aligned(r * 8, 8), :] = packed(work, aligned(r * 8 + TOP, 8), lane)
        return carry

    lax.fori_loop(0, rows // 8, one, 0, unroll=24)
    for q in range(rows // LANES):
        at = slice(q * LANES, (q + 1) * LANES)
        split_packed(pack[at, :].T, left_ref, right_ref, at)
    copy.wait()


def rows_kernel(
    work_in, left_in, right_in, above_ref, below_ref, work, left_ref, right_ref, pack
):
    tiles = tiles_of(work)
    own = left_ref.shape[2] - LANES
    bottom = TOP + own
    is_top = lax.axis_index("region") == 0
    is_bottom = lax.axis_index("region") == lax.axis_size("region") - 1

    def mirrored(first, step, to):
        for k in range(SEND):
            flip = -1.0 if k == 1 else 1.0
            for c in range(tiles):
                plane = sent_plane(work, k, c)
                for j in range(HALO):
                    work[plane, to - step * (1 + j), :] = work[plane, first + step * j, :] * flip

    def received(ref, lo):
        for k in range(SEND):
            for c in range(tiles):
                work[sent_plane(work, k, c), lo : lo + HALO, :] = ref[k * tiles + c]

    pl.when(is_top)(lambda: mirrored(TOP, 1, TOP))
    pl.when(jnp.logical_not(is_top))(lambda: received(above_ref, TOP - HALO))
    pl.when(is_bottom)(lambda: mirrored(bottom - 1, -1, bottom - 1))
    pl.when(jnp.logical_not(is_bottom))(lambda: received(below_ref, bottom))
    pack[...] = jnp.zeros_like(pack)
    lane = lane_ids(8)
    pack[0:8, :] = packed(work, slice(bottom, bottom + 8), lane)
    pack[LANES - 8 :, :] = packed(work, slice(0, 8), lane)
    split_packed(pack[...].T, left_ref, right_ref, slice(own, own + LANES))


def columns_kernel(own_left, own_right, from_left, from_right, strips):
    is_left = lax.axis_index("tile") == 0
    is_right = lax.axis_index("tile") == lax.axis_size("tile") - 1

    def mirrored(ref, side, to):
        for k in range(SEND):
            flip = -1.0 if k == 2 else 1.0
            for j in range(HALO):
                strips[side, k, to + HALO - 1 - j, :] = ref[k, j, :] * flip

    def received(ref, side, to):
        for k in range(SEND):
            strips[side, k, to : to + HALO, :] = ref[k]

    received(own_left, 0, HALO)
    received(own_right, 1, 0)
    pl.when(is_left)(lambda: mirrored(own_left, 0, 0))
    pl.when(jnp.logical_not(is_left))(lambda: received(from_left, 0, 0))
    pl.when(is_right)(lambda: mirrored(own_right, 1, HALO))
    pl.when(jnp.logical_not(is_right))(lambda: received(from_right, 1, HALO))


def roe(left, right):
    depth_l, normal_l, tangent_l, root_l, sn_l, st_l, press_l, shear_l = left
    depth_r, normal_r, tangent_r, root_r, sn_r, st_r, press_r, shear_r = right
    weight = pl.reciprocal(root_l + root_r, approx=False)
    speed = (sn_l + sn_r) * weight
    drift = (st_l + st_r) * weight
    half = (0.5 * GRAVITY) * (depth_l + depth_r)
    inverse = lax.rsqrt(half)
    celerity = half * inverse
    jump = depth_r - depth_l
    excess = (normal_r - normal_l) - speed * jump
    bend = excess * (0.5 * inverse)
    half_jump = 0.5 * jump
    slow = speed - celerity
    fast = speed + celerity
    wave_one = jnp.abs(slow) * (half_jump - bend)
    wave_three = jnp.abs(fast) * (half_jump + bend)
    wave_two = jnp.abs(speed) * ((tangent_r - tangent_l) - drift * jump)
    both = wave_one + wave_three
    flux_depth = (normal_l + normal_r) - both
    flux_normal = (press_l + press_r) - speed * both - celerity * (wave_three - wave_one)
    flux_tangent = (shear_l + shear_r) - drift * both - wave_two
    return flux_depth, flux_normal, flux_tangent


def side(depth, normal, tangent, root, sn, st):
    press = sn * sn + (0.5 * GRAVITY) * (depth * depth)
    return (depth, normal, tangent, root, sn, st, press, sn * st)


def flip(v):
    return (v[0], v[2], v[1], v[3], v[5], v[4])


def with_roots(depth, along, across):
    inverse = lax.rsqrt(depth)
    return [depth, along, across, depth * inverse, along * inverse, across * inverse]


def strip_fluxes(strips, ghost_rows):
    chunks = strips.shape[3] // LANES
    lane = lane_ids(8)
    for s in range(2):
        spans = [slice(q * LANES, (q + 1) * LANES) for q in range(chunks)]
        now = [with_roots(*[strips[s, k, :, at] for k in range(3)]) for at in spans]
        rows = []
        for q in range(chunks):
            below = [
                pltpu.roll(jnp.where(lane == 0, b, a), LANES - 1, 1)
                for a, b in zip(now[q], now[(q + 1) % chunks])
            ]
            rows.append(roe(side(*now[q]), side(*below)))
        for q, at in enumerate(spans):
            right = [pltpu.roll(v, 7, 0) for v in now[q]]
            f_depth, f_across, f_along = roe(side(*flip(now[q])), side(*flip(right)))
            active = strips[s, 3, :, at] > 0.5
            for f, flux in enumerate((f_depth, f_along, f_across)):
                above = jnp.where(lane == LANES - 1, rows[q - 1][f], rows[q][f])
                out = (flux - pltpu.roll(flux, 1, 0)) + (rows[q][f] - pltpu.roll(above, 1, 1))
                if f == 0:
                    out = out - 2.0 * strips[s, 4, :, at]
                strips[s, STRIP_DIFF + f, :, at] = jnp.where(active, out, 0.0)
                ghost_rows[(2 * f - s) % LANES, at] = flux[HALO - 1, :]


def turn_ghosts(ghost_rows, ghost):
    own = ghost_rows.shape[1] - LANES
    for q in range(own // LANES):
        at = slice(q * LANES, (q + 1) * LANES)
        ghost[TOP + q * LANES : TOP + (q + 1) * LANES, :] = ghost_rows[:, at].T
    ends = ghost_rows[:, own : own + LANES].T
    ghost[TOP + own : TOP + own + 8, :] = ends[0:8, :]
    ghost[0:8, :] = ends[LANES - 8 :, :]


def flux_kernel(part, *refs):
    if part == MAIN:
        work_in, work, derived, faces = refs
    elif part == EDGE:
        work_in, strips_in, work, strips, ghost_rows, ghost = refs
    else:
        work_in, strips_in, work, strips, derived, faces, ghost_rows, ghost = refs
    tiles = tiles_of(work)
    padded = work.shape[1]
    row_tiles = padded // 8
    active_rows = active_at(work)
    lane = lane_ids(8)
    first, last = lane == 0, lane == LANES - 1
    if part != MAIN:
        strip_fluxes(strips, ghost_rows)
        turn_ghosts(ghost_rows, ghost)

    def edge_fluxes(at):
        values = ghost[at, :]
        return [values] + [pltpu.roll(values, LANES - 2 * f, 1) for f in (1, 2)]

    if part == EDGE:

        def fix(r, carry):
            at = aligned(r * 8, 8)
            edges = edge_fluxes(at)
            active = work[active_rows, at, :] > 0.5
            for f in range(3):
                left, right = DIFF * tiles + f * tiles, DIFF * tiles + f * tiles + tiles - 1
                work[left, at, :] -= jnp.where(active & first, edges[f], 0.0)
                work[right, at, :] += jnp.where(active & last, edges[f], 0.0)
            return carry

        lax.fori_loop(0, row_tiles, fix, 0, unroll=25)
        return

    def derive(r, carry):
        for i in range(5):
            at = aligned(r * 40 + i * 8, 8)
            for c in range(tiles):
                roots = with_roots(*[work[k * tiles + c, at, :] for k in range(3)])
                for k in range(3):
                    derived[k * tiles + c, at, :] = roots[3 + k]
        return carry

    lax.fori_loop(0, row_tiles // 5, derive, 0, unroll=5)
    for p in range(3 * tiles):
        faces[p, 0:8, :] = jnp.zeros((8, LANES), jnp.float32)

    def load(c, at):
        return [ref[k * tiles + c, at, :] for ref in (work, derived) for k in range(3)]

    def fluxes(at, wrap):
        here, below = pl.ds(at, 8), pl.ds(at + 1, 8)
        now = [load(c, here) for c in range(tiles)]
        across = []
        for c in range(tiles):
            right = [
                pltpu.roll(jnp.where(first, b, a), LANES - 1, 1)
                for a, b in zip(now[c], now[(c + 1) % tiles])
            ]
            f_depth, f_across, f_along = roe(side(*flip(now[c])), side(*flip(right)))
            across.append([f_depth, f_along, f_across])
            under = [pltpu.roll(v, 7, 0) for v in now[c]] if wrap else load(c, below)
            flux = roe(side(*now[c]), side(*under))
            for f in range(3):
                faces[f * tiles + c, pl.ds(at + 8, 8), :] = flux[f]
        if part == ALL:
            edges = edge_fluxes(here)
        else:
            edges = [jnp.zeros((8, LANES), jnp.float32)] * 3
        for f in range(3):
            across[-1][f] = jnp.where(last, edges[f], across[-1][f])
        active = work[active_rows, here, :] > 0.5
        for c in range(tiles):
            for f in range(3):
                if c:
                    left = pltpu.roll(jnp.where(last, across[c - 1][f], across[c][f]), 1, 1)
                else:
                    left = jnp.where(first, edges[f], pltpu.roll(across[c][f], 1, 1))
                plane = f * tiles + c
                out = (across[c][f] - left) + (
                    faces[plane, pl.ds(at + 8, 8), :] - faces[plane, pl.ds(at + 7, 8), :]
                )
                if f == 0:
                    out = out - 2.0 * work[SOURCE * tiles + c, here, :]
                work[(DIFF + f) * tiles + c, here, :] = jnp.where(active, out, 0.0)

    def one(r, carry):
        fluxes(pl.multiple_of(r * 8, 8), False)
        return carry

    lax.fori_loop(0, row_tiles - 1, one, 0, unroll=FLUX_UNROLL)
    fluxes(padded - 8, True)


def step_ratio(peak_ref):
    peak = jnp.max(jnp.max(peak_ref[...], axis=0), axis=0, keepdims=True)
    step = (COURANT * SPACING) / peak
    return jnp.broadcast_to((0.5 / SPACING) * step, (8, LANES))


def moved(work, c, at, ratio):
    tiles = tiles_of(work)
    return [
        work[f * tiles + c, at, :] - ratio * work[(DIFF + f) * tiles + c, at, :] for f in range(3)
    ]


def move_own(work, at, ratio):
    tiles = tiles_of(work)
    for c in range(tiles):
        for f, new in enumerate(moved(work, c, at, ratio)):
            work[f * tiles + c, at, :] = new


def update_kernel(peak_ref, work_in, strips_in, work, strips, next_hbm, spread, sem):
    tiles = tiles_of(work)
    row_tiles = work.shape[1] // 8
    ratio = step_ratio(peak_ref)

    def find(r, acc):
        at = aligned(r * 8 + TOP, 8)
        active = work[active_at(work), at, :] > 0.5
        for c in range(tiles):
            acc = jnp.maximum(acc, jnp.where(active, speed_of(*moved(work, c, at, ratio)), 0.0))
        return acc

    zero = jnp.zeros((8, LANES), jnp.float32)
    spread_peak(lax.fori_loop(0, row_tiles - 2, find, zero, unroll=48), spread)
    copy = pltpu.make_async_copy(spread, next_hbm, sem)
    copy.start()
    for q in range(strips.shape[3] // LANES):
        span = slice(q * LANES, (q + 1) * LANES)
        for k in range(3):
            for s in range(2):
                strips[s, k, :, span] -= ratio * strips[s, STRIP_DIFF + k, :, span]

    def move(r, carry):
        move_own(work, aligned(r * 8, 8), ratio)
        return carry

    lax.fori_loop(0, row_tiles, move, 0, unroll=25)
    copy.wait()


def last_kernel(peak_ref, plan_ref, work, mine_ref, theirs_ref, best):
    tiles = tiles_of(work)
    blocks = plan_ref.shape[0]
    block_rows = (work.shape[1] - 2 * 8) // blocks
    ratio = step_ratio(peak_ref)

    def one_block(b, carry):
        acc = jnp.zeros((8, LANES), jnp.float32)
        for r in range(0, block_rows, 8):
            at = aligned(b * block_rows + TOP + r, 8)
            for c in range(tiles):
                acc = jnp.maximum(acc, speed_of(*moved(work, c, at, ratio)))
        best[b] = acc
        return carry

    lax.fori_loop(0, blocks, one_block, 0, unroll=24)
    is_odd = lax.rem(lax.axis_index("tile"), 2) == 1
    for j in range(mine_ref.shape[0]):
        pair = []
        for t in (2 * j, 2 * j + 1):
            acc = jnp.zeros((8, LANES), jnp.float32)
            for b in range(blocks):
                acc = jnp.maximum(acc, jnp.where(plan_ref[b] == t, best[b], 0.0))
            top = jnp.max(acc, axis=0, keepdims=True)
            pair.append(jnp.broadcast_to(jnp.max(top, axis=1, keepdims=True), (1, LANES)))
        mine_ref[j] = jnp.where(is_odd, pair[1], pair[0])
        theirs_ref[j] = jnp.where(is_odd, pair[0], pair[1])


def chip_kernel(mine_ref, other_ref, *out_refs):
    here = lax.div(lax.axis_index("tile"), 2)
    for x, out_ref in enumerate(out_refs):
        there = jnp.bitwise_xor(here, x)
        out_ref[...] = jnp.maximum(mine_ref[there], other_ref[there])


def helper_kernel(*refs):
    value = refs[0][...]
    for ref in refs[1:-1]:
        value = jnp.maximum(value, ref[...])
    refs[-1][...] = value[:, :1]


def store_kernel(peak_ref, work_in, work, depth_hbm, mom_hbm, sem):
    rows, cols = depth_hbm.shape
    tiles = cols // LANES
    ratio = step_ratio(peak_ref)

    def move(r, carry):
        move_own(work, aligned(r * 8 + TOP, 8), ratio)
        return carry

    lax.fori_loop(0, rows // 8, move, 0, unroll=8)
    copies = []
    for k, dst in enumerate([depth_hbm, mom_hbm.at[0], mom_hbm.at[1]]):
        for c in range(tiles):
            copies.append(
                pltpu.make_async_copy(
                    work.at[k * tiles + c, pl.ds(TOP, rows), :],
                    dst.at[:, pl.ds(c * LANES, LANES)],
                    sem.at[k, c],
                )
            )
    for copy in copies:
        copy.start()
    for copy in copies:
        copy.wait()


def exchange(x, axes):
    return lax.all_to_all(x, axes, 0, 0)


def swap(x, axis, apart):
    return lax.ppermute(x, axis, [(i, i ^ apart) for i in range(lax.axis_size(axis))])


def send(x, axis, forward):
    count = lax.axis_size(axis)
    pairs = [(i, (i + 1) % count) if forward else ((i + 1) % count, i) for i in range(count)]
    return lax.ppermute(x, axis, pairs)


def on_device(water_depth, momentum, wet_mask, helper_plan, breach_cells, breach_rate):
    rows, cols = water_depth.shape
    tile_count = lax.axis_size("tile")
    everyone = tile_count * lax.axis_size("region")
    blocks = wet_mask.shape[0]
    tiles = cols // LANES
    padded = rows + 2 * 8
    f32 = jnp.float32
    cells = breach_cells.reshape(-1)
    rates = breach_rate.reshape(-1)
    nbytes = 4 * 3 * rows * cols
    work_out = vmem_out(FIELDS * tiles + 1, padded, LANES)
    strips_out = vmem_out(2, STRIP_FIELDS, 2 * HALO, rows + LANES)
    strip_out = vmem_out(SEND, HALO, rows + LANES)
    edge_out = vmem_out(SEND * tiles, HALO, LANES)
    peak_out = jax.ShapeDtypeStruct((everyone, 1, LANES), f32)
    first_out = jax.ShapeDtypeStruct((everyone, FIRST, LANES), f32)

    work, plan, up, down = pl.pallas_call(
        start_kernel,
        out_shape=(work_out, pltpu.VMEM((blocks, 1, LANES), jnp.int32), edge_out, edge_out),
        in_specs=[hbm_spec()] * 6,
        out_specs=(vmem_spec(),) * 4,
        scratch_shapes=[
            pltpu.SMEM((blocks,), jnp.int32),
            pltpu.SMEM((blocks,), jnp.int32),
            pltpu.SMEM(cells.shape, jnp.int32),
            pltpu.SMEM(cells.shape, f32),
            pltpu.SemaphoreType.DMA((4,)),
            pltpu.SemaphoreType.DMA((3, tiles)),
        ],
        compiler_params=params(),
        cost_estimate=cost(2 * rows * cols, nbytes),
        name="start",
    )(
        *(
            pltpu.with_memory_space_constraint(x, pltpu.HBM)
            for x in (
                wet_mask.reshape(-1),
                helper_plan.reshape(-1),
                cells,
                rates,
                water_depth,
                momentum,
            )
        )
    )

    above = send(down, "region", True)
    below = send(up, "region", False)

    peak, left, right = pl.pallas_call(
        pack_kernel,
        out_shape=(first_out, strip_out, strip_out),
        in_specs=[vmem_spec()],
        out_specs=(hbm_spec(), vmem_spec(), vmem_spec()),
        scratch_shapes=[
            pltpu.VMEM((rows, LANES), f32),
            pltpu.VMEM(first_out.shape, f32),
            pltpu.SemaphoreType.DMA,
        ],
        compiler_params=params(),
        cost_estimate=cost(20 * rows * cols, nbytes),
        name="pack",
    )(work)

    work, left, right = pl.pallas_call(
        rows_kernel,
        out_shape=(work_out, strip_out, strip_out),
        in_specs=[vmem_spec()] * 5,
        out_specs=(vmem_spec(),) * 3,
        scratch_shapes=[pltpu.VMEM((LANES, LANES), f32)],
        input_output_aliases={0: 0, 1: 1, 2: 2},
        compiler_params=params(),
        cost_estimate=cost(rows * cols, nbytes // 8),
        name="rows",
    )(work, left, right, above, below)

    from_left = send(right, "tile", True)
    from_right = send(left, "tile", False)
    peaks = exchange(peak, ("region", "tile"))

    def flux(part, work, *strips):
        outs = (work_out, strips_out)[: 1 + len(strips)]
        main = [
            pltpu.VMEM((3 * tiles, padded, LANES), f32),
            pltpu.VMEM((3 * tiles, padded + 8, LANES), f32),
        ]
        edge = [pltpu.VMEM((LANES, rows + LANES), f32), pltpu.VMEM((padded, LANES), f32)]
        flops, moved_bytes = FLUX_COST[part]
        return pl.pallas_call(
            functools.partial(flux_kernel, part),
            out_shape=outs,
            in_specs=[vmem_spec()] * len(outs),
            out_specs=(vmem_spec(),) * len(outs),
            scratch_shapes=(main + edge, main, edge)[part],
            input_output_aliases={i: i for i in range(len(outs))},
            compiler_params=params(),
            cost_estimate=cost(int(flops * rows * cols), int(moved_bytes * nbytes)),
            name=("flux", "main", "edge")[part],
        )(work, *strips)

    (work,) = flux(MAIN, work)
    strips = pl.pallas_call(
        columns_kernel,
        out_shape=strips_out,
        in_specs=[vmem_spec()] * 4,
        out_specs=vmem_spec(),
        compiler_params=params(),
        cost_estimate=cost(rows * cols, nbytes // 8),
        name="columns",
    )(left, right, from_left, from_right)

    for step in range(STEPS):
        work, strips = flux(ALL if step else EDGE, work, strips)
        if step < STEPS - 1:
            work, strips, peak = pl.pallas_call(
                update_kernel,
                out_shape=(
                    work_out,
                    strips_out,
                    peak_out,
                ),
                in_specs=[vmem_spec()] * 3,
                out_specs=(vmem_spec(), vmem_spec(), hbm_spec()),
                scratch_shapes=[
                    pltpu.VMEM((everyone, 1, LANES), f32),
                    pltpu.SemaphoreType.DMA,
                ],
                input_output_aliases={1: 0, 2: 1},
                compiler_params=params(),
                cost_estimate=cost(20 * rows * cols, nbytes),
                name="update",
            )(peaks, work, strips)
            peaks = exchange(peak, ("region", "tile"))

    chips = tile_count // 2
    mine, theirs = pl.pallas_call(
        last_kernel,
        out_shape=(vmem_out(chips, 1, LANES),) * 2,
        in_specs=[vmem_spec()] * 3,
        out_specs=(vmem_spec(),) * 2,
        scratch_shapes=[pltpu.VMEM((blocks, 8, LANES), f32)],
        compiler_params=params(),
        cost_estimate=cost(20 * rows * cols, 2 * nbytes),
        name="last",
    )(peaks, plan, work)
    other = swap(theirs, "tile", 1)
    known = pl.pallas_call(
        chip_kernel,
        out_shape=(vmem_out(1, LANES),) * chips,
        in_specs=[vmem_spec()] * 2,
        out_specs=(vmem_spec(),) * chips,
        compiler_params=params(),
        cost_estimate=cost(tile_count, 4 * LANES * tile_count),
        name="chip",
    )(mine, other)
    known = [swap(known[x], "tile", 2 * x) for x in range(chips - 1, 0, -1)] + [known[0]]
    work, new_depth, new_momentum = pl.pallas_call(
        store_kernel,
        out_shape=(
            work_out,
            jax.ShapeDtypeStruct((rows, cols), f32),
            jax.ShapeDtypeStruct((2, rows, cols), f32),
        ),
        in_specs=[vmem_spec()] * 2,
        out_specs=(vmem_spec(), hbm_spec(), hbm_spec()),
        scratch_shapes=[pltpu.SemaphoreType.DMA((3, tiles))],
        input_output_aliases={1: 0},
        compiler_params=params(),
        cost_estimate=cost(10 * rows * cols, 2 * nbytes),
        name="store",
    )(peaks, work)
    helper = pl.pallas_call(
        helper_kernel,
        out_shape=jax.ShapeDtypeStruct((1, 1), f32),
        in_specs=[vmem_spec()] * chips,
        out_specs=vmem_spec(),
        compiler_params=params(),
        cost_estimate=cost(tile_count, 4 * LANES * tile_count),
        name="helper",
    )(*known)
    return new_depth, new_momentum, helper


def solution(mesh):
    return jax.shard_map(
        on_device,
        mesh=mesh,
        in_specs=(
            P("region", "tile"),
            P(None, "region", "tile"),
            P("region", "tile"),
            P("region", "tile"),
            P("region", "tile", None),
            P("region", "tile", None),
        ),
        out_specs=(P("region", "tile"), P(None, "region", "tile"), P("region", "tile")),
        check_vma=False,
    )
```
